32 devices in a mesh: grp: 2 (over x), ctx: 16 (over z, y, core).
Axes of the slice: x: 2, y: 2, z: 4, core: 2. Of those that a mesh axis runs over, the one named last changes fastest.
Arguments:
- tokens: bfloat16 [2, 2048, 2048], P('grp', 'ctx'), may hold values from -6 to 6
- segments: int32 [2, 2048], P('grp'), may hold values from 0 to 65, as said below
- output_cotangent_rows: bfloat16 [2, 2048, 2048], P('grp', 'ctx'), may hold values from -6 to 6
- attention_norm_gain: bfloat16 [2048], P('ctx'), may hold values from -0.5 to 0.5
- query_key_value_matrix: bfloat16 [2048, 2560], P('ctx'), may hold values from -0.125 to 0.125
- query_key_value_adapter_first: bfloat16 [2048, 256], P('ctx'), may hold values from -0.125 to 0.125
- query_key_value_adapter_second: bfloat16 [256, 2560], P('ctx'), may hold values from -0.1875 to 0.1875
- output_matrix: bfloat16 [2048, 2048], P('ctx'), may hold values from -0.75 to 0.75
- output_adapter_first: bfloat16 [2048, 256], P('ctx'), may hold values from -0.75 to 0.75
- output_adapter_second: bfloat16 [256, 2048], P('ctx'), may hold values from -0.1875 to 0.1875
- feed_norm_gain: bfloat16 [2048], P('ctx'), may hold values from -0.5 to 0.5
- gate_up_matrix: bfloat16 [2048, 32768], P('ctx'), may hold values from -0.125 to 0.125
- gate_up_adapter_first: bfloat16 [2048, 256], P('ctx'), may hold values from -0.125 to 0.125
- gate_up_adapter_second: bfloat16 [256, 32768], P('ctx'), may hold values from -0.1875 to 0.1875
- down_matrix: bfloat16 [16384, 2048], P('ctx'), may hold values from -0.046875 to 0.046875
- down_adapter_first: bfloat16 [16384, 256], P('ctx'), may hold values from -0.046875 to 0.046875
- down_adapter_second: bfloat16 [256, 2048], P('ctx'), may hold values from -0.1875 to 0.1875
Outputs:
- output: bfloat16 [2, 2048, 2048], P('grp', 'ctx')
- grad_input: bfloat16 [2, 2048, 2048], P('grp', 'ctx')
- g_attn_gain: float32 [2048], P('ctx')
- g_qkv_weight: float32 [2048, 2560], P('ctx')
- g_qkv_lora_a: float32 [2048, 256], P('ctx')
- g_qkv_lora_b: float32 [256, 2560], P('ctx')
- g_out_weight: float32 [2048, 2048], P('ctx')
- g_out_lora_a: float32 [2048, 256], P('ctx')
- g_out_lora_b: float32 [256, 2048], P('ctx')
- g_ffn_gain: float32 [2048], P('ctx')
- g_gate_up_weight: float32 [2048, 32768], P('ctx')
- g_gate_up_lora_a: float32 [2048, 256], P('ctx')
- g_gate_up_lora_b: float32 [256, 32768], P('ctx')
- g_down_weight: float32 [16384, 2048], P('ctx')
- g_down_lora_a: float32 [16384, 256], P('ctx')
- g_down_lora_b: float32 [256, 2048], P('ctx')
The draws below stay inside these ranges and needn't reach their ends.
Inputs may be any that keep to these rules, and one draw needn't show every extreme that they name: `segments`: along a sequence's positions the document numbers never fall; the last document starts at or before position 960 and runs to the end.
All inputs are finite; a program needn't handle non-finite values.
Results may differ from the reference program's by a relative error of at most 0.019.
Values may be sent and summed in bfloat16 or wider, within the bound.
No kernel may reach another device: no remote copies, remote signals or barrier semaphores. Data moves between devices by JAX's collectives and lax.ppermute only.
A program may use at most 960 MiB of HBM per device.

```python
import math
import jax
import jax.numpy as jnp
from jax import lax

MODEL_WIDTH = 2048
HEADS = 8
HD = 256
FEED_HIDDEN = 16384
ADAPTER_RANK = 256
TOK_DEV = 128
BLK = 64
SEQ = 2048
SEQS = 2
PROJECTED_COLUMNS = 2560
N_CTX = 16


doc_slots = 64


def sequence_segments(sub_key):
    key_start, key_exp, key_len = jax.random.split(sub_key, 3)
    last_start = jax.random.randint(key_start, (), SEQ // 8, SEQ // 2 - BLK + 1)
    top_exp = max(int(math.log2(SEQ)) - 2, 1)
    exponents = jax.random.randint(key_exp, (doc_slots,), 0, top_exp)
    base_len = jnp.left_shift(jnp.ones((doc_slots,), jnp.int32), exponents)
    lengths = base_len + jax.random.randint(key_len, (doc_slots,), 0, 1 << 20) % base_len
    bounds = jnp.cumsum(lengths)
    pos_rows = jnp.arange(SEQ, dtype=jnp.int32)
    doc_count = jnp.sum((bounds[None, :] <= pos_rows[:, None]).astype(jnp.int32), axis=1)
    return jnp.where(pos_rows >= last_start, doc_slots + 1, doc_count).astype(jnp.int32)


def draw_segments(key, part):
    sub_keys = jax.random.split(key, SEQS)
    return jax.vmap(sequence_segments)(sub_keys)


def steps_of(own_key, extent, cuts, least, top_value):
    def one(position, blocks):
        heights = jax.random.uniform(jax.random.fold_in(jax.random.fold_in(own_key, 6), position), (blocks,), jnp.float32, least / len(cuts), top_value / len(cuts))
        return jnp.repeat(jnp.exp(heights), extent[position] // blocks).reshape((-1,) + (1,) * (len(extent) - position - 1))

    gain = one(*cuts[0])
    for cut in cuts[1:]:
        gain = gain * one(*cut)
    return gain


def scatter_about(rng, shape, spread, limit, cuts=(), kind=jnp.bfloat16):
    entries = spread * jax.random.normal(rng, shape, jnp.float32)
    if cuts:
        entries = entries * steps_of(rng, shape, cuts, -0.22, 0.18)
    return jnp.clip(entries, -limit, limit).astype(kind)


def setup_inputs(seed: int = 0) -> dict:
    arg_keys = jax.random.split(jax.random.key(seed), 18)
    tokens = scatter_about(arg_keys[0], (SEQS, SEQ, MODEL_WIDTH), 1.0, 6.0, ((0, 2), (1, 16)))
    segments = draw_segments(jax.random.fold_in(arg_keys[17], 71), 0)
    output_cotangent_rows = scatter_about(arg_keys[2], (SEQS, SEQ, MODEL_WIDTH), 1.0, 6.0, ((0, 2), (1, 16)))
    attention_norm_gain = jnp.clip(jax.random.uniform(arg_keys[3], (MODEL_WIDTH,), jnp.float32, -0.5, 0.5) * steps_of(arg_keys[3], (MODEL_WIDTH,), ((0, 16),), -0.4, 0.0), -0.5, 0.5).astype(jnp.bfloat16)
    query_key_value_matrix = scatter_about(arg_keys[4], (MODEL_WIDTH, PROJECTED_COLUMNS), MODEL_WIDTH ** -0.5, 0.125, ((0, 16),))
    query_key_value_adapter_first = scatter_about(arg_keys[5], (MODEL_WIDTH, ADAPTER_RANK), MODEL_WIDTH ** -0.5, 0.125, ((0, 16),))
    query_key_value_adapter_second = scatter_about(arg_keys[6], (ADAPTER_RANK, PROJECTED_COLUMNS), (4 * ADAPTER_RANK) ** -0.5, 0.1875, ((0, 16),))
    output_matrix = scatter_about(arg_keys[7], (MODEL_WIDTH, MODEL_WIDTH), (MODEL_WIDTH // 32) ** -0.5, 0.75, ((0, 16),))
    output_adapter_first = scatter_about(arg_keys[8], (MODEL_WIDTH, ADAPTER_RANK), (MODEL_WIDTH // 32) ** -0.5, 0.75, ((0, 16),))
    output_adapter_second = scatter_about(arg_keys[9], (ADAPTER_RANK, MODEL_WIDTH), (4 * ADAPTER_RANK) ** -0.5, 0.1875, ((0, 16),))
    feed_norm_gain = jnp.clip(jax.random.uniform(arg_keys[10], (MODEL_WIDTH,), jnp.float32, -0.5, 0.5) * steps_of(arg_keys[10], (MODEL_WIDTH,), ((0, 16),), -0.4, 0.0), -0.5, 0.5).astype(jnp.bfloat16)
    gate_up_matrix = scatter_about(arg_keys[11], (MODEL_WIDTH, 2 * FEED_HIDDEN), MODEL_WIDTH ** -0.5, 0.125, ((0, 16),))
    gate_up_adapter_first = scatter_about(arg_keys[12], (MODEL_WIDTH, ADAPTER_RANK), MODEL_WIDTH ** -0.5, 0.125, ((0, 16),))
    gate_up_adapter_second = scatter_about(arg_keys[13], (ADAPTER_RANK, 2 * FEED_HIDDEN), (4 * ADAPTER_RANK) ** -0.5, 0.1875, ((0, 16),))
    down_matrix = scatter_about(arg_keys[14], (FEED_HIDDEN, MODEL_WIDTH), FEED_HIDDEN ** -0.5, 0.046875, ((0, 16),))
    down_adapter_first = scatter_about(arg_keys[15], (FEED_HIDDEN, ADAPTER_RANK), FEED_HIDDEN ** -0.5, 0.046875, ((0, 16),))
    down_adapter_second = scatter_about(arg_keys[16], (ADAPTER_RANK, MODEL_WIDTH), (4 * ADAPTER_RANK) ** -0.5, 0.1875, ((0, 16),))
    return dict(tokens=tokens, segments=segments, output_cotangent_rows=output_cotangent_rows, attention_norm_gain=attention_norm_gain, query_key_value_matrix=query_key_value_matrix, query_key_value_adapter_first=query_key_value_adapter_first, query_key_value_adapter_second=query_key_value_adapter_second, output_matrix=output_matrix, output_adapter_first=output_adapter_first, output_adapter_second=output_adapter_second, feed_norm_gain=feed_norm_gain, gate_up_matrix=gate_up_matrix, gate_up_adapter_first=gate_up_adapter_first, gate_up_adapter_second=gate_up_adapter_second, down_matrix=down_matrix, down_adapter_first=down_adapter_first, down_adapter_second=down_adapter_second)


norm_eps = 1e-06
rope_base = 10000.0

@jax.custom_vjp
def reduced_precision(v):
    return lax.optimization_barrier(v.astype(jnp.bfloat16)).astype(jnp.float32)

@jax.custom_vjp
def reduced_backward(v):
    return v

def low_keep(v):
    return (reduced_precision(v), None)

def low_pass(kept, grad):
    return (grad,)

def back_keep(v):
    return (v, None)

def back_low(kept, grad):
    return (reduced_precision(grad),)
reduced_precision.defvjp(low_keep, low_pass)
reduced_backward.defvjp(back_keep, back_low)

def precise_product(left_arg, right_arg):
    return jnp.dot(left_arg, right_arg, precision=lax.Precision.HIGHEST)

def positions(row_count, per_device, device_count):
    row_index = jnp.arange(row_count, dtype=jnp.int32)
    device = row_index // per_device
    within = row_index % per_device
    half_len = per_device // 2
    block_id = jnp.where(within < half_len, device, 2 * device_count - 1 - device)
    return (block_id * half_len + within % half_len).astype(jnp.int32)

def angles(pos_rows):
    frequency = rope_base ** (-2.0 * jnp.arange(HD // 2, dtype=jnp.float32) / HD)
    angle_rows = pos_rows.astype(jnp.float32)[:, None] * frequency[None, :]
    return (jnp.cos(angle_rows), jnp.sin(angle_rows))

def rotate(vectors, cosine, sine_rows):
    front_half, back_half = jnp.split(vectors, 2, axis=-1)
    return jnp.concatenate([front_half * cosine - back_half * sine_rows, back_half * cosine + front_half * sine_rows], axis=-1)

def rms_norm(values, gain_vec):
    inv_rms = lax.rsqrt(lax.optimization_barrier(jnp.mean(values * values, axis=-1, keepdims=True)) + norm_eps)
    return values * inv_rms * (1.0 + gain_vec)

def adapter_path(input_rows, weight_matrix, adapter_first, adapter_second):
    rank_projection = reduced_backward(reduced_precision(precise_product(input_rows, adapter_first)))
    return precise_product(input_rows, weight_matrix) + precise_product(rank_projection, adapter_second)

def attend(queries, key_rows, values, seg_rows, pos_rows):
    block_rows = math.gcd(SEQ, 512)
    block_count = SEQ // block_rows
    score_scale = HD ** (-0.5)

    def one_block(pieces):
        query_blk, seg_blk, pos_blk = pieces
        raw_scores = jnp.einsum('qhd,kd->qhk', query_blk, key_rows, precision=lax.Precision.HIGHEST) * score_scale
        raw_scores = reduced_backward(raw_scores)
        allowed = (seg_blk[:, None] == seg_rows[None, :]) & (pos_rows[None, :] <= pos_blk[:, None])
        scores = jnp.where(allowed[:, None, :], raw_scores, -jnp.inf)
        row_peak = lax.optimization_barrier(jnp.max(scores, axis=-1, keepdims=True))
        unnormed = jnp.exp(scores - row_peak)
        attn_probs = reduced_precision(unnormed / lax.optimization_barrier(jnp.sum(unnormed, axis=-1, keepdims=True)))
        return jnp.einsum('qhk,kd->qhd', attn_probs, values, precision=lax.Precision.HIGHEST)
    result = lax.map(jax.checkpoint(one_block), (queries.reshape(block_count, block_rows, HEADS, HD), seg_rows.reshape(block_count, block_rows), pos_rows.reshape(block_count, block_rows)))
    return result.reshape(SEQ, HEADS * HD)

def single_sequence(residual_stream, segment_row, attention_norm_gain, query_key_value_matrix, query_key_value_adapter_first, query_key_value_adapter_second, output_matrix, output_adapter_first, output_adapter_second, feed_norm_gain, gate_up_matrix, gate_up_adapter_first, gate_up_adapter_second, down_matrix, down_adapter_first, down_adapter_second):
    pos_rows = positions(SEQ, TOK_DEV, N_CTX)
    seg_rows = jnp.take(segment_row, pos_rows)
    cosine, sine_rows = angles(pos_rows)
    first_normed = reduced_precision(rms_norm(residual_stream, attention_norm_gain))
    query_key_value_rows = reduced_backward(adapter_path(first_normed, query_key_value_matrix, query_key_value_adapter_first, query_key_value_adapter_second))
    queries = reduced_precision(rotate(query_key_value_rows[:, :MODEL_WIDTH].reshape(SEQ, HEADS, HD), cosine[:, None, :], sine_rows[:, None, :]))
    key_rows = reduced_precision(rotate(query_key_value_rows[:, MODEL_WIDTH:MODEL_WIDTH + HD], cosine, sine_rows))
    value_rows = reduced_precision(query_key_value_rows[:, MODEL_WIDTH + HD:])
    attention_result = reduced_backward(reduced_precision(attend(queries, key_rows, value_rows, seg_rows, pos_rows)))
    adapter_branch = reduced_backward(adapter_path(attention_result, output_matrix, output_adapter_first, output_adapter_second))
    middle_residual = residual_stream + adapter_branch
    second_normed = reduced_precision(rms_norm(middle_residual, feed_norm_gain))
    gate_up_output = reduced_backward(adapter_path(second_normed, gate_up_matrix, gate_up_adapter_first, gate_up_adapter_second))
    hidden_activation = reduced_precision(jax.nn.gelu(gate_up_output[:, :FEED_HIDDEN], approximate=True) * gate_up_output[:, FEED_HIDDEN:])
    return middle_residual + adapter_path(hidden_activation, down_matrix, down_adapter_first, down_adapter_second)

def reference(tokens, segments, output_cotangent_rows, attention_norm_gain, query_key_value_matrix, query_key_value_adapter_first, query_key_value_adapter_second, output_matrix, output_adapter_first, output_adapter_second, feed_norm_gain, gate_up_matrix, gate_up_adapter_first, gate_up_adapter_second, down_matrix, down_adapter_first, down_adapter_second):
    weight_bundle = tuple((weight_operand.astype(jnp.float32) for weight_operand in (attention_norm_gain, query_key_value_matrix, query_key_value_adapter_first, query_key_value_adapter_second, output_matrix, output_adapter_first, output_adapter_second, feed_norm_gain, gate_up_matrix, gate_up_adapter_first, gate_up_adapter_second, down_matrix, down_adapter_first, down_adapter_second)))
    residual_stream = tokens.astype(jnp.float32)

    def forward(residual_all, *weight_list):

        def apply_one(pieces):
            return single_sequence(pieces[0], pieces[1], *weight_list)
        return lax.map(apply_one, (residual_all, segments))
    output, pullback = jax.vjp(forward, residual_stream, *weight_bundle)
    gradients = pullback(output_cotangent_rows.astype(jnp.float32))
    return (output.astype(jnp.bfloat16), gradients[0].astype(jnp.bfloat16), gradients[1], gradients[2], gradients[3], gradients[4], gradients[5], gradients[6], gradients[7], gradients[8], gradients[9], gradients[10], gradients[11], gradients[12], gradients[13], gradients[14])
```

```python
import functools

import jax
import jax.numpy as jnp
from jax import lax
from jax.experimental import pallas as pl
from jax.experimental.pallas import tpu as pltpu
from jax.sharding import PartitionSpec as P

HEADS = 8
HD = 256
norm_eps = 1e-06
rope_base = 10000.0
BF = jnp.bfloat16
F32 = jnp.float32


def mm(a, b, ca=1, cb=0):
    return lax.dot_general(a, b, (((ca,), (cb,)), ((), ())), preferred_element_type=F32)


def rotate(vectors, cosine, sine_rows):
    front, back = jnp.split(vectors, 2, axis=-1)
    return jnp.concatenate(
        [front * cosine - back * sine_rows, back * cosine + front * sine_rows], axis=-1
    )


def inv_rms(values):
    return lax.rsqrt(jnp.mean(values * values, axis=-1, keepdims=True) + norm_eps)


def norm_back(values, inv, gain, grad):
    weighted = grad * (1.0 + gain)
    inner = jnp.mean(weighted * values, axis=-1, keepdims=True)
    return inv * weighted - values * (inv * inv * inv) * inner


def after(value, *others):
    return lax.optimization_barrier((value,) + others)[0]


def deal_kernel(plane_ref, *refs):
    out_ref = refs[-1]
    each = out_ref.shape[0]
    for k in range(each):
        w_ref, b_ref = refs[k], refs[each + k]
        w_rows = w_ref.shape[0]
        out_ref[k, :w_rows] = w_ref[...]
        out_ref[k, w_rows:] = b_ref[...]


def deal_out(part, plane, matrix, second, n):
    w_rows, r_rows = matrix.shape[0], second.shape[0]
    cols = matrix.shape[1] // (4 * n)
    each = 4

    def column(k, s, plane_ref):
        return (0, (part * n + s * each + k) * 2 + plane_ref[0])

    maps = [functools.partial(column, k) for k in range(each)]
    return pl.pallas_call(
        deal_kernel,
        out_shape=jax.ShapeDtypeStruct((n, w_rows + r_rows, cols), BF),
        grid_spec=pltpu.PrefetchScalarGridSpec(
            num_scalar_prefetch=1,
            grid=(n // each,),
            in_specs=[pl.BlockSpec((w_rows, cols), m) for m in maps]
            + [pl.BlockSpec((r_rows, cols), m) for m in maps],
            out_specs=pl.BlockSpec((each, w_rows + r_rows, cols), lambda s, p: (s, 0, 0)),
        ),
        cost_estimate=pl.CostEstimate(
            flops=0, transcendentals=0, bytes_accessed=4 * n * (w_rows + r_rows) * cols
        ),
    )(plane, *([matrix] * each), *([second] * each))


def fold_kernel(gate_ref, up_ref, b_gate_ref, b_up_ref, a_ref, *refs):
    out_ref = refs[-1]
    each, w_rows = gate_ref.shape[0], a_ref.shape[0] // gate_ref.shape[0]
    cols = b_gate_ref.shape[1]
    gate = mm(a_ref[...], b_gate_ref[...])
    up = mm(a_ref[...], b_up_ref[...])
    for k in range(each):
        part = slice(k * w_rows, (k + 1) * w_rows)
        out_ref[part, :cols] = (gate_ref[k, :w_rows].astype(F32) + gate[part]).astype(BF)
        out_ref[part, cols:] = (up_ref[k, :w_rows].astype(F32) + up[part]).astype(BF)


def fold(gate, up, first, place, given):
    n, ext, cols = gate.shape
    width, rank = first.shape
    w_rows = width // n
    each = max(1, min(4, 512 // w_rows))
    seconds = [x[:, w_rows:].reshape(rank, cols) for x in (gate, up)]
    piece = pl.BlockSpec((each, ext, cols), lambda s: (s, 0, 0))
    whole = pl.BlockSpec((rank, cols), lambda s: (0, 0))
    held = [] if given is None else [given]
    return pl.pallas_call(
        fold_kernel,
        out_shape=jax.ShapeDtypeStruct((width, 4 * cols), BF),
        grid=(n // each,),
        in_specs=[piece, piece, whole, whole]
        + [pl.BlockSpec((each * w_rows, rank), lambda s: (s, 0))]
        + [pl.BlockSpec(memory_space=pl.ANY)] * len(held),
        out_specs=pl.BlockSpec((each * w_rows, 2 * cols), lambda s: (s, place)),
        input_output_aliases={5: 0} if held else {},
        cost_estimate=pl.CostEstimate(
            flops=4 * width * rank * cols, transcendentals=0, bytes_accessed=8 * width * cols
        ),
    )(gate, up, *seconds, first, *held), seconds


def forward_kernel(x_ref, w_ref, hidden_ref, act_ref, slope_ref):
    h = hidden_ref.shape[1] // 2
    c = 0.7978845608028654
    for k in (0, 1):
        both = mm(x_ref[...], w_ref[:, 2 * k * h : 2 * (k + 1) * h])
        gate, up = both[:, :h], both[:, h:]
        square = gate * gate
        t = jnp.tanh(c * gate * (1.0 + 0.044715 * square))
        half_up = 0.5 * (1.0 + t)
        act = gate * half_up
        slope = half_up + 0.5 * gate * (1.0 - t * t) * (c * (1.0 + 3 * 0.044715 * square))
        part = slice(k * h, (k + 1) * h)
        hidden_ref[:, part] = (act * up).astype(BF)
        act_ref[:, part] = act.astype(BF)
        slope_ref[:, part] = (slope * up).astype(BF)


def forward(x, w):
    t, d = x.shape
    f = w.shape[1] // 2
    tile = 256
    out = pl.BlockSpec((tile, f), lambda i: (i, 0))
    return pl.pallas_call(
        forward_kernel,
        out_shape=(jax.ShapeDtypeStruct((t, f), BF),) * 3,
        grid=(t // tile,),
        in_specs=[
            pl.BlockSpec((tile, d), lambda i: (i, 0)),
            pl.BlockSpec((d, 2 * f), lambda i: (0, 0)),
        ],
        out_specs=(out,) * 3,
        compiler_params=pltpu.CompilerParams(vmem_limit_bytes=44 * 2**20),
        cost_estimate=pl.CostEstimate(
            flops=4 * t * d * f, transcendentals=t * f, bytes_accessed=2 * (t * d + 2 * d * f + 3 * t * f)
        ),
    )(x, w)


def backward_kernel(dy_ref, w_ref, act_ref, slope_ref, out_ref):
    h = act_ref.shape[1] // 2
    for k in (0, 1):
        part = slice(k * h, (k + 1) * h)
        grad = mm(dy_ref[...], w_ref[part, :], 1, 1)
        out_ref[:, 2 * k * h : (2 * k + 1) * h] = (grad * slope_ref[:, part].astype(F32)).astype(BF)
        out_ref[:, (2 * k + 1) * h : 2 * (k + 1) * h] = (
            grad * act_ref[:, part].astype(F32)
        ).astype(BF)


def backward(dy, w, act, slope):
    t, d = dy.shape
    f = w.shape[0]
    tile = 256
    given = pl.BlockSpec((tile, f), lambda i: (i, 0))
    return pl.pallas_call(
        backward_kernel,
        out_shape=jax.ShapeDtypeStruct((t, 2 * f), BF),
        grid=(t // tile,),
        in_specs=[
            pl.BlockSpec((tile, d), lambda i: (i, 0)),
            pl.BlockSpec((f, d), lambda i: (0, 0)),
            given,
            given,
        ],
        out_specs=pl.BlockSpec((tile, 2 * f), lambda i: (i, 0)),
        compiler_params=pltpu.CompilerParams(vmem_limit_bytes=44 * 2**20),
        cost_estimate=pl.CostEstimate(
            flops=2 * t * d * f, transcendentals=0, bytes_accessed=2 * (t * d + d * f + 4 * t * f)
        ),
    )(dy, w, act, slope)


def collect_kernel(plane_ref, mine, other, *refs):
    w_ref, b_ref = refs[-2:]
    w_rows = w_ref.shape[0]
    each, _, cols = mine.shape
    for plane in (0, 1):

        @pl.when(plane_ref[0] == plane)
        def _():
            for k in range(each):
                for ref, h in ((mine, plane), (other, 1 - plane)):
                    at = slice((2 * k + h) * cols, (2 * k + h + 1) * cols)
                    w_ref[:, at] = ref[k, :w_rows].astype(F32)
                    b_ref[:, at] = ref[k, w_rows:].astype(F32)


def collect(plane, mine, other, w_rows, part, given):
    n, ext, cols = mine.shape
    each = 4
    piece = pl.BlockSpec((each, ext, cols), lambda s, _: (s, 0, 0))
    held = [] if given is None else list(given)
    steps = n // each
    return pl.pallas_call(
        collect_kernel,
        out_shape=(
            jax.ShapeDtypeStruct((w_rows, 4 * n * cols), F32),
            jax.ShapeDtypeStruct((ext - w_rows, 4 * n * cols), F32),
        ),
        grid_spec=pltpu.PrefetchScalarGridSpec(
            num_scalar_prefetch=1,
            grid=(steps,),
            in_specs=[piece, piece] + [pl.BlockSpec(memory_space=pl.ANY)] * len(held),
            out_specs=(
                pl.BlockSpec((w_rows, 2 * cols * each), lambda s, _: (0, part * steps + s)),
                pl.BlockSpec((ext - w_rows, 2 * cols * each), lambda s, _: (0, part * steps + s)),
            ),
        ),
        input_output_aliases={3: 0, 4: 1} if held else {},
        cost_estimate=pl.CostEstimate(
            flops=0, transcendentals=0, bytes_accessed=12 * n * ext * cols
        ),
    )(plane, mine, other, *held)


def stack_kernel(plane_ref, mine, other, w_ref, a_ref):
    width = w_ref.shape[1]
    own = pl.program_id(0) == plane_ref[0]

    @pl.when(own)
    def _():
        w_ref[...] = mine[:, :width].astype(F32)
        a_ref[...] = mine[:, width:].astype(F32)

    @pl.when(jnp.logical_not(own))
    def _():
        w_ref[...] = other[:, :width].astype(F32)
        a_ref[...] = other[:, width:].astype(F32)


def stack(plane, mine, other, width):
    half, cols = mine.shape
    tile = min(half, 128)
    tiles = half // tile
    given = pl.BlockSpec((tile, cols), lambda h, t, _: (t, 0))
    return pl.pallas_call(
        stack_kernel,
        out_shape=(
            jax.ShapeDtypeStruct((2 * half, width), F32),
            jax.ShapeDtypeStruct((2 * half, cols - width), F32),
        ),
        grid_spec=pltpu.PrefetchScalarGridSpec(
            num_scalar_prefetch=1,
            grid=(2, tiles),
            in_specs=[given, given],
            out_specs=(
                pl.BlockSpec((tile, width), lambda h, t, _: (h * tiles + t, 0)),
                pl.BlockSpec((tile, cols - width), lambda h, t, _: (h * tiles + t, 0)),
            ),
        ),
        cost_estimate=pl.CostEstimate(
            flops=0, transcendentals=0, bytes_accessed=16 * half * cols
        ),
    )(plane, mine, other)


def body(
    tokens,
    segments,
    output_cotangent_rows,
    attention_norm_gain,
    query_key_value_matrix,
    query_key_value_adapter_first,
    query_key_value_adapter_second,
    output_matrix,
    output_adapter_first,
    output_adapter_second,
    feed_norm_gain,
    gate_up_matrix,
    gate_up_adapter_first,
    gate_up_adapter_second,
    down_matrix,
    down_adapter_first,
    down_adapter_second,
):
    n = lax.axis_size("ctx")
    me = lax.axis_index("ctx")
    plane = lax.axis_index("grp")
    lines = n // 4
    rows = tokens.shape[1]
    width = tokens.shape[2]
    seq = rows * n
    rank = query_key_value_adapter_first.shape[1]
    qkv_cols = query_key_value_matrix.shape[1]
    feed_dev = down_matrix.shape[0]
    feed_half = feed_dev // 2
    w_rows = width // n
    r_rows = rank // n
    score_scale = HD ** (-0.5)

    def hop(x, k):
        return lax.ppermute(x, "ctx", [(i, i ^ k) for i in range(n)])

    def swap(x):
        return lax.ppermute(x, "grp", [(0, 1), (1, 0)])

    def swap_pieces(x, count):
        each = x.shape[0] // count
        return [swap(x[k * each : (k + 1) * each]) for k in range(count)]

    rel = jnp.arange(n, dtype=jnp.int32)
    rel = me ^ (rel // (2 * lines) + 2 * (rel // lines % 2) + 4 * (rel % lines))

    def reorder(x):
        r = x.shape[0] // n
        order = [4 * k + 2 * j + i for i in (0, 1) for j in (0, 1) for k in range(lines)]
        return jnp.concatenate(
            [lax.dynamic_slice_in_dim(x, (me ^ k) * r, r) for k in order], axis=0
        )

    def lines_of(x):
        return [x] + [hop(x, 4 * k) for k in range(1, lines)]

    def gather_lines(along):
        near = jnp.concatenate(along + [hop(b, 2) for b in along], axis=0)
        return jnp.concatenate([near, hop(near, 1)], axis=0)

    def gather(x):
        return gather_lines(lines_of(x))

    def scatter_halves(near, far):
        arrived = hop(far, 1)
        r = near.shape[0] // (2 * lines)
        mine = [None] * (2 * lines)
        for k in range(2 * lines):
            part = slice(k * r, (k + 1) * r)
            mine[k] = near[part].astype(F32) + arrived[part].astype(F32)
        total = None
        for k in list(range(1, lines)) + [0]:
            side = hop(mine[lines + k].astype(near.dtype), 2)
            here = mine[k] + side.astype(F32)
            if k:
                here = hop(here.astype(near.dtype), 4 * k).astype(F32)
            total = here if total is None else total + here
        return total

    def scatter(partial):
        kind = partial.dtype
        half = partial.shape[0] // 2
        mine = partial[:half].astype(F32) + hop(partial[half:], 1).astype(F32)
        half = half // 2
        mine = mine[:half] + hop(mine[half:].astype(kind), 2).astype(F32)
        r = half // lines
        total = mine[:r]
        for k in range(1, lines):
            total = total + hop(mine[k * r : (k + 1) * r].astype(kind), 4 * k).astype(F32)
        return total

    x = tokens[0].astype(F32)
    dy = output_cotangent_rows[0]
    plane_id = plane.astype(jnp.int32).reshape(1)
    ext = w_rows + r_rows

    def beside(second):
        return second.reshape(w_rows, second.shape[1] * r_rows // w_rows)

    def apart(columns):
        return columns.reshape(rank, columns.shape[1] * w_rows // r_rows)

    q_second = qkv_cols * r_rows // w_rows
    o_second = width * r_rows // w_rows
    at_q = qkv_cols + rank
    pad = -(at_q + q_second) % 128
    gains = jnp.concatenate(
        [
            attention_norm_gain[:, None],
            feed_norm_gain[:, None],
            jnp.zeros((w_rows, pad - 2), BF),
        ],
        axis=1,
    )
    qkv_ext = jnp.concatenate(
        [
            query_key_value_matrix,
            query_key_value_adapter_first,
            beside(query_key_value_adapter_second),
            gains,
        ],
        axis=1,
    )
    qkv_got = lax.all_gather(qkv_ext, "ctx", axis=0, tiled=True)
    out_ext = jnp.concatenate(
        [
            output_matrix,
            output_adapter_first,
            gate_up_adapter_first,
            beside(output_adapter_second),
            beside(down_adapter_second),
        ],
        axis=1,
    )
    out_got = lax.all_gather(out_ext, "ctx", axis=0, tiled=True)
    qkv_full = qkv_got[:, :at_q]
    qkv_second = apart(qkv_got[:, at_q : at_q + q_second])
    gains_full = qkv_got[:, at_q + q_second : at_q + q_second + 2].astype(F32).T
    attn_gain, feed_gain = gains_full[:1], gains_full[1:]
    out_full = out_got[:, : width + rank]
    gate_up_first = out_got[:, width + rank : width + 2 * rank]
    out_second = apart(out_got[:, width + 2 * rank : width + 2 * rank + o_second])
    down_second = apart(out_got[:, width + 2 * rank + o_second :])

    def exchange(pieces):
        flat = pieces.reshape(n * ext, feed_half)
        return lax.all_to_all(flat, "ctx", 0, 0, tiled=True).reshape(n, ext, feed_half)

    gate_mine = exchange(deal_out(0, plane_id, gate_up_matrix, gate_up_adapter_second, n))
    up_sent = deal_out(1, plane_id, gate_up_matrix, gate_up_adapter_second, n)

    def own_first(x):
        pair = x.reshape(2, feed_half, x.shape[1])
        a = lax.dynamic_index_in_dim(pair, plane, 0, False)
        b = lax.dynamic_index_in_dim(pair, 1 - plane, 0, False)
        return jnp.concatenate([a, b], axis=0)

    down_first = own_first(down_adapter_first)
    down_eff = (own_first(down_matrix).astype(F32) + mm(down_first, down_second)).astype(BF)

    def positions(device):
        within = jnp.arange(rows, dtype=jnp.int32)
        half = rows // 2
        block = jnp.where(within < half, device[:, None], 2 * n - 1 - device[:, None])
        return block * half + within % half

    local_pos = positions(me[None])[0]
    key_pos = positions(rel).reshape(seq)
    half = rows // 2
    local_seg = jnp.concatenate(
        [
            lax.dynamic_slice_in_dim(segments[0], me * half, half),
            lax.dynamic_slice_in_dim(segments[0], (2 * n - 1 - me) * half, half),
        ]
    )
    doc_start = jnp.sum(
        (segments[0][None, :] < local_seg[:, None]).astype(jnp.int32), axis=1
    )
    allowed = (key_pos[None, :] >= doc_start[:, None]) & (key_pos[None, :] <= local_pos[:, None])
    frequency = rope_base ** (-2.0 * jnp.arange(HD // 2, dtype=F32) / HD)
    angle_rows = local_pos.astype(F32)[:, None] * frequency[None, :]
    cosine, sine_rows = jnp.cos(angle_rows), jnp.sin(angle_rows)

    inv_one = inv_rms(x)
    norm_one = (x * inv_one * (1.0 + attn_gain)).astype(BF)
    norm_one = after(norm_one, gate_mine, up_sent)
    qkv_base = mm(norm_one, qkv_full)
    inner_qkv = qkv_base[:, qkv_cols:].astype(BF)
    qkv = qkv_base[:, :qkv_cols] + mm(inner_qkv, qkv_second)
    q = rotate(
        qkv[:, :width].reshape(rows, HEADS, HD), cosine[:, None, :], sine_rows[:, None, :]
    ).astype(BF)
    q_flat = q.reshape(rows * HEADS, HD)
    k_mine = rotate(qkv[:, width : width + HD], cosine, sine_rows).astype(BF)
    kv_mine = jnp.concatenate([k_mine, qkv[:, width + HD :].astype(BF)], axis=1)
    kv_all = gather(kv_mine)
    dy_got = lax.all_gather(after(dy, kv_mine), "ctx", axis=0, tiled=True)
    up_mine = exchange(after(up_sent, kv_all))
    gate_pieces = swap_pieces(gate_mine, 2)
    kv_all = after(kv_all, gate_pieces[0])
    k_all, v_all = kv_all[:, :HD], kv_all[:, HD:]
    raw = mm(q_flat, k_all, 1, 1).reshape(rows, HEADS, seq) * score_scale
    scores = jnp.where(allowed[:, None, :], raw, -jnp.inf)
    peak = jnp.max(scores, axis=-1, keepdims=True)
    unnormed = jnp.exp(scores - peak)
    total = jnp.sum(unnormed, axis=-1, keepdims=True)
    probs = (unnormed / total).astype(BF).reshape(rows * HEADS, seq)
    attended_f = mm(after(probs, gate_pieces[1]), v_all)
    gate_other = jnp.concatenate(gate_pieces, axis=0)
    attended = attended_f.reshape(rows, width).astype(BF)
    attended = after(attended, up_mine)
    up_pieces = swap_pieces(up_mine, 2)
    out_base = mm(attended, out_full)
    inner_out = out_base[:, width:].astype(BF)
    mid = x + out_base[:, :width] + mm(inner_out, out_second)

    inv_two = inv_rms(mid)
    norm_two = (mid * inv_two * (1.0 + feed_gain)).astype(BF)
    all_rows = gather(norm_two)
    all_dy = reorder(dy_got)
    up_other = jnp.concatenate(up_pieces, axis=0)
    w_eff, (gate_b, up_b) = fold(gate_mine, up_mine, gate_up_first, 0, None)
    w_eff, _ = fold(gate_other, up_other, gate_up_first, 1, w_eff)
    hidden, act, slope = forward(all_rows, w_eff)
    h = feed_half
    half_seq = seq // 2
    down_part = mm(hidden[:, h:], all_dy, 0, 0).astype(BF)
    grads = backward(after(all_dy, down_part), down_eff, act, slope)
    down_pieces = swap_pieces(down_part, 4)
    grads = after(grads, down_pieces[0])
    far_part = mm(grads[half_seq:], w_eff, 1, 1).astype(BF)
    near_part = mm(after(grads[:half_seq], far_part, down_pieces[1]), w_eff, 1, 1).astype(BF)
    grad_norm_two = scatter_halves(near_part, far_part)

    late_rows, late_grads = lax.optimization_barrier(
        (all_rows, grads, near_part, down_pieces[2])
    )[:2]
    other_part = mm(late_rows, late_grads[:, 2 * h :], 0, 0).astype(BF)
    gate_pieces, up_pieces = swap_pieces(other_part[:, :h], 4), swap_pieces(other_part[:, h:], 4)
    out_part = mm(after(hidden, other_part, down_pieces[3]), down_eff).astype(BF)
    down_part = jnp.concatenate(down_pieces, axis=0)
    down_half = (
        mm(after(hidden, out_part, gate_pieces[0])[:, :h], all_dy, 0, 0) + down_part.astype(F32)
    ).astype(BF)
    g_down_first = mm(down_half, down_second, 1, 1).astype(BF)
    down_rows = jnp.concatenate([down_half, g_down_first], axis=1)

    pieces = jnp.concatenate(
        [
            norm_one.reshape(rows, n, w_rows),
            inner_qkv.reshape(rows, n, r_rows),
            attended.reshape(rows, n, w_rows),
            inner_out.reshape(rows, n, r_rows),
        ],
        axis=2,
    ).transpose(1, 0, 2)
    pieces = after(pieces, all_rows)
    inputs = lax.all_to_all(pieces.reshape(seq, 2 * ext), "ctx", 0, 0, tiled=True)

    grad_norm_two = after(grad_norm_two, down_rows, inputs, *gate_pieces[:2])
    feed_gain_rows = jnp.sum(grad_norm_two * mid * inv_two, axis=0, keepdims=True)
    grad_mid = dy.astype(F32) + norm_back(mid, inv_two, feed_gain, grad_norm_two)
    grad_branch = grad_mid.astype(BF)
    branch_all = lax.all_gather(grad_branch, "ctx", axis=0, tiled=True)
    grad_inner_out = mm(grad_branch, out_second, 1, 1).astype(BF)
    grad_attended = mm(
        jnp.concatenate([grad_branch, grad_inner_out], axis=1), out_full, 1, 1
    )
    delta = jnp.sum(
        (grad_attended * attended.astype(F32)).reshape(rows * HEADS, HD), axis=1, keepdims=True
    )
    grad_flat = grad_attended.astype(BF).reshape(rows * HEADS, HD)
    gate_part = jnp.concatenate(gate_pieces, axis=0)
    gate_half = (
        mm(after(all_rows, grad_flat), grads[:, :h], 0, 0) + gate_part.astype(F32)
    ).astype(BF)
    gate_second = mm(gate_up_first, gate_half, 0, 0).astype(BF)
    gate_ext = jnp.concatenate(
        [gate_half.reshape(n, w_rows, h), gate_second.reshape(n, r_rows, h)], axis=1
    )
    gate_got = exchange(gate_ext)
    grad_flat = after(grad_flat, gate_ext, up_pieces[0])
    grad_probs = mm(grad_flat, v_all, 1, 1)
    grad_scores = (probs.astype(F32) * (grad_probs - delta)).astype(BF)
    grad_scores = after(grad_scores, up_pieces[1])
    grad_k = mm(grad_scores, q_flat, 0, 0) * score_scale
    grad_v = mm(probs, grad_flat, 0, 0)
    kv_part = jnp.concatenate([grad_k, grad_v], axis=1).astype(BF)
    grad_kv = scatter(kv_part)
    grad_q = mm(after(grad_scores, kv_part, up_pieces[2]), k_all) * score_scale
    grad_q_rows = (
        rotate(grad_q.reshape(rows, HEADS, HD), cosine[:, None, :], -sine_rows[:, None, :])
        .reshape(rows, width)
        .astype(BF)
    )
    q_all = lax.all_gather(grad_q_rows, "ctx", axis=0, tiled=True)
    up_part = jnp.concatenate(up_pieces, axis=0)
    up_half = (
        mm(after(all_rows, grad_q_rows), grads[:, h : 2 * h], 0, 0) + up_part.astype(F32)
    ).astype(BF)
    down_back = swap(after(down_rows, up_half))
    grad_kv = after(grad_kv, up_half, grad_q_rows)
    grad_k_rows = rotate(grad_kv[:, :HD], cosine, -sine_rows)
    grad_kv_rows = jnp.concatenate([grad_k_rows, grad_kv[:, HD:]], axis=1).astype(BF)
    kv_all_grads = gather(grad_kv_rows)
    up_second = mm(gate_up_first, after(up_half, grad_kv_rows), 0, 0).astype(BF)
    up_ext = jnp.concatenate(
        [up_half.reshape(n, w_rows, h), up_second.reshape(n, r_rows, h)], axis=1
    )
    up_ext = after(up_ext, gate_got)
    up_got = exchange(up_ext)
    grad_qkv = jnp.concatenate([grad_q_rows, grad_kv_rows], axis=1)
    grad_qkv = after(grad_qkv, up_ext)
    grad_inner_qkv = mm(grad_qkv, qkv_second, 1, 1).astype(BF)
    grad_norm_one = mm(
        jnp.concatenate([grad_qkv, grad_inner_qkv], axis=1), qkv_full, 1, 1
    )
    attn_gain_rows = jnp.sum(grad_norm_one * x * inv_one, axis=0, keepdims=True)
    grad_input = (grad_mid + norm_back(x, inv_one, attn_gain, grad_norm_one)).astype(BF)
    gate_back = swap_pieces(gate_got, 2)

    def both_planes(own):
        own = own.astype(BF)
        return own.astype(F32) + swap(own).astype(F32)

    g_out = mm(inputs[:, ext:], after(branch_all, grad_input), 0, 0).astype(BF)

    small = jnp.concatenate(
        [
            (mm(gate_half, gate_b, 1, 1) + mm(up_half, up_b, 1, 1))
            .astype(BF)
            .reshape(n, w_rows, rank),
            mm(down_first[:h], after(down_half, g_out), 0, 0)
            .astype(BF)
            .reshape(n, w_rows, width * r_rows // w_rows),
        ],
        axis=2,
    )
    small = after(small, g_out)
    small = scatter(reorder(small.reshape(n * w_rows, small.shape[2])))
    gain_rows = jnp.concatenate([attn_gain_rows, feed_gain_rows], axis=0)
    gain_rows = gain_rows.reshape(2, n, w_rows).transpose(1, 0, 2).reshape(2 * n, w_rows)
    gain_rows = scatter(reorder(gain_rows))

    down_grads = stack(plane_id, down_rows, after(down_back, small), width)
    output = (mid + scatter(after(out_part, kv_all_grads, gate_back[0]))).astype(BF)
    gate_got_other = jnp.concatenate(gate_back, axis=0)
    gate_up_grads = collect(
        plane_id, gate_got, after(gate_got_other, down_grads[0]), w_rows, 0, None
    )
    up_got_other = jnp.concatenate(swap_pieces(up_got, 2), axis=0)
    gate_up_grads = collect(plane_id, up_got, up_got_other, w_rows, 1, gate_up_grads)

    g_q = mm(inputs[:, :ext], q_all, 0, 0)
    inputs_rel = reorder(inputs[:, :ext])
    g_kv = mm(inputs_rel, kv_all_grads, 0, 0)
    g_qkv = jnp.concatenate([g_q, g_kv], axis=1).astype(BF)
    g_out = both_planes(g_out)
    small = both_planes(small)
    g_qkv = both_planes(g_qkv)
    gain_rows = gain_rows + swap(gain_rows)
    g_gu_first = small[:, :rank]
    g_down_second = small[:, rank:].reshape(r_rows, width)
    g_out_first = mm(g_out[:w_rows].astype(BF), out_second, 1, 1)
    g_qkv_first = mm(g_qkv[:w_rows].astype(BF), qkv_second, 1, 1)

    return (
        output[None],
        grad_input[None],
        gain_rows[0],
        g_qkv[:w_rows],
        g_qkv_first,
        g_qkv[w_rows:],
        g_out[:w_rows],
        g_out_first,
        g_out[w_rows:],
        gain_rows[1],
        gate_up_grads[0],
        g_gu_first,
        gate_up_grads[1],
        down_grads[0],
        down_grads[1],
        g_down_second,
    )


def solution(mesh):
    rows = P("grp", "ctx", None)
    vector, matrix = P("ctx"), P("ctx", None)
    return jax.shard_map(
        body,
        mesh=mesh,
        in_specs=(rows, P("grp", None), rows, vector)
        + (matrix,) * 6
        + (vector,)
        + (matrix,) * 6,
        out_specs=(rows, rows, vector) + (matrix,) * 6 + (vector,) + (matrix,) * 6,
        check_vma=False,
    )
```

```python
import functools

import jax
import jax.numpy as jnp
from jax import lax
from jax.experimental import pallas as pl
from jax.experimental.pallas import tpu as pltpu
from jax.sharding import PartitionSpec as P

HEADS = 8
HD = 256
norm_eps = 1e-06
rope_base = 10000.0
BF = jnp.bfloat16
F32 = jnp.float32


def mm(a, b, ca=1, cb=0):
    return lax.dot_general(a, b, (((ca,), (cb,)), ((), ())), preferred_element_type=F32)


def rotate(vectors, cosine, sine_rows):
    front, back = jnp.split(vectors, 2, axis=-1)
    return jnp.concatenate(
        [front * cosine - back * sine_rows, back * cosine + front * sine_rows], axis=-1
    )


def inv_rms(values):
    return lax.rsqrt(jnp.mean(values * values, axis=-1, keepdims=True) + norm_eps)


def norm_back(values, inv, gain, grad):
    weighted = grad * (1.0 + gain)
    inner = jnp.mean(weighted * values, axis=-1, keepdims=True)
    return inv * weighted - values * (inv * inv * inv) * inner


def after(value, *others):
    return lax.optimization_barrier((value,) + others)[0]


def deal_kernel(plane_ref, *refs):
    out_ref = refs[-1]
    each = out_ref.shape[0]
    for k in range(each):
        w_ref, b_ref = refs[k], refs[each + k]
        w_rows = w_ref.shape[0]
        out_ref[k, :w_rows] = w_ref[...]
        out_ref[k, w_rows:] = b_ref[...]


def deal_out(part, plane, matrix, second, n):
    w_rows, r_rows = matrix.shape[0], second.shape[0]
    cols = matrix.shape[1] // (4 * n)
    each = 4

    def column(k, s, plane_ref):
        return (0, (part * n + s * each + k) * 2 + plane_ref[0])

    maps = [functools.partial(column, k) for k in range(each)]
    return pl.pallas_call(
        deal_kernel,
        out_shape=jax.ShapeDtypeStruct((n, w_rows + r_rows, cols), BF),
        grid_spec=pltpu.PrefetchScalarGridSpec(
            num_scalar_prefetch=1,
            grid=(n // each,),
            in_specs=[pl.BlockSpec((w_rows, cols), m) for m in maps]
            + [pl.BlockSpec((r_rows, cols), m) for m in maps],
            out_specs=pl.BlockSpec((each, w_rows + r_rows, cols), lambda s, p: (s, 0, 0)),
        ),
        cost_estimate=pl.CostEstimate(
            flops=0, transcendentals=0, bytes_accessed=4 * n * (w_rows + r_rows) * cols
        ),
    )(plane, *([matrix] * each), *([second] * each))


def fold_kernel(gate_ref, up_ref, b_gate_ref, b_up_ref, a_ref, *refs):
    out_ref = refs[-1]
    each, w_rows = gate_ref.shape[0], a_ref.shape[0] // gate_ref.shape[0]
    cols = b_gate_ref.shape[1]
    gate = mm(a_ref[...], b_gate_ref[...])
    up = mm(a_ref[...], b_up_ref[...])
    for k in range(each):
        part = slice(k * w_rows, (k + 1) * w_rows)
        out_ref[part, :cols] = (gate_ref[k, :w_rows].astype(F32) + gate[part]).astype(BF)
        out_ref[part, cols:] = (up_ref[k, :w_rows].astype(F32) + up[part]).astype(BF)


def fold(gate, up, first, place, given):
    n, ext, cols = gate.shape
    width, rank = first.shape
    w_rows = width // n
    each = max(1, min(4, 512 // w_rows))
    seconds = [x[:, w_rows:].reshape(rank, cols) for x in (gate, up)]
    piece = pl.BlockSpec((each, ext, cols), lambda s: (s, 0, 0))
    whole = pl.BlockSpec((rank, cols), lambda s: (0, 0))
    held = [] if given is None else [given]
    return pl.pallas_call(
        fold_kernel,
        out_shape=jax.ShapeDtypeStruct((width, 4 * cols), BF),
        grid=(n // each,),
        in_specs=[piece, piece, whole, whole]
        + [pl.BlockSpec((each * w_rows, rank), lambda s: (s, 0))]
        + [pl.BlockSpec(memory_space=pl.ANY)] * len(held),
        out_specs=pl.BlockSpec((each * w_rows, 2 * cols), lambda s: (s, place)),
        input_output_aliases={5: 0} if held else {},
        cost_estimate=pl.CostEstimate(
            flops=4 * width * rank * cols, transcendentals=0, bytes_accessed=8 * width * cols
        ),
    )(gate, up, *seconds, first, *held), seconds


def forward_kernel(x_ref, w_ref, hidden_ref, act_ref, slope_ref):
    h = hidden_ref.shape[1] // 2
    c = 0.7978845608028654
    for k in (0, 1):
        both = mm(x_ref[...], w_ref[:, 2 * k * h : 2 * (k + 1) * h])
        gate, up = both[:, :h], both[:, h:]
        square = gate * gate
        t = jnp.tanh(c * gate * (1.0 + 0.044715 * square))
        half_up = 0.5 * (1.0 + t)
        act = gate * half_up
        slope = half_up + 0.5 * gate * (1.0 - t * t) * (c * (1.0 + 3 * 0.044715 * square))
        part = slice(k * h, (k + 1) * h)
        hidden_ref[:, part] = (act * up).astype(BF)
        act_ref[:, part] = act.astype(BF)
        slope_ref[:, part] = (slope * up).astype(BF)


def forward(x, w):
    t, d = x.shape
    f = w.shape[1] // 2
    tile = 256
    out = pl.BlockSpec((tile, f), lambda i: (i, 0))
    return pl.pallas_call(
        forward_kernel,
        out_shape=(jax.ShapeDtypeStruct((t, f), BF),) * 3,
        grid=(t // tile,),
        in_specs=[
            pl.BlockSpec((tile, d), lambda i: (i, 0)),
            pl.BlockSpec((d, 2 * f), lambda i: (0, 0)),
        ],
        out_specs=(out,) * 3,
        compiler_params=pltpu.CompilerParams(vmem_limit_bytes=44 * 2**20),
        cost_estimate=pl.CostEstimate(
            flops=4 * t * d * f, transcendentals=t * f, bytes_accessed=2 * (t * d + 2 * d * f + 3 * t * f)
        ),
    )(x, w)


def backward_kernel(dy_ref, w_ref, act_ref, slope_ref, out_ref):
    h = act_ref.shape[1] // 2
    for k in (0, 1):
        part = slice(k * h, (k + 1) * h)
        grad = mm(dy_ref[...], w_ref[part, :], 1, 1)
        out_ref[:, 2 * k * h : (2 * k + 1) * h] = (grad * slope_ref[:, part].astype(F32)).astype(BF)
        out_ref[:, (2 * k + 1) * h : 2 * (k + 1) * h] = (
            grad * act_ref[:, part].astype(F32)
        ).astype(BF)


def backward(dy, w, act, slope):
    t, d = dy.shape
    f = w.shape[0]
    tile = 256
    given = pl.BlockSpec((tile, f), lambda i: (i, 0))
    return pl.pallas_call(
        backward_kernel,
        out_shape=jax.ShapeDtypeStruct((t, 2 * f), BF),
        grid=(t // tile,),
        in_specs=[
            pl.BlockSpec((tile, d), lambda i: (i, 0)),
            pl.BlockSpec((f, d), lambda i: (0, 0)),
            given,
            given,
        ],
        out_specs=pl.BlockSpec((tile, 2 * f), lambda i: (i, 0)),
        compiler_params=pltpu.CompilerParams(vmem_limit_bytes=44 * 2**20),
        cost_estimate=pl.CostEstimate(
            flops=2 * t * d * f, transcendentals=0, bytes_accessed=2 * (t * d + d * f + 4 * t * f)
        ),
    )(dy, w, act, slope)


def collect_kernel(plane_ref, mine, other, *refs):
    w_ref, b_ref = refs[-2:]
    w_rows = w_ref.shape[0]
    each, _, cols = mine.shape
    for plane in (0, 1):

        @pl.when(plane_ref[0] == plane)
        def _():
            for k in range(each):
                for ref, h in ((mine, plane), (other, 1 - plane)):
                    at = slice((2 * k + h) * cols, (2 * k + h + 1) * cols)
                    w_ref[:, at] = ref[k, :w_rows].astype(F32)
                    b_ref[:, at] = ref[k, w_rows:].astype(F32)


def collect(plane, mine, other, w_rows, part, given):
    n, ext, cols = mine.shape
    each = 4
    piece = pl.BlockSpec((each, ext, cols), lambda s, _: (s, 0, 0))
    held = [] if given is None else list(given)
    steps = n // each
    return pl.pallas_call(
        collect_kernel,
        out_shape=(
            jax.ShapeDtypeStruct((w_rows, 4 * n * cols), F32),
            jax.ShapeDtypeStruct((ext - w_rows, 4 * n * cols), F32),
        ),
        grid_spec=pltpu.PrefetchScalarGridSpec(
            num_scalar_prefetch=1,
            grid=(steps,),
            in_specs=[piece, piece] + [pl.BlockSpec(memory_space=pl.ANY)] * len(held),
            out_specs=(
                pl.BlockSpec((w_rows, 2 * cols * each), lambda s, _: (0, part * steps + s)),
                pl.BlockSpec((ext - w_rows, 2 * cols * each), lambda s, _: (0, part * steps + s)),
            ),
        ),
        input_output_aliases={3: 0, 4: 1} if held else {},
        cost_estimate=pl.CostEstimate(
            flops=0, transcendentals=0, bytes_accessed=12 * n * ext * cols
        ),
    )(plane, mine, other, *held)


def stack_kernel(plane_ref, mine, other, w_ref, a_ref):
    width = w_ref.shape[1]
    own = pl.program_id(0) == plane_ref[0]

    @pl.when(own)
    def _():
        w_ref[...] = mine[:, :width].astype(F32)
        a_ref[...] = mine[:, width:].astype(F32)

    @pl.when(jnp.logical_not(own))
    def _():
        w_ref[...] = other[:, :width].astype(F32)
        a_ref[...] = other[:, width:].astype(F32)


def stack(plane, mine, other, width):
    half, cols = mine.shape
    tile = min(half, 128)
    tiles = half // tile
    given = pl.BlockSpec((tile, cols), lambda h, t, _: (t, 0))
    return pl.pallas_call(
        stack_kernel,
        out_shape=(
            jax.ShapeDtypeStruct((2 * half, width), F32),
            jax.ShapeDtypeStruct((2 * half, cols - width), F32),
        ),
        grid_spec=pltpu.PrefetchScalarGridSpec(
            num_scalar_prefetch=1,
            grid=(2, tiles),
            in_specs=[given, given],
            out_specs=(
                pl.BlockSpec((tile, width), lambda h, t, _: (h * tiles + t, 0)),
                pl.BlockSpec((tile, cols - width), lambda h, t, _: (h * tiles + t, 0)),
            ),
        ),
        cost_estimate=pl.CostEstimate(
            flops=0, transcendentals=0, bytes_accessed=16 * half * cols
        ),
    )(plane, mine, other)


def body(
    tokens,
    segments,
    output_cotangent_rows,
    attention_norm_gain,
    query_key_value_matrix,
    query_key_value_adapter_first,
    query_key_value_adapter_second,
    output_matrix,
    output_adapter_first,
    output_adapter_second,
    feed_norm_gain,
    gate_up_matrix,
    gate_up_adapter_first,
    gate_up_adapter_second,
    down_matrix,
    down_adapter_first,
    down_adapter_second,
):
    n = lax.axis_size("ctx")
    me = lax.axis_index("ctx")
    plane = lax.axis_index("grp")
    lines = n // 4
    rows = tokens.shape[1]
    width = tokens.shape[2]
    seq = rows * n
    rank = query_key_value_adapter_first.shape[1]
    qkv_cols = query_key_value_matrix.shape[1]
    feed_dev = down_matrix.shape[0]
    feed_half = feed_dev // 2
    w_rows = width // n
    r_rows = rank // n
    score_scale = HD ** (-0.5)

    def hop(x, k):
        return lax.ppermute(x, "ctx", [(i, i ^ k) for i in range(n)])

    def swap(x):
        return lax.ppermute(x, "grp", [(0, 1), (1, 0)])

    def swap_pieces(x, count):
        each = x.shape[0] // count
        return [swap(x[k * each : (k + 1) * each]) for k in range(count)]

    rel = jnp.arange(n, dtype=jnp.int32)
    rel = me ^ (rel // (2 * lines) + 2 * (rel // lines % 2) + 4 * (rel % lines))

    def reorder(x):
        r = x.shape[0] // n
        order = [4 * k + 2 * j + i for i in (0, 1) for j in (0, 1) for k in range(lines)]
        return jnp.concatenate(
            [lax.dynamic_slice_in_dim(x, (me ^ k) * r, r) for k in order], axis=0
        )

    def lines_of(x):
        return [x] + [hop(x, 4 * k) for k in range(1, lines)]

    def gather_near(x):
        along = lines_of(x)
        return jnp.concatenate(along + [hop(b, 2) for b in along], axis=0)

    def gather(x):
        near = gather_near(x)
        return jnp.concatenate([near, hop(near, 1)], axis=0)

    def fold_core(near, arrived):
        r = near.shape[0] // (2 * lines)
        parts = [slice(k * r, (k + 1) * r) for k in range(2 * lines)]
        both = [near[p].astype(F32) + arrived[p].astype(F32) for p in parts]
        return both[:lines], [x.astype(near.dtype) for x in both[lines:]]

    def all_after(values, *others):
        return lax.optimization_barrier((*values, *others))[: len(values)]

    def scatter(near, far):
        kind = near.dtype
        mine = near.astype(F32) + hop(far, 1).astype(F32)
        half = near.shape[0] // 2
        mine = mine[:half] + hop(mine[half:].astype(kind), 2).astype(F32)
        r = half // lines
        total = mine[:r]
        for k in range(1, lines):
            total = total + hop(mine[k * r : (k + 1) * r].astype(kind), 4 * k).astype(F32)
        return total

    def scatter_whole(partial):
        half = partial.shape[0] // 2
        return scatter(partial[:half], partial[half:])

    x = tokens[0].astype(F32)
    dy = output_cotangent_rows[0]
    plane_id = plane.astype(jnp.int32).reshape(1)
    ext = w_rows + r_rows

    def beside(second):
        return second.reshape(w_rows, second.shape[1] * r_rows // w_rows)

    def apart(columns):
        return columns.reshape(rank, columns.shape[1] * w_rows // r_rows)

    q_second = qkv_cols * r_rows // w_rows
    o_second = width * r_rows // w_rows
    at_q = qkv_cols + rank
    pad = -(at_q + q_second) % 128
    gains = jnp.concatenate(
        [
            attention_norm_gain[:, None],
            feed_norm_gain[:, None],
            jnp.zeros((w_rows, pad - 2), BF),
        ],
        axis=1,
    )
    qkv_ext = jnp.concatenate(
        [
            query_key_value_matrix,
            query_key_value_adapter_first,
            beside(query_key_value_adapter_second),
            gains,
        ],
        axis=1,
    )
    qkv_got = lax.all_gather(qkv_ext, "ctx", axis=0, tiled=True)
    out_ext = jnp.concatenate(
        [
            output_matrix,
            output_adapter_first,
            gate_up_adapter_first,
            beside(output_adapter_second),
            beside(down_adapter_second),
        ],
        axis=1,
    )
    out_got = lax.all_gather(out_ext, "ctx", axis=0, tiled=True)
    qkv_full = qkv_got[:, :at_q]
    qkv_second = apart(qkv_got[:, at_q : at_q + q_second])
    gains_full = qkv_got[:, at_q + q_second : at_q + q_second + 2].astype(F32).T
    attn_gain, feed_gain = gains_full[:1], gains_full[1:]

    def exchange(pieces):
        flat = pieces.reshape(n * ext, feed_half)
        return lax.all_to_all(flat, "ctx", 0, 0, tiled=True).reshape(n, ext, feed_half)

    gate_mine = exchange(deal_out(0, plane_id, gate_up_matrix, gate_up_adapter_second, n))
    up_sent = deal_out(1, plane_id, gate_up_matrix, gate_up_adapter_second, n)

    def own_first(x):
        pair = x.reshape(2, feed_half, x.shape[1])
        a = lax.dynamic_index_in_dim(pair, plane, 0, False)
        b = lax.dynamic_index_in_dim(pair, 1 - plane, 0, False)
        return jnp.concatenate([a, b], axis=0)

    down_first, down_rows = own_first(down_adapter_first), own_first(down_matrix)

    def positions(device):
        within = jnp.arange(rows, dtype=jnp.int32)
        half = rows // 2
        block = jnp.where(within < half, device[:, None], 2 * n - 1 - device[:, None])
        return block * half + within % half

    local_pos = positions(me[None])[0]
    key_pos = positions(rel).reshape(seq)
    half = rows // 2
    local_seg = jnp.concatenate(
        [
            lax.dynamic_slice_in_dim(segments[0], me * half, half),
            lax.dynamic_slice_in_dim(segments[0], (2 * n - 1 - me) * half, half),
        ]
    )
    doc_start = jnp.sum(
        (segments[0][None, :] < local_seg[:, None]).astype(jnp.int32), axis=1
    )
    allowed = (key_pos[None, :] >= doc_start[:, None]) & (key_pos[None, :] <= local_pos[:, None])
    frequency = rope_base ** (-2.0 * jnp.arange(HD // 2, dtype=F32) / HD)
    angle_rows = local_pos.astype(F32)[:, None] * frequency[None, :]
    cosine, sine_rows = jnp.cos(angle_rows), jnp.sin(angle_rows)

    inv_one = inv_rms(x)
    norm_one = (x * inv_one * (1.0 + attn_gain)).astype(BF)
    norm_one = after(norm_one, gate_mine, up_sent)
    qkv_base = mm(norm_one, qkv_full)
    inner_qkv = qkv_base[:, qkv_cols:].astype(BF)
    qkv = qkv_base[:, :qkv_cols] + mm(inner_qkv, qkv_second)
    q = rotate(
        qkv[:, :width].reshape(rows, HEADS, HD), cosine[:, None, :], sine_rows[:, None, :]
    ).astype(BF)
    q_flat = q.reshape(rows * HEADS, HD)
    k_mine = rotate(qkv[:, width : width + HD], cosine, sine_rows).astype(BF)
    kv_mine = jnp.concatenate([k_mine, qkv[:, width + HD :].astype(BF)], axis=1)
    kv_all = gather(kv_mine)
    dy_got = lax.all_gather(after(dy, kv_mine), "ctx", axis=0, tiled=True)
    up_mine = exchange(after(up_sent, kv_all))
    gate_pieces = swap_pieces(gate_mine, 2)
    kv_all = after(kv_all, gate_pieces[0])
    k_all, v_all = kv_all[:, :HD], kv_all[:, HD:]
    raw = mm(q_flat, k_all, 1, 1).reshape(rows, HEADS, seq) * score_scale
    scores = jnp.where(allowed[:, None, :], raw, -jnp.inf)
    peak = jnp.max(scores, axis=-1, keepdims=True)
    unnormed = jnp.exp(scores - peak)
    total = jnp.sum(unnormed, axis=-1, keepdims=True)
    probs = (unnormed / total).astype(BF).reshape(rows * HEADS, seq)
    out_got = after(out_got, probs)
    out_full = out_got[:, : width + rank]
    gate_up_first = out_got[:, width + rank : width + 2 * rank]
    out_second = apart(out_got[:, width + 2 * rank : width + 2 * rank + o_second])
    down_second = apart(out_got[:, width + 2 * rank + o_second :])
    down_eff = (down_rows.astype(F32) + mm(down_first, down_second)).astype(BF)
    attended_f = mm(after(probs, gate_pieces[1]), v_all)
    gate_other = jnp.concatenate(gate_pieces, axis=0)
    attended = attended_f.reshape(rows, width).astype(BF)
    attended = after(attended, up_mine)
    up_pieces = swap_pieces(up_mine, 2)
    out_base = mm(attended, out_full)
    inner_out = out_base[:, width:].astype(BF)
    mid = x + out_base[:, :width] + mm(inner_out, out_second)

    inv_two = inv_rms(mid)
    norm_two = (mid * inv_two * (1.0 + feed_gain)).astype(BF)
    near_rows = gather_near(norm_two)
    all_dy = reorder(dy_got)
    up_other = jnp.concatenate(up_pieces, axis=0)
    w_eff, (gate_b, up_b) = fold(gate_mine, up_mine, gate_up_first, 0, None)
    w_eff, _ = fold(gate_other, up_other, gate_up_first, 1, w_eff)
    near_rows = after(near_rows, w_eff, down_eff)
    all_rows = jnp.concatenate([near_rows, hop(near_rows, 1)], axis=0)
    hidden, act, slope = forward(after(all_rows, all_dy), w_eff)
    h = feed_half
    half_seq = seq // 2
    down_part = mm(hidden[:, h:], all_dy, 0, 0).astype(BF)
    grads = backward(after(all_dy, down_part), down_eff, act, slope)
    down_part = swap(down_part)
    far_part = mm(grads[half_seq:], w_eff, 1, 1).astype(BF)
    near_part = mm(after(grads, far_part)[:half_seq], w_eff, 1, 1).astype(BF)
    here, there = fold_core(near_part, hop(far_part, 1))
    sides = [hop(part, 2) for part in there]

    late_rows, late_grads = lax.optimization_barrier(
        (all_rows, grads, near_part, *there)
    )[:2]
    other_part = mm(late_rows, late_grads[:, 2 * h :], 0, 0).astype(BF)
    gate_part, up_part = swap(other_part[:, :h]), swap(other_part[:, h:])
    sides = all_after(sides, other_part)
    sums = [a + b.astype(F32) for a, b in zip(here, sides)]
    line_sums = [part.astype(BF) for part in sums[1:]]
    arrivals = [hop(part, 4 * (k + 1)) for k, part in enumerate(line_sums)]
    late_hidden = after(hidden, other_part)
    out_far = mm(late_hidden[half_seq:], down_eff).astype(BF)
    out_near = mm(late_hidden[:half_seq], down_eff).astype(BF)
    down_half = (
        mm(after(hidden, other_part)[:, :h], all_dy, 0, 0) + down_part.astype(F32)
    ).astype(BF)
    g_down_first = mm(down_half, down_second, 1, 1).astype(BF)
    down_rows = jnp.concatenate([down_half, g_down_first], axis=1)

    late_rows = after(all_rows, down_rows, out_near, out_far, *line_sums)
    gate_half = (mm(late_rows, grads[:, :h], 0, 0) + gate_part.astype(F32)).astype(BF)

    pieces = jnp.concatenate(
        [
            norm_one.reshape(rows, n, w_rows),
            inner_qkv.reshape(rows, n, r_rows),
            attended.reshape(rows, n, w_rows),
            inner_out.reshape(rows, n, r_rows),
        ],
        axis=2,
    ).transpose(1, 0, 2)
    pieces = after(pieces, all_rows)
    inputs = lax.all_to_all(pieces.reshape(seq, 2 * ext), "ctx", 0, 0, tiled=True)

    arrivals = all_after(arrivals, gate_half, inputs)
    grad_norm_two = sums[0] + sum(part.astype(F32) for part in arrivals)
    feed_gain_rows = jnp.sum(grad_norm_two * mid * inv_two, axis=0, keepdims=True)
    grad_mid = dy.astype(F32) + norm_back(mid, inv_two, feed_gain, grad_norm_two)
    grad_branch = grad_mid.astype(BF)
    branch_all = lax.all_gather(grad_branch, "ctx", axis=0, tiled=True)
    grad_inner_out = mm(grad_branch, out_second, 1, 1).astype(BF)
    grad_attended = mm(
        jnp.concatenate([grad_branch, grad_inner_out], axis=1), out_full, 1, 1
    )
    delta = jnp.sum(
        (grad_attended * attended.astype(F32)).reshape(rows * HEADS, HD), axis=1, keepdims=True
    )
    grad_flat = grad_attended.astype(BF).reshape(rows * HEADS, HD)
    gate_second = mm(gate_up_first, gate_half, 0, 0).astype(BF)
    gate_ext = jnp.concatenate(
        [gate_half.reshape(n, w_rows, h), gate_second.reshape(n, r_rows, h)], axis=1
    )
    gate_got = exchange(gate_ext)
    grad_flat = after(grad_flat, gate_ext)
    grad_probs = mm(grad_flat, v_all, 1, 1)
    grad_scores = (probs.astype(F32) * (grad_probs - delta)).astype(BF)
    grad_scores = after(grad_scores, up_part)
    grad_k = mm(grad_scores, q_flat, 0, 0) * score_scale
    grad_v = mm(probs, grad_flat, 0, 0)
    kv_part = jnp.concatenate([grad_k, grad_v], axis=1).astype(BF)
    grad_kv = scatter_whole(kv_part)
    grad_q = mm(after(grad_scores, kv_part), k_all) * score_scale
    grad_q_rows = (
        rotate(grad_q.reshape(rows, HEADS, HD), cosine[:, None, :], -sine_rows[:, None, :])
        .reshape(rows, width)
        .astype(BF)
    )
    q_all = lax.all_gather(grad_q_rows, "ctx", axis=0, tiled=True)
    up_half = (
        mm(after(all_rows, grad_q_rows, gate_got), grads[:, h : 2 * h], 0, 0)
        + up_part.astype(F32)
    ).astype(BF)
    down_back = swap(after(down_rows, up_part))
    grad_kv = after(grad_kv, up_half, down_back)
    grad_k_rows = rotate(grad_kv[:, :HD], cosine, -sine_rows)
    grad_kv_rows = jnp.concatenate([grad_k_rows, grad_kv[:, HD:]], axis=1).astype(BF)
    kv_all_grads = gather(grad_kv_rows)
    up_second = mm(gate_up_first, after(up_half, grad_kv_rows), 0, 0).astype(BF)
    up_ext = jnp.concatenate(
        [up_half.reshape(n, w_rows, h), up_second.reshape(n, r_rows, h)], axis=1
    )
    up_ext = after(up_ext, gate_got)
    up_got = exchange(up_ext)
    grad_qkv = jnp.concatenate([grad_q_rows, grad_kv_rows], axis=1)
    grad_qkv = after(grad_qkv, up_ext)
    grad_inner_qkv = mm(grad_qkv, qkv_second, 1, 1).astype(BF)
    grad_norm_one = mm(
        jnp.concatenate([grad_qkv, grad_inner_qkv], axis=1), qkv_full, 1, 1
    )
    attn_gain_rows = jnp.sum(grad_norm_one * x * inv_one, axis=0, keepdims=True)
    grad_input = (grad_mid + norm_back(x, inv_one, attn_gain, grad_norm_one)).astype(BF)
    gate_back = swap(after(gate_got, down_back))
    output = (mid + scatter(out_near, after(out_far, kv_all_grads))).astype(BF)

    def both_planes(own):
        own = own.astype(BF)
        return own.astype(F32) + swap(own).astype(F32)

    g_out = mm(inputs[:, ext:], after(branch_all, grad_input), 0, 0).astype(BF)

    small = jnp.concatenate(
        [
            (mm(gate_half, gate_b, 1, 1) + mm(up_half, up_b, 1, 1))
            .astype(BF)
            .reshape(n, w_rows, rank),
            mm(down_first[:h], after(down_half, g_out), 0, 0)
            .astype(BF)
            .reshape(n, w_rows, width * r_rows // w_rows),
        ],
        axis=2,
    )
    small = after(small, g_out)
    small = scatter_whole(reorder(small.reshape(n * w_rows, small.shape[2])))
    gain_rows = jnp.concatenate([attn_gain_rows, feed_gain_rows], axis=0)
    gain_rows = gain_rows.reshape(2, n, w_rows).transpose(1, 0, 2).reshape(2 * n, w_rows)
    gain_rows = scatter_whole(reorder(gain_rows))

    down_grads = stack(plane_id, down_rows, after(down_back, small), width)
    gate_up_grads = collect(
        plane_id, gate_got, after(gate_back, down_grads[0]), w_rows, 0, None
    )
    up_got_other = swap(after(up_got, gate_back))
    gate_up_grads = collect(plane_id, up_got, up_got_other, w_rows, 1, gate_up_grads)

    g_q = mm(inputs[:, :ext], q_all, 0, 0)
    inputs_rel = reorder(inputs[:, :ext])
    g_kv = mm(inputs_rel, kv_all_grads, 0, 0)
    g_qkv = jnp.concatenate([g_q, g_kv], axis=1).astype(BF)
    g_out = both_planes(after(g_out, gate_back))
    small = both_planes(after(small, gate_back))
    g_qkv = both_planes(g_qkv)
    gain_rows = gain_rows + swap(after(gain_rows, up_got_other))
    g_gu_first = small[:, :rank]
    g_down_second = small[:, rank:].reshape(r_rows, width)
    g_out_first = mm(g_out[:w_rows].astype(BF), out_second, 1, 1)
    g_qkv_first = mm(g_qkv[:w_rows].astype(BF), qkv_second, 1, 1)

    return (
        output[None],
        grad_input[None],
        gain_rows[0],
        g_qkv[:w_rows],
        g_qkv_first,
        g_qkv[w_rows:],
        g_out[:w_rows],
        g_out_first,
        g_out[w_rows:],
        gain_rows[1],
        gate_up_grads[0],
        g_gu_first,
        gate_up_grads[1],
        down_grads[0],
        down_grads[1],
        g_down_second,
    )


def solution(mesh):
    rows = P("grp", "ctx", None)
    vector, matrix = P("ctx"), P("ctx", None)
    return jax.shard_map(
        body,
        mesh=mesh,
        in_specs=(rows, P("grp", None), rows, vector)
        + (matrix,) * 6
        + (vector,)
        + (matrix,) * 6,
        out_specs=(rows, rows, vector) + (matrix,) * 6 + (vector,) + (matrix,) * 6,
        check_vma=False,
    )
```

```python
import functools

import jax
import jax.numpy as jnp
from jax import lax
from jax.experimental import pallas as pl
from jax.experimental.pallas import tpu as pltpu
from jax.sharding import PartitionSpec as P

HEADS = 8
HD = 256
norm_eps = 1e-06
rope_base = 10000.0
BF = jnp.bfloat16
F32 = jnp.float32


def mm(a, b, ca=1, cb=0):
    return lax.dot_general(a, b, (((ca,), (cb,)), ((), ())), preferred_element_type=F32)


def rotate(vectors, cosine, sine_rows):
    front, back = jnp.split(vectors, 2, axis=-1)
    return jnp.concatenate(
        [front * cosine - back * sine_rows, back * cosine + front * sine_rows], axis=-1
    )


def inv_rms(values):
    return lax.rsqrt(jnp.mean(values * values, axis=-1, keepdims=True) + norm_eps)


def norm_back(values, inv, gain, grad):
    weighted = grad * (1.0 + gain)
    inner = jnp.mean(weighted * values, axis=-1, keepdims=True)
    return inv * weighted - values * (inv * inv * inv) * inner


def after(value, *others):
    return lax.optimization_barrier((value,) + others)[0]


def deal_kernel(plane_ref, *refs):
    out_ref = refs[-1]
    each = out_ref.shape[0]
    for k in range(each):
        w_ref, b_ref = refs[k], refs[each + k]
        w_rows = w_ref.shape[0]
        out_ref[k, :w_rows] = w_ref[...]
        out_ref[k, w_rows:] = b_ref[...]


def deal_out(part, plane, matrix, second, n):
    w_rows, r_rows = matrix.shape[0], second.shape[0]
    cols = matrix.shape[1] // (4 * n)
    each = 4

    def column(k, s, plane_ref):
        return (0, (part * n + s * each + k) * 2 + plane_ref[0])

    maps = [functools.partial(column, k) for k in range(each)]
    return pl.pallas_call(
        deal_kernel,
        out_shape=jax.ShapeDtypeStruct((n, w_rows + r_rows, cols), BF),
        grid_spec=pltpu.PrefetchScalarGridSpec(
            num_scalar_prefetch=1,
            grid=(n // each,),
            in_specs=[pl.BlockSpec((w_rows, cols), m) for m in maps]
            + [pl.BlockSpec((r_rows, cols), m) for m in maps],
            out_specs=pl.BlockSpec((each, w_rows + r_rows, cols), lambda s, p: (s, 0, 0)),
        ),
        cost_estimate=pl.CostEstimate(
            flops=0, transcendentals=0, bytes_accessed=4 * n * (w_rows + r_rows) * cols
        ),
    )(plane, *([matrix] * each), *([second] * each))


def fold_kernel(gate_ref, up_ref, b_gate_ref, b_up_ref, a_ref, *refs):
    out_ref = refs[-1]
    each, w_rows = gate_ref.shape[0], a_ref.shape[0] // gate_ref.shape[0]
    cols = b_gate_ref.shape[1]
    gate = mm(a_ref[...], b_gate_ref[...])
    up = mm(a_ref[...], b_up_ref[...])
    for k in range(each):
        part = slice(k * w_rows, (k + 1) * w_rows)
        out_ref[part, :cols] = (gate_ref[k, :w_rows].astype(F32) + gate[part]).astype(BF)
        out_ref[part, cols:] = (up_ref[k, :w_rows].astype(F32) + up[part]).astype(BF)


def fold(gate, up, first, place, given):
    n, ext, cols = gate.shape
    width, rank = first.shape
    w_rows = width // n
    each = max(1, min(4, 512 // w_rows))
    seconds = [x[:, w_rows:].reshape(rank, cols) for x in (gate, up)]
    piece = pl.BlockSpec((each, ext, cols), lambda s: (s, 0, 0))
    whole = pl.BlockSpec((rank, cols), lambda s: (0, 0))
    held = [] if given is None else [given]
    return pl.pallas_call(
        fold_kernel,
        out_shape=jax.ShapeDtypeStruct((width, 4 * cols), BF),
        grid=(n // each,),
        in_specs=[piece, piece, whole, whole]
        + [pl.BlockSpec((each * w_rows, rank), lambda s: (s, 0))]
        + [pl.BlockSpec(memory_space=pl.ANY)] * len(held),
        out_specs=pl.BlockSpec((each * w_rows, 2 * cols), lambda s: (s, place)),
        input_output_aliases={5: 0} if held else {},
        cost_estimate=pl.CostEstimate(
            flops=4 * width * rank * cols, transcendentals=0, bytes_accessed=8 * width * cols
        ),
    )(gate, up, *seconds, first, *held), seconds


def forward_kernel(x_ref, w_ref, hidden_ref, act_ref, slope_ref):
    h = hidden_ref.shape[1] // 2
    c = 0.7978845608028654
    for k in (0, 1):
        both = mm(x_ref[...], w_ref[:, 2 * k * h : 2 * (k + 1) * h])
        gate, up = both[:, :h], both[:, h:]
        square = gate * gate
        t = jnp.tanh(c * gate * (1.0 + 0.044715 * square))
        half_up = 0.5 * (1.0 + t)
        act = gate * half_up
        slope = half_up + 0.5 * gate * (1.0 - t * t) * (c * (1.0 + 3 * 0.044715 * square))
        part = slice(k * h, (k + 1) * h)
        hidden_ref[:, part] = (act * up).astype(BF)
        act_ref[:, part] = act.astype(BF)
        slope_ref[:, part] = (slope * up).astype(BF)


def forward(x, w):
    t, d = x.shape
    f = w.shape[1] // 2
    tile = 256
    out = pl.BlockSpec((tile, f), lambda i: (i, 0))
    return pl.pallas_call(
        forward_kernel,
        out_shape=(jax.ShapeDtypeStruct((t, f), BF),) * 3,
        grid=(t // tile,),
        in_specs=[
            pl.BlockSpec((tile, d), lambda i: (i, 0)),
            pl.BlockSpec((d, 2 * f), lambda i: (0, 0)),
        ],
        out_specs=(out,) * 3,
        compiler_params=pltpu.CompilerParams(vmem_limit_bytes=44 * 2**20),
        cost_estimate=pl.CostEstimate(
            flops=4 * t * d * f, transcendentals=t * f, bytes_accessed=2 * (t * d + 2 * d * f + 3 * t * f)
        ),
    )(x, w)


def backward_kernel(dy_ref, w_ref, act_ref, slope_ref, out_ref):
    h = act_ref.shape[1] // 2
    for k in (0, 1):
        part = slice(k * h, (k + 1) * h)
        grad = mm(dy_ref[...], w_ref[part, :], 1, 1)
        out_ref[:, 2 * k * h : (2 * k + 1) * h] = (grad * slope_ref[:, part].astype(F32)).astype(BF)
        out_ref[:, (2 * k + 1) * h : 2 * (k + 1) * h] = (
            grad * act_ref[:, part].astype(F32)
        ).astype(BF)


def backward(dy, w, act, slope):
    t, d = dy.shape
    f = w.shape[0]
    tile = 256
    given = pl.BlockSpec((tile, f), lambda i: (i, 0))
    return pl.pallas_call(
        backward_kernel,
        out_shape=jax.ShapeDtypeStruct((t, 2 * f), BF),
        grid=(t // tile,),
        in_specs=[
            pl.BlockSpec((tile, d), lambda i: (i, 0)),
            pl.BlockSpec((f, d), lambda i: (0, 0)),
            given,
            given,
        ],
        out_specs=pl.BlockSpec((tile, 2 * f), lambda i: (i, 0)),
        compiler_params=pltpu.CompilerParams(vmem_limit_bytes=44 * 2**20),
        cost_estimate=pl.CostEstimate(
            flops=2 * t * d * f, transcendentals=0, bytes_accessed=2 * (t * d + d * f + 4 * t * f)
        ),
    )(dy, w, act, slope)


def collect_kernel(plane_ref, mine, other, *refs):
    w_ref, b_ref = refs[-2:]
    w_rows = w_ref.shape[0]
    each, _, cols = mine.shape
    for plane in (0, 1):

        @pl.when(plane_ref[0] == plane)
        def _():
            for k in range(each):
                for ref, h in ((mine, plane), (other, 1 - plane)):
                    at = slice((2 * k + h) * cols, (2 * k + h + 1) * cols)
                    w_ref[:, at] = ref[k, :w_rows].astype(F32)
                    b_ref[:, at] = ref[k, w_rows:].astype(F32)


def collect(plane, mine, other, w_rows, part, given):
    n, ext, cols = mine.shape
    each = 4
    piece = pl.BlockSpec((each, ext, cols), lambda s, _: (s, 0, 0))
    held = [] if given is None else list(given)
    steps = n // each
    return pl.pallas_call(
        collect_kernel,
        out_shape=(
            jax.ShapeDtypeStruct((w_rows, 4 * n * cols), F32),
            jax.ShapeDtypeStruct((ext - w_rows, 4 * n * cols), F32),
        ),
        grid_spec=pltpu.PrefetchScalarGridSpec(
            num_scalar_prefetch=1,
            grid=(steps,),
            in_specs=[piece, piece] + [pl.BlockSpec(memory_space=pl.ANY)] * len(held),
            out_specs=(
                pl.BlockSpec((w_rows, 2 * cols * each), lambda s, _: (0, part * steps + s)),
                pl.BlockSpec((ext - w_rows, 2 * cols * each), lambda s, _: (0, part * steps + s)),
            ),
        ),
        input_output_aliases={3: 0, 4: 1} if held else {},
        cost_estimate=pl.CostEstimate(
            flops=0, transcendentals=0, bytes_accessed=12 * n * ext * cols
        ),
    )(plane, mine, other, *held)


def stack_kernel(plane_ref, mine, other, w_ref, a_ref):
    width = w_ref.shape[1]
    own = pl.program_id(0) == plane_ref[0]

    @pl.when(own)
    def _():
        w_ref[...] = mine[:, :width].astype(F32)
        a_ref[...] = mine[:, width:].astype(F32)

    @pl.when(jnp.logical_not(own))
    def _():
        w_ref[...] = other[:, :width].astype(F32)
        a_ref[...] = other[:, width:].astype(F32)


def stack(plane, mine, other, width):
    half, cols = mine.shape
    tile = min(half, 128)
    tiles = half // tile
    given = pl.BlockSpec((tile, cols), lambda h, t, _: (t, 0))
    return pl.pallas_call(
        stack_kernel,
        out_shape=(
            jax.ShapeDtypeStruct((2 * half, width), F32),
            jax.ShapeDtypeStruct((2 * half, cols - width), F32),
        ),
        grid_spec=pltpu.PrefetchScalarGridSpec(
            num_scalar_prefetch=1,
            grid=(2, tiles),
            in_specs=[given, given],
            out_specs=(
                pl.BlockSpec((tile, width), lambda h, t, _: (h * tiles + t, 0)),
                pl.BlockSpec((tile, cols - width), lambda h, t, _: (h * tiles + t, 0)),
            ),
        ),
        cost_estimate=pl.CostEstimate(
            flops=0, transcendentals=0, bytes_accessed=16 * half * cols
        ),
    )(plane, mine, other)


def body(
    tokens,
    segments,
    output_cotangent_rows,
    attention_norm_gain,
    query_key_value_matrix,
    query_key_value_adapter_first,
    query_key_value_adapter_second,
    output_matrix,
    output_adapter_first,
    output_adapter_second,
    feed_norm_gain,
    gate_up_matrix,
    gate_up_adapter_first,
    gate_up_adapter_second,
    down_matrix,
    down_adapter_first,
    down_adapter_second,
):
    n = lax.axis_size("ctx")
    me = lax.axis_index("ctx")
    plane = lax.axis_index("grp")
    lines = n // 4
    rows = tokens.shape[1]
    width = tokens.shape[2]
    seq = rows * n
    rank = query_key_value_adapter_first.shape[1]
    qkv_cols = query_key_value_matrix.shape[1]
    feed_dev = down_matrix.shape[0]
    feed_half = feed_dev // 2
    w_rows = width // n
    r_rows = rank // n
    score_scale = HD ** (-0.5)

    def hop(x, k):
        return lax.ppermute(x, "ctx", [(i, i ^ k) for i in range(n)])

    def swap(x):
        return lax.ppermute(x, "grp", [(0, 1), (1, 0)])

    def swap_pieces(x, count):
        each = x.shape[0] // count
        return [swap(x[k * each : (k + 1) * each]) for k in range(count)]

    rel = jnp.arange(n, dtype=jnp.int32)
    rel = me ^ (rel // (2 * lines) + 2 * (rel // lines % 2) + 4 * (rel % lines))

    def reorder(x):
        r = x.shape[0] // n
        order = [4 * k + 2 * j + i for i in (0, 1) for j in (0, 1) for k in range(lines)]
        return jnp.concatenate(
            [lax.dynamic_slice_in_dim(x, (me ^ k) * r, r) for k in order], axis=0
        )

    def lines_of(x):
        return [x] + [hop(x, 4 * k) for k in range(1, lines)]

    def gather(x):
        along = lines_of(x)
        near = jnp.concatenate(along + [hop(b, 2) for b in along], axis=0)
        return jnp.concatenate([near, hop(near, 1)], axis=0)

    chip, core = me // 2, me % 2

    def gather_chips(x):
        along = lines_of(x)
        blocks = [(2 * k, b) for k, b in enumerate(along)]
        blocks = blocks + [(k + 1, hop(b, 2)) for k, b in blocks]
        near = jnp.zeros((x.shape[0] * n // 2, x.shape[1]), x.dtype)
        for k, b in blocks:
            near = lax.dynamic_update_slice_in_dim(near, b, (chip ^ k) * x.shape[0], 0)
        return near

    def fold_core(near, arrived):
        r = near.shape[0] // (2 * lines)

        def block(k):
            at = (chip ^ k) * r
            a = lax.dynamic_slice_in_dim(near, at, r).astype(F32)
            return a + lax.dynamic_slice_in_dim(arrived, at, r).astype(F32)

        here = [block(2 * k) for k in range(lines)]
        return here, [block(2 * k + 1).astype(near.dtype) for k in range(lines)]

    def all_after(values, *others):
        return lax.optimization_barrier((*values, *others))[: len(values)]

    def scatter(near, far):
        kind = near.dtype
        mine = near.astype(F32) + hop(far, 1).astype(F32)
        half = near.shape[0] // 2
        mine = mine[:half] + hop(mine[half:].astype(kind), 2).astype(F32)
        r = half // lines
        total = mine[:r]
        for k in range(1, lines):
            total = total + hop(mine[k * r : (k + 1) * r].astype(kind), 4 * k).astype(F32)
        return total

    def scatter_whole(partial):
        half = partial.shape[0] // 2
        return scatter(partial[:half], partial[half:])

    x = tokens[0].astype(F32)
    dy = output_cotangent_rows[0]
    plane_id = plane.astype(jnp.int32).reshape(1)
    ext = w_rows + r_rows

    def beside(second):
        return second.reshape(w_rows, second.shape[1] * r_rows // w_rows)

    def apart(columns):
        return columns.reshape(rank, columns.shape[1] * w_rows // r_rows)

    q_second = qkv_cols * r_rows // w_rows
    o_second = width * r_rows // w_rows
    at_q = qkv_cols + rank
    pad = -(at_q + q_second) % 128
    gains = jnp.concatenate(
        [
            attention_norm_gain[:, None],
            feed_norm_gain[:, None],
            jnp.zeros((w_rows, pad - 2), BF),
        ],
        axis=1,
    )
    qkv_ext = jnp.concatenate(
        [
            query_key_value_matrix,
            query_key_value_adapter_first,
            beside(query_key_value_adapter_second),
            gains,
        ],
        axis=1,
    )
    qkv_got = lax.all_gather(qkv_ext, "ctx", axis=0, tiled=True)
    out_ext = jnp.concatenate(
        [
            output_matrix,
            output_adapter_first,
            gate_up_adapter_first,
            beside(output_adapter_second),
            beside(down_adapter_second),
        ],
        axis=1,
    )
    out_got = lax.all_gather(out_ext, "ctx", axis=0, tiled=True)
    qkv_full = qkv_got[:, :at_q]
    qkv_second = apart(qkv_got[:, at_q : at_q + q_second])
    gains_full = qkv_got[:, at_q + q_second : at_q + q_second + 2].astype(F32).T
    attn_gain, feed_gain = gains_full[:1], gains_full[1:]

    def exchange(pieces):
        flat = pieces.reshape(n * ext, feed_half)
        return lax.all_to_all(flat, "ctx", 0, 0, tiled=True).reshape(n, ext, feed_half)

    gate_mine = exchange(deal_out(0, plane_id, gate_up_matrix, gate_up_adapter_second, n))
    up_sent = deal_out(1, plane_id, gate_up_matrix, gate_up_adapter_second, n)

    def own_first(x):
        pair = x.reshape(2, feed_half, x.shape[1])
        a = lax.dynamic_index_in_dim(pair, plane, 0, False)
        b = lax.dynamic_index_in_dim(pair, 1 - plane, 0, False)
        return jnp.concatenate([a, b], axis=0)

    down_first, down_rows = own_first(down_adapter_first), own_first(down_matrix)

    def positions(device):
        within = jnp.arange(rows, dtype=jnp.int32)
        half = rows // 2
        block = jnp.where(within < half, device[:, None], 2 * n - 1 - device[:, None])
        return block * half + within % half

    local_pos = positions(me[None])[0]
    key_pos = positions(rel).reshape(seq)
    half = rows // 2
    local_seg = jnp.concatenate(
        [
            lax.dynamic_slice_in_dim(segments[0], me * half, half),
            lax.dynamic_slice_in_dim(segments[0], (2 * n - 1 - me) * half, half),
        ]
    )
    doc_start = jnp.sum(
        (segments[0][None, :] < local_seg[:, None]).astype(jnp.int32), axis=1
    )
    allowed = (key_pos[None, :] >= doc_start[:, None]) & (key_pos[None, :] <= local_pos[:, None])
    frequency = rope_base ** (-2.0 * jnp.arange(HD // 2, dtype=F32) / HD)
    angle_rows = local_pos.astype(F32)[:, None] * frequency[None, :]
    cosine, sine_rows = jnp.cos(angle_rows), jnp.sin(angle_rows)

    inv_one = inv_rms(x)
    norm_one = (x * inv_one * (1.0 + attn_gain)).astype(BF)
    norm_one = after(norm_one, gate_mine, up_sent)
    qkv_base = mm(norm_one, qkv_full)
    inner_qkv = qkv_base[:, qkv_cols:].astype(BF)
    qkv = qkv_base[:, :qkv_cols] + mm(inner_qkv, qkv_second)
    q = rotate(
        qkv[:, :width].reshape(rows, HEADS, HD), cosine[:, None, :], sine_rows[:, None, :]
    ).astype(BF)
    q_flat = q.reshape(rows * HEADS, HD)
    k_mine = rotate(qkv[:, width : width + HD], cosine, sine_rows).astype(BF)
    kv_mine = jnp.concatenate([k_mine, qkv[:, width + HD :].astype(BF)], axis=1)
    kv_all = gather(kv_mine)
    dy_got = lax.all_gather(after(dy, kv_mine), "ctx", axis=0, tiled=True)
    up_mine = exchange(after(up_sent, kv_all))
    gate_pieces = swap_pieces(gate_mine, 2)
    kv_all = after(kv_all, gate_pieces[0])
    k_all, v_all = kv_all[:, :HD], kv_all[:, HD:]
    raw = mm(q_flat, k_all, 1, 1).reshape(rows, HEADS, seq) * score_scale
    scores = jnp.where(allowed[:, None, :], raw, -jnp.inf)
    peak = jnp.max(scores, axis=-1, keepdims=True)
    unnormed = jnp.exp(scores - peak)
    total = jnp.sum(unnormed, axis=-1, keepdims=True)
    probs = (unnormed / total).astype(BF).reshape(rows * HEADS, seq)
    out_got = after(out_got, probs)
    out_full = out_got[:, : width + rank]
    gate_up_first = out_got[:, width + rank : width + 2 * rank]
    out_second = apart(out_got[:, width + 2 * rank : width + 2 * rank + o_second])
    down_second = apart(out_got[:, width + 2 * rank + o_second :])
    down_eff = (down_rows.astype(F32) + mm(down_first, down_second)).astype(BF)
    attended_f = mm(after(probs, gate_pieces[1]), v_all)
    gate_other = jnp.concatenate(gate_pieces, axis=0)
    attended = attended_f.reshape(rows, width).astype(BF)
    attended = after(attended, up_mine)
    up_pieces = swap_pieces(up_mine, 2)
    out_base = mm(attended, out_full)
    inner_out = out_base[:, width:].astype(BF)
    mid = x + out_base[:, :width] + mm(inner_out, out_second)

    inv_two = inv_rms(mid)
    norm_two = (mid * inv_two * (1.0 + feed_gain)).astype(BF)
    near_rows = gather_chips(norm_two)
    dy_pair = dy_got.reshape(n // 2, 2, rows, width)
    all_dy = jnp.concatenate(
        [
            lax.dynamic_index_in_dim(dy_pair, c, 1, False).reshape(n // 2 * rows, width)
            for c in (core, 1 - core)
        ],
        axis=0,
    )
    up_other = jnp.concatenate(up_pieces, axis=0)
    w_eff, (gate_b, up_b) = fold(gate_mine, up_mine, gate_up_first, 0, None)
    w_eff, _ = fold(gate_other, up_other, gate_up_first, 1, w_eff)
    near_rows = after(near_rows, w_eff, down_eff)
    all_rows = jnp.concatenate([near_rows, hop(near_rows, 1)], axis=0)
    hidden, act, slope = forward(after(all_rows, all_dy), w_eff)
    h = feed_half
    half_seq = seq // 2
    down_part = mm(hidden[:, h:], all_dy, 0, 0).astype(BF)
    grads = backward(after(all_dy, down_part), down_eff, act, slope)
    down_part = swap(down_part)
    far_part = mm(grads[half_seq:], w_eff, 1, 1).astype(BF)
    near_part = mm(after(grads, far_part)[:half_seq], w_eff, 1, 1).astype(BF)
    here, there = fold_core(near_part, hop(far_part, 1))
    sides = [hop(part, 2) for part in there]

    late_rows, late_grads = lax.optimization_barrier(
        (all_rows, grads, near_part, *there)
    )[:2]
    other_part = mm(late_rows, late_grads[:, 2 * h :], 0, 0).astype(BF)
    gate_part, up_part = swap(other_part[:, :h]), swap(other_part[:, h:])
    sides = all_after(sides, other_part)
    sums = [a + b.astype(F32) for a, b in zip(here, sides)]
    line_sums = [part.astype(BF) for part in sums[1:]]
    arrivals = [hop(part, 4 * (k + 1)) for k, part in enumerate(line_sums)]
    late_hidden = after(hidden, other_part)
    out_far = mm(late_hidden[half_seq:], down_eff).astype(BF)
    out_near = mm(late_hidden[:half_seq], down_eff).astype(BF)
    down_half = (
        mm(after(hidden, other_part)[:, :h], all_dy, 0, 0) + down_part.astype(F32)
    ).astype(BF)
    g_down_first = mm(down_half, down_second, 1, 1).astype(BF)
    down_rows = jnp.concatenate([down_half, g_down_first], axis=1)

    late_rows = after(all_rows, down_rows, out_near, out_far, *line_sums)
    gate_half = (mm(late_rows, grads[:, :h], 0, 0) + gate_part.astype(F32)).astype(BF)

    pieces = jnp.concatenate(
        [
            norm_one.reshape(rows, n, w_rows),
            inner_qkv.reshape(rows, n, r_rows),
            attended.reshape(rows, n, w_rows),
            inner_out.reshape(rows, n, r_rows),
        ],
        axis=2,
    ).transpose(1, 0, 2)
    pieces = after(pieces, all_rows)
    inputs = lax.all_to_all(pieces.reshape(seq, 2 * ext), "ctx", 0, 0, tiled=True)

    arrivals = all_after(arrivals, gate_half, inputs)
    grad_norm_two = sums[0] + sum(part.astype(F32) for part in arrivals)
    feed_gain_rows = jnp.sum(grad_norm_two * mid * inv_two, axis=0, keepdims=True)
    grad_mid = dy.astype(F32) + norm_back(mid, inv_two, feed_gain, grad_norm_two)
    grad_branch = grad_mid.astype(BF)
    grad_inner_out = mm(grad_branch, out_second, 1, 1).astype(BF)
    grad_attended = mm(
        jnp.concatenate([grad_branch, grad_inner_out], axis=1), out_full, 1, 1
    )
    delta = jnp.sum(
        (grad_attended * attended.astype(F32)).reshape(rows * HEADS, HD), axis=1, keepdims=True
    )
    grad_flat = grad_attended.astype(BF).reshape(rows * HEADS, HD)
    gate_second = mm(gate_up_first, gate_half, 0, 0).astype(BF)
    gate_ext = jnp.concatenate(
        [gate_half.reshape(n, w_rows, h), gate_second.reshape(n, r_rows, h)], axis=1
    )
    gate_got = exchange(gate_ext)
    grad_flat = after(grad_flat, gate_ext)
    grad_probs = mm(grad_flat, v_all, 1, 1)
    grad_scores = (probs.astype(F32) * (grad_probs - delta)).astype(BF)
    grad_scores = after(grad_scores, up_part)
    grad_k = mm(grad_scores, q_flat, 0, 0) * score_scale
    grad_v = mm(probs, grad_flat, 0, 0)
    kv_part = jnp.concatenate([grad_k, grad_v], axis=1).astype(BF)
    grad_kv = scatter_whole(kv_part)
    grad_q = mm(after(grad_scores, kv_part), k_all) * score_scale
    grad_q_rows = (
        rotate(grad_q.reshape(rows, HEADS, HD), cosine[:, None, :], -sine_rows[:, None, :])
        .reshape(rows, width)
        .astype(BF)
    )
    q_all = lax.all_gather(grad_q_rows, "ctx", axis=0, tiled=True)
    up_half = (
        mm(after(all_rows, grad_q_rows, gate_got), grads[:, h : 2 * h], 0, 0)
        + up_part.astype(F32)
    ).astype(BF)
    down_back = swap(after(down_rows, up_part))
    out_here, out_there = fold_core(out_near, hop(after(out_far, grad_kv), 1))
    out_side = hop(jnp.concatenate(out_there, axis=0), 2)
    branch_all = lax.all_gather(after(grad_branch, grad_kv), "ctx", axis=0, tiled=True)
    grad_kv = after(grad_kv, up_half, down_back)
    grad_k_rows = rotate(grad_kv[:, :HD], cosine, -sine_rows)
    grad_kv_rows = jnp.concatenate([grad_k_rows, grad_kv[:, HD:]], axis=1).astype(BF)
    kv_all_grads = gather(grad_kv_rows)
    up_second = mm(gate_up_first, after(up_half, grad_kv_rows), 0, 0).astype(BF)
    up_ext = jnp.concatenate(
        [up_half.reshape(n, w_rows, h), up_second.reshape(n, r_rows, h)], axis=1
    )
    up_ext = after(up_ext, gate_got)
    up_got = exchange(up_ext)
    grad_qkv = jnp.concatenate([grad_q_rows, grad_kv_rows], axis=1)
    grad_qkv = after(grad_qkv, up_ext)
    grad_inner_qkv = mm(grad_qkv, qkv_second, 1, 1).astype(BF)
    grad_norm_one = mm(
        after(jnp.concatenate([grad_qkv, grad_inner_qkv], axis=1), out_side), qkv_full, 1, 1
    )
    attn_gain_rows = jnp.sum(grad_norm_one * x * inv_one, axis=0, keepdims=True)
    grad_input = (grad_mid + norm_back(x, inv_one, attn_gain, grad_norm_one)).astype(BF)
    gate_back = swap(after(gate_got, down_back))
    output = mid + out_here[0] + out_side[:rows].astype(F32)
    for k in range(1, lines):
        part = out_here[k] + out_side[k * rows : (k + 1) * rows].astype(F32)
        output = output + hop(part.astype(BF), 4 * k).astype(F32)
    output = output.astype(BF)

    def both_planes(own):
        own = own.astype(BF)
        return own.astype(F32) + swap(own).astype(F32)


    small = jnp.concatenate(
        [
            (mm(gate_half, gate_b, 1, 1) + mm(up_half, up_b, 1, 1))
            .astype(BF)
            .reshape(n, w_rows, rank),
            mm(down_first[:h], after(down_half, grad_input), 0, 0)
            .astype(BF)
            .reshape(n, w_rows, width * r_rows // w_rows),
        ],
        axis=2,
    )
    small = scatter_whole(reorder(small.reshape(n * w_rows, small.shape[2])))
    gain_rows = jnp.concatenate([attn_gain_rows, feed_gain_rows], axis=0)
    gain_rows = gain_rows.reshape(2, n, w_rows).transpose(1, 0, 2).reshape(2 * n, w_rows)
    gain_rows = scatter_whole(reorder(gain_rows))

    down_grads = stack(plane_id, down_rows, after(down_back, grad_input), width)
    gate_up_grads = collect(
        plane_id, gate_got, after(gate_back, grad_input), w_rows, 0, None
    )
    up_got_other = swap(after(up_got, gate_back))
    gate_up_grads = collect(plane_id, up_got, up_got_other, w_rows, 1, gate_up_grads)

    g_q = mm(inputs[:, :ext], after(q_all, down_grads[0]), 0, 0)
    g_out = mm(inputs[:, ext:], after(branch_all, g_q), 0, 0).astype(BF)
    inputs_rel = reorder(inputs[:, :ext])
    g_kv = mm(inputs_rel, kv_all_grads, 0, 0)
    g_qkv = jnp.concatenate([g_q, g_kv], axis=1).astype(BF)
    g_out = g_out.astype(F32) + after(swap(g_out), gate_up_grads[0]).astype(F32)
    small = both_planes(after(small, gate_back))
    g_qkv = both_planes(g_qkv)
    gain_rows = gain_rows + swap(after(gain_rows, up_got_other))
    g_gu_first = small[:, :rank]
    g_down_second = small[:, rank:].reshape(r_rows, width)
    g_out_first = mm(g_out[:w_rows].astype(BF), out_second, 1, 1)
    g_qkv_first = mm(g_qkv[:w_rows].astype(BF), qkv_second, 1, 1)

    return (
        output[None],
        grad_input[None],
        gain_rows[0],
        g_qkv[:w_rows],
        g_qkv_first,
        g_qkv[w_rows:],
        g_out[:w_rows],
        g_out_first,
        g_out[w_rows:],
        gain_rows[1],
        gate_up_grads[0],
        g_gu_first,
        gate_up_grads[1],
        down_grads[0],
        down_grads[1],
        g_down_second,
    )


def solution(mesh):
    rows = P("grp", "ctx", None)
    vector, matrix = P("ctx"), P("ctx", None)
    return jax.shard_map(
        body,
        mesh=mesh,
        in_specs=(rows, P("grp", None), rows, vector)
        + (matrix,) * 6
        + (vector,)
        + (matrix,) * 6,
        out_specs=(rows, rows, vector) + (matrix,) * 6 + (vector,) + (matrix,) * 6,
        check_vma=False,
    )
```

```python
import functools

import jax
import jax.numpy as jnp
from jax import lax
from jax.experimental import pallas as pl
from jax.experimental.pallas import tpu as pltpu
from jax.sharding import PartitionSpec as P

HEADS = 8
HD = 256
norm_eps = 1e-06
rope_base = 10000.0
BF = jnp.bfloat16
F32 = jnp.float32


def mm(a, b, ca=1, cb=0):
    return lax.dot_general(a, b, (((ca,), (cb,)), ((), ())), preferred_element_type=F32)


def rotate(vectors, cosine, sine_rows):
    front, back = jnp.split(vectors, 2, axis=-1)
    return jnp.concatenate(
        [front * cosine - back * sine_rows, back * cosine + front * sine_rows], axis=-1
    )


def inv_rms(values):
    return lax.rsqrt(jnp.mean(values * values, axis=-1, keepdims=True) + norm_eps)


def norm_back(values, inv, gain, grad):
    weighted = grad * (1.0 + gain)
    inner = jnp.mean(weighted * values, axis=-1, keepdims=True)
    return inv * weighted - values * (inv * inv * inv) * inner


def after(value, *others):
    return lax.optimization_barrier((value,) + others)[0]


def deal_kernel(plane_ref, *refs):
    out_ref = refs[-1]
    each = out_ref.shape[0]
    for k in range(each):
        w_ref, b_ref = refs[k], refs[each + k]
        w_rows = w_ref.shape[0]
        out_ref[k, :w_rows] = w_ref[...]
        out_ref[k, w_rows:] = b_ref[...]


def deal_out(part, plane, matrix, second, n):
    w_rows, r_rows = matrix.shape[0], second.shape[0]
    cols = matrix.shape[1] // (4 * n)
    each = 4

    def column(k, s, plane_ref):
        return (0, (part * n + s * each + k) * 2 + plane_ref[0])

    maps = [functools.partial(column, k) for k in range(each)]
    return pl.pallas_call(
        deal_kernel,
        out_shape=jax.ShapeDtypeStruct((n, w_rows + r_rows, cols), BF),
        grid_spec=pltpu.PrefetchScalarGridSpec(
            num_scalar_prefetch=1,
            grid=(n // each,),
            in_specs=[pl.BlockSpec((w_rows, cols), m) for m in maps]
            + [pl.BlockSpec((r_rows, cols), m) for m in maps],
            out_specs=pl.BlockSpec((each, w_rows + r_rows, cols), lambda s, p: (s, 0, 0)),
        ),
        cost_estimate=pl.CostEstimate(
            flops=0, transcendentals=0, bytes_accessed=4 * n * (w_rows + r_rows) * cols
        ),
    )(plane, *([matrix] * each), *([second] * each))


def fold_kernel(gate_ref, up_ref, b_gate_ref, b_up_ref, a_ref, *refs):
    out_ref = refs[-1]
    each, w_rows = gate_ref.shape[0], a_ref.shape[0] // gate_ref.shape[0]
    cols = b_gate_ref.shape[1]
    gate = mm(a_ref[...], b_gate_ref[...])
    up = mm(a_ref[...], b_up_ref[...])
    for k in range(each):
        part = slice(k * w_rows, (k + 1) * w_rows)
        out_ref[part, :cols] = (gate_ref[k, :w_rows].astype(F32) + gate[part]).astype(BF)
        out_ref[part, cols:] = (up_ref[k, :w_rows].astype(F32) + up[part]).astype(BF)


def fold(gate, up, first, place, given):
    n, ext, cols = gate.shape
    width, rank = first.shape
    w_rows = width // n
    each = max(1, min(4, 512 // w_rows))
    seconds = [x[:, w_rows:].reshape(rank, cols) for x in (gate, up)]
    piece = pl.BlockSpec((each, ext, cols), lambda s: (s, 0, 0))
    whole = pl.BlockSpec((rank, cols), lambda s: (0, 0))
    held = [] if given is None else [given]
    return pl.pallas_call(
        fold_kernel,
        out_shape=jax.ShapeDtypeStruct((width, 4 * cols), BF),
        grid=(n // each,),
        in_specs=[piece, piece, whole, whole]
        + [pl.BlockSpec((each * w_rows, rank), lambda s: (s, 0))]
        + [pl.BlockSpec(memory_space=pl.ANY)] * len(held),
        out_specs=pl.BlockSpec((each * w_rows, 2 * cols), lambda s: (s, place)),
        input_output_aliases={5: 0} if held else {},
        cost_estimate=pl.CostEstimate(
            flops=4 * width * rank * cols, transcendentals=0, bytes_accessed=8 * width * cols
        ),
    )(gate, up, *seconds, first, *held), seconds


def forward_kernel(x_ref, w_ref, hidden_ref, act_ref, slope_ref):
    h = hidden_ref.shape[1] // 2
    c = 0.7978845608028654
    for k in (0, 1):
        both = mm(x_ref[...], w_ref[:, 2 * k * h : 2 * (k + 1) * h])
        gate, up = both[:, :h], both[:, h:]
        square = gate * gate
        t = jnp.tanh(c * gate * (1.0 + 0.044715 * square))
        half_up = 0.5 * (1.0 + t)
        act = gate * half_up
        slope = half_up + 0.5 * gate * (1.0 - t * t) * (c * (1.0 + 3 * 0.044715 * square))
        part = slice(k * h, (k + 1) * h)
        hidden_ref[:, part] = (act * up).astype(BF)
        act_ref[:, part] = act.astype(BF)
        slope_ref[:, part] = (slope * up).astype(BF)


def forward(x, w):
    t, d = x.shape
    f = w.shape[1] // 2
    tile = 256
    out = pl.BlockSpec((tile, f), lambda i: (i, 0))
    return pl.pallas_call(
        forward_kernel,
        out_shape=(jax.ShapeDtypeStruct((t, f), BF),) * 3,
        grid=(t // tile,),
        in_specs=[
            pl.BlockSpec((tile, d), lambda i: (i, 0)),
            pl.BlockSpec((d, 2 * f), lambda i: (0, 0)),
        ],
        out_specs=(out,) * 3,
        compiler_params=pltpu.CompilerParams(vmem_limit_bytes=44 * 2**20),
        cost_estimate=pl.CostEstimate(
            flops=4 * t * d * f, transcendentals=t * f, bytes_accessed=2 * (t * d + 2 * d * f + 3 * t * f)
        ),
    )(x, w)


def backward_kernel(dy_ref, w_ref, act_ref, slope_ref, out_ref):
    h = act_ref.shape[1] // 2
    for k in (0, 1):
        part = slice(k * h, (k + 1) * h)
        grad = mm(dy_ref[...], w_ref[part, :], 1, 1)
        out_ref[:, 2 * k * h : (2 * k + 1) * h] = (grad * slope_ref[:, part].astype(F32)).astype(BF)
        out_ref[:, (2 * k + 1) * h : 2 * (k + 1) * h] = (
            grad * act_ref[:, part].astype(F32)
        ).astype(BF)


def backward(dy, w, act, slope):
    t, d = dy.shape
    f = w.shape[0]
    tile = 256
    given = pl.BlockSpec((tile, f), lambda i: (i, 0))
    return pl.pallas_call(
        backward_kernel,
        out_shape=jax.ShapeDtypeStruct((t, 2 * f), BF),
        grid=(t // tile,),
        in_specs=[
            pl.BlockSpec((tile, d), lambda i: (i, 0)),
            pl.BlockSpec((f, d), lambda i: (0, 0)),
            given,
            given,
        ],
        out_specs=pl.BlockSpec((tile, 2 * f), lambda i: (i, 0)),
        compiler_params=pltpu.CompilerParams(vmem_limit_bytes=44 * 2**20),
        cost_estimate=pl.CostEstimate(
            flops=2 * t * d * f, transcendentals=0, bytes_accessed=2 * (t * d + d * f + 4 * t * f)
        ),
    )(dy, w, act, slope)


def collect_kernel(plane_ref, mine, other, *refs):
    w_ref, b_ref = refs[-2:]
    w_rows = w_ref.shape[0]
    each, _, cols = mine.shape
    for plane in (0, 1):

        @pl.when(plane_ref[0] == plane)
        def _():
            for k in range(each):
                for ref, h in ((mine, plane), (other, 1 - plane)):
                    at = slice((2 * k + h) * cols, (2 * k + h + 1) * cols)
                    w_ref[:, at] = ref[k, :w_rows].astype(F32)
                    b_ref[:, at] = ref[k, w_rows:].astype(F32)


def collect(plane, mine, other, w_rows, part, given):
    n, ext, cols = mine.shape
    each = 4
    piece = pl.BlockSpec((each, ext, cols), lambda s, _: (s, 0, 0))
    held = [] if given is None else list(given)
    steps = n // each
    return pl.pallas_call(
        collect_kernel,
        out_shape=(
            jax.ShapeDtypeStruct((w_rows, 4 * n * cols), F32),
            jax.ShapeDtypeStruct((ext - w_rows, 4 * n * cols), F32),
        ),
        grid_spec=pltpu.PrefetchScalarGridSpec(
            num_scalar_prefetch=1,
            grid=(steps,),
            in_specs=[piece, piece] + [pl.BlockSpec(memory_space=pl.ANY)] * len(held),
            out_specs=(
                pl.BlockSpec((w_rows, 2 * cols * each), lambda s, _: (0, part * steps + s)),
                pl.BlockSpec((ext - w_rows, 2 * cols * each), lambda s, _: (0, part * steps + s)),
            ),
        ),
        input_output_aliases={3: 0, 4: 1} if held else {},
        cost_estimate=pl.CostEstimate(
            flops=0, transcendentals=0, bytes_accessed=12 * n * ext * cols
        ),
    )(plane, mine, other, *held)


def stack_kernel(plane_ref, mine, other, w_ref, a_ref):
    width = w_ref.shape[1]
    own = pl.program_id(0) == plane_ref[0]

    @pl.when(own)
    def _():
        w_ref[...] = mine[:, :width].astype(F32)
        a_ref[...] = mine[:, width:].astype(F32)

    @pl.when(jnp.logical_not(own))
    def _():
        w_ref[...] = other[:, :width].astype(F32)
        a_ref[...] = other[:, width:].astype(F32)


def stack(plane, mine, other, width):
    half, cols = mine.shape
    tile = min(half, 128)
    tiles = half // tile
    given = pl.BlockSpec((tile, cols), lambda h, t, _: (t, 0))
    return pl.pallas_call(
        stack_kernel,
        out_shape=(
            jax.ShapeDtypeStruct((2 * half, width), F32),
            jax.ShapeDtypeStruct((2 * half, cols - width), F32),
        ),
        grid_spec=pltpu.PrefetchScalarGridSpec(
            num_scalar_prefetch=1,
            grid=(2, tiles),
            in_specs=[given, given],
            out_specs=(
                pl.BlockSpec((tile, width), lambda h, t, _: (h * tiles + t, 0)),
                pl.BlockSpec((tile, cols - width), lambda h, t, _: (h * tiles + t, 0)),
            ),
        ),
        cost_estimate=pl.CostEstimate(
            flops=0, transcendentals=0, bytes_accessed=16 * half * cols
        ),
    )(plane, mine, other)


def body(
    tokens,
    segments,
    output_cotangent_rows,
    attention_norm_gain,
    query_key_value_matrix,
    query_key_value_adapter_first,
    query_key_value_adapter_second,
    output_matrix,
    output_adapter_first,
    output_adapter_second,
    feed_norm_gain,
    gate_up_matrix,
    gate_up_adapter_first,
    gate_up_adapter_second,
    down_matrix,
    down_adapter_first,
    down_adapter_second,
):
    n = lax.axis_size("ctx")
    me = lax.axis_index("ctx")
    plane = lax.axis_index("grp")
    lines = n // 4
    rows = tokens.shape[1]
    width = tokens.shape[2]
    seq = rows * n
    rank = query_key_value_adapter_first.shape[1]
    qkv_cols = query_key_value_matrix.shape[1]
    feed_dev = down_matrix.shape[0]
    feed_half = feed_dev // 2
    w_rows = width // n
    r_rows = rank // n
    score_scale = HD ** (-0.5)

    def hop(x, k):
        return lax.ppermute(x, "ctx", [(i, i ^ k) for i in range(n)])

    def swap(x):
        return lax.ppermute(x, "grp", [(0, 1), (1, 0)])

    def swap_pieces(x, count):
        each = x.shape[0] // count
        return [swap(x[k * each : (k + 1) * each]) for k in range(count)]

    rel = jnp.arange(n, dtype=jnp.int32)
    rel = me ^ (rel // (2 * lines) + 2 * (rel // lines % 2) + 4 * (rel % lines))

    def reorder(x):
        r = x.shape[0] // n
        order = [4 * k + 2 * j + i for i in (0, 1) for j in (0, 1) for k in range(lines)]
        return jnp.concatenate(
            [lax.dynamic_slice_in_dim(x, (me ^ k) * r, r) for k in order], axis=0
        )

    def lines_of(x):
        return [x] + [hop(x, 4 * k) for k in range(1, lines)]

    def gather(x):
        along = lines_of(x)
        near = jnp.concatenate(along + [hop(b, 2) for b in along], axis=0)
        return jnp.concatenate([near, hop(near, 1)], axis=0)

    chip, core = me // 2, me % 2

    def gather_chips(x):
        along = lines_of(x)
        blocks = [(2 * k, b) for k, b in enumerate(along)]
        blocks = blocks + [(k + 1, hop(b, 2)) for k, b in blocks]
        near = jnp.zeros((x.shape[0] * n // 2, x.shape[1]), x.dtype)
        for k, b in blocks:
            near = lax.dynamic_update_slice_in_dim(near, b, (chip ^ k) * x.shape[0], 0)
        return near

    def fold_core(near, arrived):
        r = near.shape[0] // (2 * lines)

        def block(k):
            at = (chip ^ k) * r
            a = lax.dynamic_slice_in_dim(near, at, r).astype(F32)
            return a + lax.dynamic_slice_in_dim(arrived, at, r).astype(F32)

        here = [block(2 * k) for k in range(lines)]
        return here, [block(2 * k + 1).astype(near.dtype) for k in range(lines)]

    def all_after(values, *others):
        return lax.optimization_barrier((*values, *others))[: len(values)]

    def scatter(near, far):
        kind = near.dtype
        mine = near.astype(F32) + hop(far, 1).astype(F32)
        half = near.shape[0] // 2
        mine = mine[:half] + hop(mine[half:].astype(kind), 2).astype(F32)
        r = half // lines
        total = mine[:r]
        for k in range(1, lines):
            total = total + hop(mine[k * r : (k + 1) * r].astype(kind), 4 * k).astype(F32)
        return total

    def scatter_whole(partial):
        half = partial.shape[0] // 2
        return scatter(partial[:half], partial[half:])

    x = tokens[0].astype(F32)
    dy = output_cotangent_rows[0]
    plane_id = plane.astype(jnp.int32).reshape(1)
    ext = w_rows + r_rows

    def beside(second):
        return second.reshape(w_rows, second.shape[1] * r_rows // w_rows)

    def apart(columns):
        return columns.reshape(rank, columns.shape[1] * w_rows // r_rows)

    q_second = qkv_cols * r_rows // w_rows
    o_second = width * r_rows // w_rows
    at_q = qkv_cols + rank
    pad = -(at_q + q_second) % 128
    gains = jnp.concatenate(
        [
            attention_norm_gain[:, None],
            feed_norm_gain[:, None],
            jnp.zeros((w_rows, pad - 2), BF),
        ],
        axis=1,
    )
    qkv_ext = jnp.concatenate(
        [
            query_key_value_matrix,
            query_key_value_adapter_first,
            beside(query_key_value_adapter_second),
            gains,
        ],
        axis=1,
    )
    qkv_got = lax.all_gather(qkv_ext, "ctx", axis=0, tiled=True)
    out_ext = jnp.concatenate(
        [
            output_matrix,
            output_adapter_first,
            gate_up_adapter_first,
            beside(output_adapter_second),
            beside(down_adapter_second),
        ],
        axis=1,
    )
    out_got = lax.all_gather(out_ext, "ctx", axis=0, tiled=True)
    qkv_full = qkv_got[:, :at_q]
    qkv_second = apart(qkv_got[:, at_q : at_q + q_second])
    gains_full = qkv_got[:, at_q + q_second : at_q + q_second + 2].astype(F32).T
    attn_gain, feed_gain = gains_full[:1], gains_full[1:]

    def exchange(pieces):
        flat = pieces.reshape(n * ext, feed_half)
        return lax.all_to_all(flat, "ctx", 0, 0, tiled=True).reshape(n, ext, feed_half)

    gate_mine = exchange(deal_out(0, plane_id, gate_up_matrix, gate_up_adapter_second, n))
    up_sent = deal_out(1, plane_id, gate_up_matrix, gate_up_adapter_second, n)

    def own_first(x):
        pair = x.reshape(2, feed_half, x.shape[1])
        a = lax.dynamic_index_in_dim(pair, plane, 0, False)
        b = lax.dynamic_index_in_dim(pair, 1 - plane, 0, False)
        return jnp.concatenate([a, b], axis=0)

    down_first, down_rows = own_first(down_adapter_first), own_first(down_matrix)

    def positions(device):
        within = jnp.arange(rows, dtype=jnp.int32)
        half = rows // 2
        block = jnp.where(within < half, device[:, None], 2 * n - 1 - device[:, None])
        return block * half + within % half

    local_pos = positions(me[None])[0]
    key_pos = positions(rel).reshape(seq)
    half = rows // 2
    local_seg = jnp.concatenate(
        [
            lax.dynamic_slice_in_dim(segments[0], me * half, half),
            lax.dynamic_slice_in_dim(segments[0], (2 * n - 1 - me) * half, half),
        ]
    )
    doc_start = jnp.sum(
        (segments[0][None, :] < local_seg[:, None]).astype(jnp.int32), axis=1
    )
    allowed = (key_pos[None, :] >= doc_start[:, None]) & (key_pos[None, :] <= local_pos[:, None])
    frequency = rope_base ** (-2.0 * jnp.arange(HD // 2, dtype=F32) / HD)
    angle_rows = local_pos.astype(F32)[:, None] * frequency[None, :]
    cosine, sine_rows = jnp.cos(angle_rows), jnp.sin(angle_rows)

    inv_one = inv_rms(x)
    norm_one = (x * inv_one * (1.0 + attn_gain)).astype(BF)
    norm_one = after(norm_one, gate_mine, up_sent)
    qkv_base = mm(norm_one, qkv_full)
    inner_qkv = qkv_base[:, qkv_cols:].astype(BF)
    qkv = qkv_base[:, :qkv_cols] + mm(inner_qkv, qkv_second)
    q = rotate(
        qkv[:, :width].reshape(rows, HEADS, HD), cosine[:, None, :], sine_rows[:, None, :]
    ).astype(BF)
    q_flat = q.reshape(rows * HEADS, HD)
    k_mine = rotate(qkv[:, width : width + HD], cosine, sine_rows).astype(BF)
    kv_mine = jnp.concatenate([k_mine, qkv[:, width + HD :].astype(BF)], axis=1)
    kv_all = gather(kv_mine)
    dy_got = lax.all_gather(after(dy, kv_mine), "ctx", axis=0, tiled=True)
    up_mine = exchange(after(up_sent, kv_all))
    gate_pieces = swap_pieces(gate_mine, 2)
    kv_all = after(kv_all, gate_pieces[0])
    k_all, v_all = kv_all[:, :HD], kv_all[:, HD:]
    raw = mm(q_flat, k_all, 1, 1).reshape(rows, HEADS, seq) * score_scale
    scores = jnp.where(allowed[:, None, :], raw, -jnp.inf)
    peak = jnp.max(scores, axis=-1, keepdims=True)
    unnormed = jnp.exp(scores - peak)
    total = jnp.sum(unnormed, axis=-1, keepdims=True)
    probs = (unnormed / total).astype(BF).reshape(rows * HEADS, seq)
    out_got = after(out_got, probs)
    out_full = out_got[:, : width + rank]
    gate_up_first = out_got[:, width + rank : width + 2 * rank]
    out_second = apart(out_got[:, width + 2 * rank : width + 2 * rank + o_second])
    down_second = apart(out_got[:, width + 2 * rank + o_second :])
    down_eff = (down_rows.astype(F32) + mm(down_first, down_second)).astype(BF)
    attended_f = mm(after(probs, gate_pieces[1]), v_all)
    gate_other = jnp.concatenate(gate_pieces, axis=0)
    attended = attended_f.reshape(rows, width).astype(BF)
    attended = after(attended, up_mine)
    up_pieces = swap_pieces(up_mine, 2)
    out_base = mm(attended, out_full)
    inner_out = out_base[:, width:].astype(BF)
    mid = x + out_base[:, :width] + mm(inner_out, out_second)

    inv_two = inv_rms(mid)
    norm_two = (mid * inv_two * (1.0 + feed_gain)).astype(BF)
    near_rows = gather_chips(norm_two)
    dy_pair = dy_got.reshape(n // 2, 2, rows, width)
    all_dy = jnp.concatenate(
        [
            lax.dynamic_index_in_dim(dy_pair, c, 1, False).reshape(n // 2 * rows, width)
            for c in (core, 1 - core)
        ],
        axis=0,
    )
    up_other = jnp.concatenate(up_pieces, axis=0)
    w_eff, (gate_b, up_b) = fold(gate_mine, up_mine, gate_up_first, 0, None)
    w_eff, _ = fold(gate_other, up_other, gate_up_first, 1, w_eff)
    near_rows = after(near_rows, w_eff, down_eff)
    all_rows = jnp.concatenate([near_rows, hop(near_rows, 1)], axis=0)
    hidden, act, slope = forward(after(all_rows, all_dy), w_eff)
    h = feed_half
    half_seq = seq // 2
    down_part = mm(hidden[:, h:], all_dy, 0, 0).astype(BF)
    grads = backward(after(all_dy, down_part), down_eff, act, slope)
    down_part = swap(down_part)
    far_part = mm(grads[half_seq:], w_eff, 1, 1).astype(BF)
    near_part = mm(after(grads, far_part)[:half_seq], w_eff, 1, 1).astype(BF)
    here, there = fold_core(near_part, hop(far_part, 1))
    sides = [hop(part, 2) for part in there]

    late_rows, late_grads = lax.optimization_barrier(
        (all_rows, grads, near_part, *there)
    )[:2]
    other_part = mm(late_rows, late_grads[:, 2 * h :], 0, 0).astype(BF)
    gate_part, up_part = swap(other_part[:, :h]), swap(other_part[:, h:])
    sides = all_after(sides, other_part)
    sums = [a + b.astype(F32) for a, b in zip(here, sides)]
    line_sums = [part.astype(BF) for part in sums[1:]]
    arrivals = [hop(part, 4 * (k + 1)) for k, part in enumerate(line_sums)]
    late_hidden = after(hidden, other_part)
    out_far = mm(late_hidden[half_seq:], down_eff).astype(BF)
    out_near = mm(late_hidden[:half_seq], down_eff).astype(BF)
    down_half = (
        mm(after(hidden, other_part)[:, :h], all_dy, 0, 0) + down_part.astype(F32)
    ).astype(BF)
    g_down_first = mm(down_half, down_second, 1, 1).astype(BF)
    down_rows = jnp.concatenate([down_half, g_down_first], axis=1)

    out_here, out_there = fold_core(out_near, hop(out_far, 1))
    out_there = all_after(out_there, *line_sums)
    out_side = [hop(part, 2) for part in out_there]
    late_rows = after(all_rows, down_rows, *line_sums, *out_there)
    gate_half = (mm(late_rows, grads[:, :h], 0, 0) + gate_part.astype(F32)).astype(BF)
    late_rows = after(all_rows, gate_half)
    up_half = (mm(late_rows, grads[:, h : 2 * h], 0, 0) + up_part.astype(F32)).astype(BF)

    pieces = jnp.concatenate(
        [
            norm_one.reshape(rows, n, w_rows),
            inner_qkv.reshape(rows, n, r_rows),
            attended.reshape(rows, n, w_rows),
            inner_out.reshape(rows, n, r_rows),
        ],
        axis=2,
    ).transpose(1, 0, 2)
    pieces = after(pieces, all_rows)
    inputs = lax.all_to_all(pieces.reshape(seq, 2 * ext), "ctx", 0, 0, tiled=True)

    arrivals = all_after(arrivals, up_half, inputs)
    grad_norm_two = sums[0] + sum(part.astype(F32) for part in arrivals)
    feed_gain_rows = jnp.sum(grad_norm_two * mid * inv_two, axis=0, keepdims=True)
    grad_mid = dy.astype(F32) + norm_back(mid, inv_two, feed_gain, grad_norm_two)
    grad_branch = grad_mid.astype(BF)
    branch_all = lax.all_gather(grad_branch, "ctx", axis=0, tiled=True)
    grad_inner_out = mm(grad_branch, out_second, 1, 1).astype(BF)
    grad_attended = mm(
        jnp.concatenate([grad_branch, grad_inner_out], axis=1), out_full, 1, 1
    )
    delta = jnp.sum(
        (grad_attended * attended.astype(F32)).reshape(rows * HEADS, HD), axis=1, keepdims=True
    )
    grad_flat = grad_attended.astype(BF).reshape(rows * HEADS, HD)
    gate_second = mm(gate_up_first, gate_half, 0, 0).astype(BF)
    gate_ext = jnp.concatenate(
        [gate_half.reshape(n, w_rows, h), gate_second.reshape(n, r_rows, h)], axis=1
    )
    grad_flat = after(grad_flat, gate_ext)
    down_back = swap(after(down_rows, up_half))
    grad_probs = mm(grad_flat, v_all, 1, 1)
    grad_scores = (probs.astype(F32) * (grad_probs - delta)).astype(BF)
    grad_scores = after(grad_scores, down_back, *out_side)
    grad_k = mm(grad_scores, q_flat, 0, 0) * score_scale
    grad_v = mm(probs, grad_flat, 0, 0)
    kv_part = jnp.concatenate([grad_k, grad_v], axis=1).astype(BF)
    grad_kv = scatter_whole(kv_part)
    grad_q = mm(after(grad_scores, kv_part), k_all) * score_scale
    grad_q_rows = (
        rotate(grad_q.reshape(rows, HEADS, HD), cosine[:, None, :], -sine_rows[:, None, :])
        .reshape(rows, width)
        .astype(BF)
    )
    q_all = lax.all_gather(grad_q_rows, "ctx", axis=0, tiled=True)
    out_parts = [out_here[k] + out_side[k].astype(F32) for k in range(lines)]
    out_lines = [part.astype(BF) for part in out_parts[1:]]
    out_lines = all_after(out_lines, grad_kv)
    out_lines = [hop(part, 4 * (k + 1)) for k, part in enumerate(out_lines)]
    gate_got = exchange(after(gate_ext, grad_kv))
    grad_k_rows = rotate(grad_kv[:, :HD], cosine, -sine_rows)
    grad_kv_rows = jnp.concatenate([grad_k_rows, grad_kv[:, HD:]], axis=1).astype(BF)
    kv_all_grads = gather(grad_kv_rows)
    up_second = mm(gate_up_first, after(up_half, kv_part), 0, 0).astype(BF)
    up_ext = jnp.concatenate(
        [up_half.reshape(n, w_rows, h), up_second.reshape(n, r_rows, h)], axis=1
    )
    up_got = exchange(after(up_ext, grad_kv))
    grad_qkv = jnp.concatenate([grad_q_rows, grad_kv_rows], axis=1)
    grad_qkv = after(grad_qkv, up_ext)
    grad_inner_qkv = mm(grad_qkv, qkv_second, 1, 1).astype(BF)
    grad_norm_one = mm(
        jnp.concatenate([grad_qkv, grad_inner_qkv], axis=1), qkv_full, 1, 1
    )
    attn_gain_rows = jnp.sum(grad_norm_one * x * inv_one, axis=0, keepdims=True)
    grad_input = (grad_mid + norm_back(x, inv_one, attn_gain, grad_norm_one)).astype(BF)
    gate_back = swap(after(gate_got, down_back))
    output = (mid + out_parts[0] + sum(part.astype(F32) for part in out_lines)).astype(BF)

    def both_planes(own):
        own = own.astype(BF)
        return own.astype(F32) + swap(own).astype(F32)


    small = jnp.concatenate(
        [
            (mm(gate_half, gate_b, 1, 1) + mm(up_half, up_b, 1, 1))
            .astype(BF)
            .reshape(n, w_rows, rank),
            mm(down_first[:h], after(down_half, grad_input), 0, 0)
            .astype(BF)
            .reshape(n, w_rows, width * r_rows // w_rows),
        ],
        axis=2,
    )
    small = scatter_whole(reorder(small.reshape(n * w_rows, small.shape[2])))
    gain_rows = jnp.concatenate([attn_gain_rows, feed_gain_rows], axis=0)
    gain_rows = gain_rows.reshape(2, n, w_rows).transpose(1, 0, 2).reshape(2 * n, w_rows)
    gain_rows = scatter_whole(reorder(gain_rows))

    down_grads = stack(plane_id, down_rows, after(down_back, grad_input), width)
    gate_up_grads = collect(
        plane_id, gate_got, after(gate_back, grad_input), w_rows, 0, None
    )
    up_got_other = swap(after(up_got, gate_back))
    gate_up_grads = collect(plane_id, up_got, up_got_other, w_rows, 1, gate_up_grads)

    g_out = mm(inputs[:, ext:], after(branch_all, down_grads[0]), 0, 0).astype(BF)
    g_q = mm(inputs[:, :ext], after(q_all, g_out), 0, 0)
    inputs_rel = reorder(inputs[:, :ext])
    g_kv = mm(inputs_rel, kv_all_grads, 0, 0)
    g_qkv = jnp.concatenate([g_q, g_kv], axis=1).astype(BF)
    g_out = both_planes(after(g_out, gate_back))
    small = both_planes(after(small, gate_back))
    g_qkv = g_qkv.astype(F32) + after(swap(g_qkv), gate_up_grads[0]).astype(F32)
    gain_rows = gain_rows + swap(after(gain_rows, up_got_other))
    g_gu_first = small[:, :rank]
    g_down_second = small[:, rank:].reshape(r_rows, width)
    g_out_first = mm(g_out[:w_rows].astype(BF), out_second, 1, 1)
    g_qkv_first = mm(g_qkv[:w_rows].astype(BF), qkv_second, 1, 1)

    return (
        output[None],
        grad_input[None],
        gain_rows[0],
        g_qkv[:w_rows],
        g_qkv_first,
        g_qkv[w_rows:],
        g_out[:w_rows],
        g_out_first,
        g_out[w_rows:],
        gain_rows[1],
        gate_up_grads[0],
        g_gu_first,
        gate_up_grads[1],
        down_grads[0],
        down_grads[1],
        g_down_second,
    )


def solution(mesh):
    rows = P("grp", "ctx", None)
    vector, matrix = P("ctx"), P("ctx", None)
    return jax.shard_map(
        body,
        mesh=mesh,
        in_specs=(rows, P("grp", None), rows, vector)
        + (matrix,) * 6
        + (vector,)
        + (matrix,) * 6,
        out_specs=(rows, rows, vector) + (matrix,) * 6 + (vector,) + (matrix,) * 6,
        check_vma=False,
    )
```

```python
import functools

import jax
import jax.numpy as jnp
from jax import lax
from jax.experimental import pallas as pl
from jax.experimental.pallas import tpu as pltpu
from jax.sharding import PartitionSpec as P

HEADS = 8
HD = 256
norm_eps = 1e-06
rope_base = 10000.0
BF = jnp.bfloat16
F32 = jnp.float32


def mm(a, b, ca=1, cb=0):
    return lax.dot_general(a, b, (((ca,), (cb,)), ((), ())), preferred_element_type=F32)


def rotate(vectors, cosine, sine_rows):
    front, back = jnp.split(vectors, 2, axis=-1)
    return jnp.concatenate(
        [front * cosine - back * sine_rows, back * cosine + front * sine_rows], axis=-1
    )


def inv_rms(values):
    return lax.rsqrt(jnp.mean(values * values, axis=-1, keepdims=True) + norm_eps)


def norm_back(values, inv, gain, grad):
    weighted = grad * (1.0 + gain)
    inner = jnp.mean(weighted * values, axis=-1, keepdims=True)
    return inv * weighted - values * (inv * inv * inv) * inner


def after(value, *others):
    return lax.optimization_barrier((value,) + others)[0]


def deal_kernel(plane_ref, *refs):
    out_ref = refs[-1]
    each = out_ref.shape[0]
    for k in range(each):
        w_ref, b_ref = refs[k], refs[each + k]
        w_rows = w_ref.shape[0]
        out_ref[k, :w_rows] = w_ref[...]
        out_ref[k, w_rows:] = b_ref[...]


def deal_out(part, plane, matrix, second, n):
    w_rows, r_rows = matrix.shape[0], second.shape[0]
    cols = matrix.shape[1] // (4 * n)
    each = 4

    def column(k, s, plane_ref):
        return (0, (part * n + s * each + k) * 2 + plane_ref[0])

    maps = [functools.partial(column, k) for k in range(each)]
    return pl.pallas_call(
        deal_kernel,
        out_shape=jax.ShapeDtypeStruct((n, w_rows + r_rows, cols), BF),
        grid_spec=pltpu.PrefetchScalarGridSpec(
            num_scalar_prefetch=1,
            grid=(n // each,),
            in_specs=[pl.BlockSpec((w_rows, cols), m) for m in maps]
            + [pl.BlockSpec((r_rows, cols), m) for m in maps],
            out_specs=pl.BlockSpec((each, w_rows + r_rows, cols), lambda s, p: (s, 0, 0)),
        ),
        cost_estimate=pl.CostEstimate(
            flops=0, transcendentals=0, bytes_accessed=4 * n * (w_rows + r_rows) * cols
        ),
    )(plane, *([matrix] * each), *([second] * each))


def fold_kernel(gate_ref, up_ref, b_gate_ref, b_up_ref, a_ref, *refs):
    out_ref = refs[-1]
    each, w_rows = gate_ref.shape[0], a_ref.shape[0] // gate_ref.shape[0]
    cols = b_gate_ref.shape[1]
    gate = mm(a_ref[...], b_gate_ref[...])
    up = mm(a_ref[...], b_up_ref[...])
    for k in range(each):
        part = slice(k * w_rows, (k + 1) * w_rows)
        out_ref[part, :cols] = (gate_ref[k, :w_rows].astype(F32) + gate[part]).astype(BF)
        out_ref[part, cols:] = (up_ref[k, :w_rows].astype(F32) + up[part]).astype(BF)


def fold(gate, up, first, place, given):
    n, ext, cols = gate.shape
    width, rank = first.shape
    w_rows = width // n
    each = max(1, min(4, 512 // w_rows))
    seconds = [x[:, w_rows:].reshape(rank, cols) for x in (gate, up)]
    piece = pl.BlockSpec((each, ext, cols), lambda s: (s, 0, 0))
    whole = pl.BlockSpec((rank, cols), lambda s: (0, 0))
    held = [] if given is None else [given]
    return pl.pallas_call(
        fold_kernel,
        out_shape=jax.ShapeDtypeStruct((width, 4 * cols), BF),
        grid=(n // each,),
        in_specs=[piece, piece, whole, whole]
        + [pl.BlockSpec((each * w_rows, rank), lambda s: (s, 0))]
        + [pl.BlockSpec(memory_space=pl.ANY)] * len(held),
        out_specs=pl.BlockSpec((each * w_rows, 2 * cols), lambda s: (s, place)),
        input_output_aliases={5: 0} if held else {},
        cost_estimate=pl.CostEstimate(
            flops=4 * width * rank * cols, transcendentals=0, bytes_accessed=8 * width * cols
        ),
    )(gate, up, *seconds, first, *held), seconds


def forward_kernel(core_ref, x_ref, w_ref, hidden_ref, act_ref, slope_ref):
    h = act_ref.shape[1] // 2
    rows = hidden_ref.shape[1]
    c = 0.7978845608028654
    for k in (0, 1):
        both = mm(x_ref[...], w_ref[:, 2 * k * h : 2 * (k + 1) * h])
        gate, up = both[:, :h], both[:, h:]
        square = gate * gate
        t = jnp.tanh(c * gate * (1.0 + 0.044715 * square))
        half_up = 0.5 * (1.0 + t)
        act = gate * half_up
        slope = half_up + 0.5 * gate * (1.0 - t * t) * (c * (1.0 + 3 * 0.044715 * square))
        part = slice(k * h, (k + 1) * h)
        hidden = (act * up).astype(BF)
        for j in range(hidden_ref.shape[0]):
            hidden_ref[j, :, part] = hidden[j * rows : (j + 1) * rows]
        act_ref[:, part] = act.astype(BF)
        slope_ref[:, part] = (slope * up).astype(BF)


def owner(tiles):
    def place(i, core_ref):
        mine = i < tiles // 2
        return (i % (tiles // 2), jnp.where(mine, core_ref[0], 1 - core_ref[0]), 0, 0)

    return place


def forward(core, x, w, rows):
    t, d = x.shape
    f = w.shape[1] // 2
    tile = 2 * rows
    out = pl.BlockSpec((tile, f), lambda i, _: (i, 0))
    ordered = pl.BlockSpec((2, None, rows, f), owner(t // tile))
    return pl.pallas_call(
        forward_kernel,
        out_shape=(jax.ShapeDtypeStruct((t // tile, 2, rows, f), BF),)
        + (jax.ShapeDtypeStruct((t, f), BF),) * 2,
        grid_spec=pltpu.PrefetchScalarGridSpec(
            num_scalar_prefetch=1,
            grid=(t // tile,),
            in_specs=[
                pl.BlockSpec((tile, d), lambda i, _: (i, 0)),
                pl.BlockSpec((d, 2 * f), lambda i, _: (0, 0)),
            ],
            out_specs=(ordered, out, out),
        ),
        compiler_params=pltpu.CompilerParams(vmem_limit_bytes=44 * 2**20),
        cost_estimate=pl.CostEstimate(
            flops=4 * t * d * f, transcendentals=t * f, bytes_accessed=2 * (t * d + 2 * d * f + 3 * t * f)
        ),
    )(core, x, w)


def backward_kernel(core_ref, dy_ref, w_ref, act_ref, slope_ref, out_ref):
    h = act_ref.shape[1] // 2
    dy = dy_ref[...].reshape(act_ref.shape[0], dy_ref.shape[2])
    for k in (0, 1):
        part = slice(k * h, (k + 1) * h)
        grad = mm(dy, w_ref[part, :], 1, 1)
        out_ref[:, 2 * k * h : (2 * k + 1) * h] = (grad * slope_ref[:, part].astype(F32)).astype(BF)
        out_ref[:, (2 * k + 1) * h : 2 * (k + 1) * h] = (
            grad * act_ref[:, part].astype(F32)
        ).astype(BF)


def backward(core, dy, w, act, slope, rows):
    t, f = act.shape
    d = dy.shape[1]
    tile = 2 * rows
    given = pl.BlockSpec((tile, f), lambda i, _: (i, 0))
    return pl.pallas_call(
        backward_kernel,
        out_shape=jax.ShapeDtypeStruct((t, 2 * f), BF),
        grid_spec=pltpu.PrefetchScalarGridSpec(
            num_scalar_prefetch=1,
            grid=(t // tile,),
            in_specs=[
                pl.BlockSpec((2, None, rows, d), owner(t // tile)),
                pl.BlockSpec((f, d), lambda i, _: (0, 0)),
                given,
                given,
            ],
            out_specs=pl.BlockSpec((tile, 2 * f), lambda i, _: (i, 0)),
        ),
        compiler_params=pltpu.CompilerParams(vmem_limit_bytes=44 * 2**20),
        cost_estimate=pl.CostEstimate(
            flops=2 * t * d * f, transcendentals=0, bytes_accessed=2 * (t * d + d * f + 4 * t * f)
        ),
    )(core, dy.reshape(t // tile, 2, rows, d), w, act, slope)


def collect_kernel(plane_ref, mine, other, *refs):
    w_ref, b_ref = refs[-2:]
    w_rows = w_ref.shape[0]
    each, _, cols = mine.shape
    for plane in (0, 1):

        @pl.when(plane_ref[0] == plane)
        def _():
            for k in range(each):
                for ref, h in ((mine, plane), (other, 1 - plane)):
                    at = slice((2 * k + h) * cols, (2 * k + h + 1) * cols)
                    w_ref[:, at] = ref[k, :w_rows].astype(F32)
                    b_ref[:, at] = ref[k, w_rows:].astype(F32)


def collect(plane, mine, other, w_rows, part, given):
    n, ext, cols = mine.shape
    each = 4
    piece = pl.BlockSpec((each, ext, cols), lambda s, _: (s, 0, 0))
    held = [] if given is None else list(given)
    steps = n // each
    return pl.pallas_call(
        collect_kernel,
        out_shape=(
            jax.ShapeDtypeStruct((w_rows, 4 * n * cols), F32),
            jax.ShapeDtypeStruct((ext - w_rows, 4 * n * cols), F32),
        ),
        grid_spec=pltpu.PrefetchScalarGridSpec(
            num_scalar_prefetch=1,
            grid=(steps,),
            in_specs=[piece, piece] + [pl.BlockSpec(memory_space=pl.ANY)] * len(held),
            out_specs=(
                pl.BlockSpec((w_rows, 2 * cols * each), lambda s, _: (0, part * steps + s)),
                pl.BlockSpec((ext - w_rows, 2 * cols * each), lambda s, _: (0, part * steps + s)),
            ),
        ),
        input_output_aliases={3: 0, 4: 1} if held else {},
        cost_estimate=pl.CostEstimate(
            flops=0, transcendentals=0, bytes_accessed=12 * n * ext * cols
        ),
    )(plane, mine, other, *held)


def stack_kernel(plane_ref, mine, other, w_ref, a_ref):
    width = w_ref.shape[1]
    own = pl.program_id(0) == plane_ref[0]

    @pl.when(own)
    def _():
        w_ref[...] = mine[:, :width].astype(F32)
        a_ref[...] = mine[:, width:].astype(F32)

    @pl.when(jnp.logical_not(own))
    def _():
        w_ref[...] = other[:, :width].astype(F32)
        a_ref[...] = other[:, width:].astype(F32)


def stack(plane, mine, other, width):
    half, cols = mine.shape
    tile = min(half, 128)
    tiles = half // tile
    given = pl.BlockSpec((tile, cols), lambda h, t, _: (t, 0))
    return pl.pallas_call(
        stack_kernel,
        out_shape=(
            jax.ShapeDtypeStruct((2 * half, width), F32),
            jax.ShapeDtypeStruct((2 * half, cols - width), F32),
        ),
        grid_spec=pltpu.PrefetchScalarGridSpec(
            num_scalar_prefetch=1,
            grid=(2, tiles),
            in_specs=[given, given],
            out_specs=(
                pl.BlockSpec((tile, width), lambda h, t, _: (h * tiles + t, 0)),
                pl.BlockSpec((tile, cols - width), lambda h, t, _: (h * tiles + t, 0)),
            ),
        ),
        cost_estimate=pl.CostEstimate(
            flops=0, transcendentals=0, bytes_accessed=16 * half * cols
        ),
    )(plane, mine, other)


def body(
    tokens,
    segments,
    output_cotangent_rows,
    attention_norm_gain,
    query_key_value_matrix,
    query_key_value_adapter_first,
    query_key_value_adapter_second,
    output_matrix,
    output_adapter_first,
    output_adapter_second,
    feed_norm_gain,
    gate_up_matrix,
    gate_up_adapter_first,
    gate_up_adapter_second,
    down_matrix,
    down_adapter_first,
    down_adapter_second,
):
    n = lax.axis_size("ctx")
    me = lax.axis_index("ctx")
    plane = lax.axis_index("grp")
    lines = n // 4
    rows = tokens.shape[1]
    width = tokens.shape[2]
    seq = rows * n
    rank = query_key_value_adapter_first.shape[1]
    qkv_cols = query_key_value_matrix.shape[1]
    feed_dev = down_matrix.shape[0]
    feed_half = feed_dev // 2
    w_rows = width // n
    r_rows = rank // n
    score_scale = HD ** (-0.5)

    def hop(x, k):
        return lax.ppermute(x, "ctx", [(i, i ^ k) for i in range(n)])

    def swap(x):
        return lax.ppermute(x, "grp", [(0, 1), (1, 0)])

    def swap_pieces(x, count):
        each = x.shape[0] // count
        return [swap(x[k * each : (k + 1) * each]) for k in range(count)]

    rel = jnp.arange(n, dtype=jnp.int32)
    rel = me ^ (rel // (2 * lines) + 2 * (rel // lines % 2) + 4 * (rel % lines))

    def reorder(x):
        r = x.shape[0] // n
        order = [4 * k + 2 * j + i for i in (0, 1) for j in (0, 1) for k in range(lines)]
        return jnp.concatenate(
            [lax.dynamic_slice_in_dim(x, (me ^ k) * r, r) for k in order], axis=0
        )

    def lines_of(x):
        return [x] + [hop(x, 4 * k) for k in range(1, lines)]

    def gather(x):
        along = lines_of(x)
        near = jnp.concatenate(along + [hop(b, 2) for b in along], axis=0)
        return jnp.concatenate([near, hop(near, 1)], axis=0)

    chip, core = me // 2, me % 2

    def gather_chips(x):
        along = lines_of(x)
        blocks = [(2 * k, b) for k, b in enumerate(along)]
        blocks = blocks + [(k + 1, hop(b, 2)) for k, b in blocks]
        near = jnp.zeros((x.shape[0] * n // 2, x.shape[1]), x.dtype)
        for k, b in blocks:
            near = lax.dynamic_update_slice_in_dim(near, b, (chip ^ k) * x.shape[0], 0)
        return near

    def fold_core(near, arrived):
        r = near.shape[0] // (2 * lines)

        def block(k):
            at = (chip ^ k) * r
            a = lax.dynamic_slice_in_dim(near, at, r).astype(F32)
            return a + lax.dynamic_slice_in_dim(arrived, at, r).astype(F32)

        here = [block(2 * k) for k in range(lines)]
        return here, [block(2 * k + 1).astype(near.dtype) for k in range(lines)]

    def all_after(values, *others):
        return lax.optimization_barrier((*values, *others))[: len(values)]

    def scatter(near, far):
        kind = near.dtype
        mine = near.astype(F32) + hop(far, 1).astype(F32)
        half = near.shape[0] // 2
        mine = mine[:half] + hop(mine[half:].astype(kind), 2).astype(F32)
        r = half // lines
        total = mine[:r]
        for k in range(1, lines):
            total = total + hop(mine[k * r : (k + 1) * r].astype(kind), 4 * k).astype(F32)
        return total

    def scatter_whole(partial):
        half = partial.shape[0] // 2
        return scatter(partial[:half], partial[half:])

    x = tokens[0].astype(F32)
    dy = output_cotangent_rows[0]
    plane_id = plane.astype(jnp.int32).reshape(1)
    ext = w_rows + r_rows

    def beside(second):
        return second.reshape(w_rows, second.shape[1] * r_rows // w_rows)

    def apart(columns):
        return columns.reshape(rank, columns.shape[1] * w_rows // r_rows)

    q_second = qkv_cols * r_rows // w_rows
    o_second = width * r_rows // w_rows
    at_q = qkv_cols + rank
    pad = -(at_q + q_second) % 128
    gains = jnp.concatenate(
        [
            attention_norm_gain[:, None],
            feed_norm_gain[:, None],
            jnp.zeros((w_rows, pad - 2), BF),
        ],
        axis=1,
    )
    qkv_ext = jnp.concatenate(
        [
            query_key_value_matrix,
            query_key_value_adapter_first,
            beside(query_key_value_adapter_second),
            gains,
        ],
        axis=1,
    )
    qkv_got = lax.all_gather(qkv_ext, "ctx", axis=0, tiled=True)
    out_ext = jnp.concatenate(
        [
            output_matrix,
            output_adapter_first,
            gate_up_adapter_first,
            beside(output_adapter_second),
            beside(down_adapter_second),
        ],
        axis=1,
    )
    out_got = lax.all_gather(out_ext, "ctx", axis=0, tiled=True)
    qkv_full = qkv_got[:, :at_q]
    qkv_second = apart(qkv_got[:, at_q : at_q + q_second])
    gains_full = qkv_got[:, at_q + q_second : at_q + q_second + 2].astype(F32).T
    attn_gain, feed_gain = gains_full[:1], gains_full[1:]

    def exchange(pieces):
        flat = pieces.reshape(n * ext, feed_half)
        return lax.all_to_all(flat, "ctx", 0, 0, tiled=True).reshape(n, ext, feed_half)

    gate_mine = exchange(deal_out(0, plane_id, gate_up_matrix, gate_up_adapter_second, n))
    up_sent = deal_out(1, plane_id, gate_up_matrix, gate_up_adapter_second, n)

    def own_first(x):
        pair = x.reshape(2, feed_half, x.shape[1])
        a = lax.dynamic_index_in_dim(pair, plane, 0, False)
        b = lax.dynamic_index_in_dim(pair, 1 - plane, 0, False)
        return jnp.concatenate([a, b], axis=0)

    down_first, down_rows = own_first(down_adapter_first), own_first(down_matrix)

    def positions(device):
        within = jnp.arange(rows, dtype=jnp.int32)
        half = rows // 2
        block = jnp.where(within < half, device[:, None], 2 * n - 1 - device[:, None])
        return block * half + within % half

    local_pos = positions(me[None])[0]
    key_pos = positions(rel).reshape(seq)
    half = rows // 2
    local_seg = jnp.concatenate(
        [
            lax.dynamic_slice_in_dim(segments[0], me * half, half),
            lax.dynamic_slice_in_dim(segments[0], (2 * n - 1 - me) * half, half),
        ]
    )
    doc_start = jnp.sum(
        (segments[0][None, :] < local_seg[:, None]).astype(jnp.int32), axis=1
    )
    allowed = (key_pos[None, :] >= doc_start[:, None]) & (key_pos[None, :] <= local_pos[:, None])
    frequency = rope_base ** (-2.0 * jnp.arange(HD // 2, dtype=F32) / HD)
    angle_rows = local_pos.astype(F32)[:, None] * frequency[None, :]
    cosine, sine_rows = jnp.cos(angle_rows), jnp.sin(angle_rows)

    inv_one = inv_rms(x)
    norm_one = (x * inv_one * (1.0 + attn_gain)).astype(BF)
    norm_one = after(norm_one, gate_mine, up_sent)
    qkv_base = mm(norm_one, qkv_full)
    inner_qkv = qkv_base[:, qkv_cols:].astype(BF)
    qkv = qkv_base[:, :qkv_cols] + mm(inner_qkv, qkv_second)
    q = rotate(
        qkv[:, :width].reshape(rows, HEADS, HD), cosine[:, None, :], sine_rows[:, None, :]
    ).astype(BF)
    q_flat = q.reshape(rows * HEADS, HD)
    k_mine = rotate(qkv[:, width : width + HD], cosine, sine_rows).astype(BF)
    kv_mine = jnp.concatenate([k_mine, qkv[:, width + HD :].astype(BF)], axis=1)
    kv_all = gather(kv_mine)
    dy_got = lax.all_gather(after(dy, kv_mine), "ctx", axis=0, tiled=True)
    up_mine = exchange(after(up_sent, kv_all))
    gate_pieces = swap_pieces(gate_mine, 2)
    kv_all = after(kv_all, gate_pieces[0])
    k_all, v_all = kv_all[:, :HD], kv_all[:, HD:]
    raw = mm(q_flat, k_all, 1, 1).reshape(rows, HEADS, seq) * score_scale
    scores = jnp.where(allowed[:, None, :], raw, -jnp.inf)
    peak = jnp.max(scores, axis=-1, keepdims=True)
    unnormed = jnp.exp(scores - peak)
    total = jnp.sum(unnormed, axis=-1, keepdims=True)
    probs = (unnormed / total).astype(BF).reshape(rows * HEADS, seq)
    out_got = after(out_got, probs)
    out_full = out_got[:, : width + rank]
    gate_up_first = out_got[:, width + rank : width + 2 * rank]
    out_second = apart(out_got[:, width + 2 * rank : width + 2 * rank + o_second])
    down_second = apart(out_got[:, width + 2 * rank + o_second :])
    down_eff = (down_rows.astype(F32) + mm(down_first, down_second)).astype(BF)
    attended_f = mm(after(probs, gate_pieces[1]), v_all)
    gate_other = jnp.concatenate(gate_pieces, axis=0)
    attended = attended_f.reshape(rows, width).astype(BF)
    attended = after(attended, up_mine)
    up_pieces = swap_pieces(up_mine, 2)
    out_base = mm(attended, out_full)
    inner_out = out_base[:, width:].astype(BF)
    mid = x + out_base[:, :width] + mm(inner_out, out_second)

    inv_two = inv_rms(mid)
    norm_two = (mid * inv_two * (1.0 + feed_gain)).astype(BF)
    near_rows = gather_chips(norm_two)
    core_id = core.astype(jnp.int32).reshape(1)
    up_other = jnp.concatenate(up_pieces, axis=0)
    w_eff, (gate_b, up_b) = fold(gate_mine, up_mine, gate_up_first, 0, None)
    w_eff, _ = fold(gate_other, up_other, gate_up_first, 1, w_eff)
    near_rows = after(near_rows, w_eff, down_eff)
    all_rows = jnp.concatenate([near_rows, hop(near_rows, 1)], axis=0)
    hidden, act, slope = forward(core_id, all_rows, w_eff, rows)
    hidden = hidden.reshape(seq, feed_dev)
    out_part = mm(hidden, down_eff).astype(BF)
    out_sum = lax.psum_scatter(out_part, "ctx", scatter_dimension=0, tiled=True)
    h = feed_half
    half_seq = seq // 2
    down_part = mm(after(hidden, out_part)[:, h:], dy_got, 0, 0).astype(BF)
    grads = backward(core_id, after(dy_got, down_part), down_eff, act, slope, rows)
    down_part = swap(down_part)
    far_part = mm(grads[half_seq:], w_eff, 1, 1).astype(BF)
    near_part = mm(after(grads, far_part)[:half_seq], w_eff, 1, 1).astype(BF)
    here, there = fold_core(near_part, hop(far_part, 1))
    sides = [hop(part, 2) for part in there]

    late_rows, late_grads = lax.optimization_barrier(
        (all_rows, grads, near_part, *there)
    )[:2]
    other_part = mm(late_rows, late_grads[:, 2 * h :], 0, 0).astype(BF)
    gate_part, up_part = swap(other_part[:, :h]), swap(other_part[:, h:])
    sides = all_after(sides, other_part)
    sums = [a + b.astype(F32) for a, b in zip(here, sides)]
    line_sums = [part.astype(BF) for part in sums[1:]]
    arrivals = [hop(part, 4 * (k + 1)) for k, part in enumerate(line_sums)]
    down_half = (
        mm(after(hidden, other_part)[:, :h], dy_got, 0, 0) + down_part.astype(F32)
    ).astype(BF)
    g_down_first = mm(down_half, down_second, 1, 1).astype(BF)
    down_rows = jnp.concatenate([down_half, g_down_first], axis=1)

    late_rows = after(all_rows, down_rows, *line_sums)
    gate_half = (mm(late_rows, grads[:, :h], 0, 0) + gate_part.astype(F32)).astype(BF)

    pieces = jnp.concatenate(
        [
            norm_one.reshape(rows, n, w_rows),
            inner_qkv.reshape(rows, n, r_rows),
            attended.reshape(rows, n, w_rows),
            inner_out.reshape(rows, n, r_rows),
        ],
        axis=2,
    ).transpose(1, 0, 2)
    pieces = after(pieces, all_rows)
    inputs = lax.all_to_all(pieces.reshape(seq, 2 * ext), "ctx", 0, 0, tiled=True)

    arrivals = all_after(arrivals, gate_half, inputs)
    grad_norm_two = sums[0] + sum(part.astype(F32) for part in arrivals)
    feed_gain_rows = jnp.sum(grad_norm_two * mid * inv_two, axis=0, keepdims=True)
    grad_mid = dy.astype(F32) + norm_back(mid, inv_two, feed_gain, grad_norm_two)
    grad_branch = grad_mid.astype(BF)
    branch_all = lax.all_gather(grad_branch, "ctx", axis=0, tiled=True)
    grad_inner_out = mm(grad_branch, out_second, 1, 1).astype(BF)
    grad_attended = mm(
        jnp.concatenate([grad_branch, grad_inner_out], axis=1), out_full, 1, 1
    )
    delta = jnp.sum(
        (grad_attended * attended.astype(F32)).reshape(rows * HEADS, HD), axis=1, keepdims=True
    )
    grad_flat = grad_attended.astype(BF).reshape(rows * HEADS, HD)
    gate_second = mm(gate_up_first, gate_half, 0, 0).astype(BF)
    gate_ext = jnp.concatenate(
        [gate_half.reshape(n, w_rows, h), gate_second.reshape(n, r_rows, h)], axis=1
    )
    gate_got = exchange(gate_ext)
    grad_flat = after(grad_flat, gate_ext, out_sum)
    grad_probs = mm(grad_flat, v_all, 1, 1)
    grad_scores = (probs.astype(F32) * (grad_probs - delta)).astype(BF)
    grad_scores = after(grad_scores, up_part)
    grad_k = mm(grad_scores, q_flat, 0, 0) * score_scale
    grad_v = mm(probs, grad_flat, 0, 0)
    kv_part = jnp.concatenate([grad_k, grad_v], axis=1).astype(BF)
    grad_kv = scatter_whole(kv_part)
    grad_q = mm(after(grad_scores, kv_part), k_all) * score_scale
    grad_q_rows = (
        rotate(grad_q.reshape(rows, HEADS, HD), cosine[:, None, :], -sine_rows[:, None, :])
        .reshape(rows, width)
        .astype(BF)
    )
    q_all = lax.all_gather(grad_q_rows, "ctx", axis=0, tiled=True)
    up_half = (
        mm(after(all_rows, grad_q_rows, gate_got), grads[:, h : 2 * h], 0, 0)
        + up_part.astype(F32)
    ).astype(BF)
    down_back = swap(after(down_rows, up_part))
    grad_kv = after(grad_kv, up_half, down_back)
    grad_k_rows = rotate(grad_kv[:, :HD], cosine, -sine_rows)
    grad_kv_rows = jnp.concatenate([grad_k_rows, grad_kv[:, HD:]], axis=1).astype(BF)
    kv_all_grads = gather(grad_kv_rows)
    up_second = mm(gate_up_first, after(up_half, grad_kv_rows), 0, 0).astype(BF)
    up_ext = jnp.concatenate(
        [up_half.reshape(n, w_rows, h), up_second.reshape(n, r_rows, h)], axis=1
    )
    up_ext = after(up_ext, gate_got)
    up_got = exchange(up_ext)
    grad_qkv = jnp.concatenate([grad_q_rows, grad_kv_rows], axis=1)
    grad_qkv = after(grad_qkv, up_ext)
    grad_inner_qkv = mm(grad_qkv, qkv_second, 1, 1).astype(BF)
    grad_norm_one = mm(
        jnp.concatenate([grad_qkv, grad_inner_qkv], axis=1), qkv_full, 1, 1
    )
    attn_gain_rows = jnp.sum(grad_norm_one * x * inv_one, axis=0, keepdims=True)
    grad_input = (grad_mid + norm_back(x, inv_one, attn_gain, grad_norm_one)).astype(BF)
    gate_back = swap(after(gate_got, down_back))
    output = (mid + out_sum.astype(F32)).astype(BF)

    def both_planes(own):
        own = own.astype(BF)
        return own.astype(F32) + swap(own).astype(F32)


    small = jnp.concatenate(
        [
            (mm(gate_half, gate_b, 1, 1) + mm(up_half, up_b, 1, 1))
            .astype(BF)
            .reshape(n, w_rows, rank),
            mm(down_first[:h], after(down_half, grad_input), 0, 0)
            .astype(BF)
            .reshape(n, w_rows, width * r_rows // w_rows),
        ],
        axis=2,
    )
    small = scatter_whole(reorder(small.reshape(n * w_rows, small.shape[2])))
    gain_rows = jnp.concatenate([attn_gain_rows, feed_gain_rows], axis=0)
    gain_rows = gain_rows.reshape(2, n, w_rows).transpose(1, 0, 2).reshape(2 * n, w_rows)
    gain_rows = scatter_whole(reorder(gain_rows))

    down_grads = stack(plane_id, down_rows, after(down_back, grad_input), width)
    gate_up_grads = collect(
        plane_id, gate_got, after(gate_back, grad_input), w_rows, 0, None
    )
    up_got_other = swap(after(up_got, gate_back))
    gate_up_grads = collect(plane_id, up_got, up_got_other, w_rows, 1, gate_up_grads)

    g_out = mm(inputs[:, ext:], after(branch_all, down_grads[0]), 0, 0).astype(BF)
    g_q = mm(inputs[:, :ext], after(q_all, g_out), 0, 0)
    inputs_rel = reorder(inputs[:, :ext])
    g_kv = mm(inputs_rel, kv_all_grads, 0, 0)
    g_qkv = jnp.concatenate([g_q, g_kv], axis=1).astype(BF)
    g_out = both_planes(after(g_out, gate_back))
    small = both_planes(after(small, gate_back))
    g_qkv = g_qkv.astype(F32) + after(swap(g_qkv), gate_up_grads[0]).astype(F32)
    gain_rows = gain_rows + swap(after(gain_rows, up_got_other))
    g_gu_first = small[:, :rank]
    g_down_second = small[:, rank:].reshape(r_rows, width)
    g_out_first = mm(g_out[:w_rows].astype(BF), out_second, 1, 1)
    g_qkv_first = mm(g_qkv[:w_rows].astype(BF), qkv_second, 1, 1)

    return (
        output[None],
        grad_input[None],
        gain_rows[0],
        g_qkv[:w_rows],
        g_qkv_first,
        g_qkv[w_rows:],
        g_out[:w_rows],
        g_out_first,
        g_out[w_rows:],
        gain_rows[1],
        gate_up_grads[0],
        g_gu_first,
        gate_up_grads[1],
        down_grads[0],
        down_grads[1],
        g_down_second,
    )


def solution(mesh):
    rows = P("grp", "ctx", None)
    vector, matrix = P("ctx"), P("ctx", None)
    return jax.shard_map(
        body,
        mesh=mesh,
        in_specs=(rows, P("grp", None), rows, vector)
        + (matrix,) * 6
        + (vector,)
        + (matrix,) * 6,
        out_specs=(rows, rows, vector) + (matrix,) * 6 + (vector,) + (matrix,) * 6,
        check_vma=False,
    )
```

```python
import functools

import jax
import jax.numpy as jnp
from jax import lax
from jax.experimental import pallas as pl
from jax.experimental.pallas import tpu as pltpu
from jax.sharding import PartitionSpec as P

HEADS = 8
HD = 256
norm_eps = 1e-06
rope_base = 10000.0
BF = jnp.bfloat16
F32 = jnp.float32


def mm(a, b, ca=1, cb=0):
    return lax.dot_general(a, b, (((ca,), (cb,)), ((), ())), preferred_element_type=F32)


def rotate(vectors, cosine, sine_rows):
    front, back = jnp.split(vectors, 2, axis=-1)
    return jnp.concatenate(
        [front * cosine - back * sine_rows, back * cosine + front * sine_rows], axis=-1
    )


def inv_rms(values):
    return lax.rsqrt(jnp.mean(values * values, axis=-1, keepdims=True) + norm_eps)


def norm_back(values, inv, gain, grad):
    weighted = grad * (1.0 + gain)
    inner = jnp.mean(weighted * values, axis=-1, keepdims=True)
    return inv * weighted - values * (inv * inv * inv) * inner


def after(value, *others):
    return lax.optimization_barrier((value,) + others)[0]


def deal_kernel(plane_ref, *refs):
    out_ref = refs[-1]
    each = out_ref.shape[0]
    for k in range(each):
        w_ref, b_ref = refs[k], refs[each + k]
        w_rows = w_ref.shape[0]
        out_ref[k, :w_rows] = w_ref[...]
        out_ref[k, w_rows:] = b_ref[...]


def deal_out(part, plane, matrix, second, n):
    w_rows, r_rows = matrix.shape[0], second.shape[0]
    cols = matrix.shape[1] // (4 * n)
    each = 4

    def column(k, s, plane_ref):
        return (0, (part * n + s * each + k) * 2 + plane_ref[0])

    maps = [functools.partial(column, k) for k in range(each)]
    return pl.pallas_call(
        deal_kernel,
        out_shape=jax.ShapeDtypeStruct((n, w_rows + r_rows, cols), BF),
        grid_spec=pltpu.PrefetchScalarGridSpec(
            num_scalar_prefetch=1,
            grid=(n // each,),
            in_specs=[pl.BlockSpec((w_rows, cols), m) for m in maps]
            + [pl.BlockSpec((r_rows, cols), m) for m in maps],
            out_specs=pl.BlockSpec((each, w_rows + r_rows, cols), lambda s, p: (s, 0, 0)),
        ),
        cost_estimate=pl.CostEstimate(
            flops=0, transcendentals=0, bytes_accessed=4 * n * (w_rows + r_rows) * cols
        ),
    )(plane, *([matrix] * each), *([second] * each))


def fold_kernel(gate_ref, up_ref, b_gate_ref, b_up_ref, a_ref, *refs):
    out_ref = refs[-1]
    each, w_rows = gate_ref.shape[0], a_ref.shape[0] // gate_ref.shape[0]
    cols = b_gate_ref.shape[1]
    gate = mm(a_ref[...], b_gate_ref[...])
    up = mm(a_ref[...], b_up_ref[...])
    for k in range(each):
        part = slice(k * w_rows, (k + 1) * w_rows)
        out_ref[part, :cols] = (gate_ref[k, :w_rows].astype(F32) + gate[part]).astype(BF)
        out_ref[part, cols:] = (up_ref[k, :w_rows].astype(F32) + up[part]).astype(BF)


def fold(gate, up, first, place, given):
    n, ext, cols = gate.shape
    width, rank = first.shape
    w_rows = width // n
    each = max(1, min(4, 512 // w_rows))
    seconds = [x[:, w_rows:].reshape(rank, cols) for x in (gate, up)]
    piece = pl.BlockSpec((each, ext, cols), lambda s: (s, 0, 0))
    whole = pl.BlockSpec((rank, cols), lambda s: (0, 0))
    held = [] if given is None else [given]
    return pl.pallas_call(
        fold_kernel,
        out_shape=jax.ShapeDtypeStruct((width, 4 * cols), BF),
        grid=(n // each,),
        in_specs=[piece, piece, whole, whole]
        + [pl.BlockSpec((each * w_rows, rank), lambda s: (s, 0))]
        + [pl.BlockSpec(memory_space=pl.ANY)] * len(held),
        out_specs=pl.BlockSpec((each * w_rows, 2 * cols), lambda s: (s, place)),
        input_output_aliases={5: 0} if held else {},
        cost_estimate=pl.CostEstimate(
            flops=4 * width * rank * cols, transcendentals=0, bytes_accessed=8 * width * cols
        ),
    )(gate, up, *seconds, first, *held), seconds


def forward_kernel(core_ref, x_ref, w_ref, hidden_ref, act_ref, slope_ref):
    h = act_ref.shape[1] // 2
    rows = hidden_ref.shape[1]
    c = 0.7978845608028654
    for k in (0, 1):
        both = mm(x_ref[...], w_ref[:, 2 * k * h : 2 * (k + 1) * h])
        gate, up = both[:, :h], both[:, h:]
        square = gate * gate
        t = jnp.tanh(c * gate * (1.0 + 0.044715 * square))
        half_up = 0.5 * (1.0 + t)
        act = gate * half_up
        slope = half_up + 0.5 * gate * (1.0 - t * t) * (c * (1.0 + 3 * 0.044715 * square))
        part = slice(k * h, (k + 1) * h)
        hidden = (act * up).astype(BF)
        for j in range(hidden_ref.shape[0]):
            hidden_ref[j, :, part] = hidden[j * rows : (j + 1) * rows]
        act_ref[:, part] = act.astype(BF)
        slope_ref[:, part] = (slope * up).astype(BF)


def owner(tiles):
    def place(i, core_ref):
        mine = i < tiles // 2
        return (i % (tiles // 2), jnp.where(mine, core_ref[0], 1 - core_ref[0]), 0, 0)

    return place


def forward(core, x, w, rows):
    t, d = x.shape
    f = w.shape[1] // 2
    tile = 2 * rows
    out = pl.BlockSpec((tile, f), lambda i, _: (i, 0))
    ordered = pl.BlockSpec((2, None, rows, f), owner(t // tile))
    return pl.pallas_call(
        forward_kernel,
        out_shape=(jax.ShapeDtypeStruct((t // tile, 2, rows, f), BF),)
        + (jax.ShapeDtypeStruct((t, f), BF),) * 2,
        grid_spec=pltpu.PrefetchScalarGridSpec(
            num_scalar_prefetch=1,
            grid=(t // tile,),
            in_specs=[
                pl.BlockSpec((tile, d), lambda i, _: (i, 0)),
                pl.BlockSpec((d, 2 * f), lambda i, _: (0, 0)),
            ],
            out_specs=(ordered, out, out),
        ),
        compiler_params=pltpu.CompilerParams(vmem_limit_bytes=44 * 2**20),
        cost_estimate=pl.CostEstimate(
            flops=4 * t * d * f, transcendentals=t * f, bytes_accessed=2 * (t * d + 2 * d * f + 3 * t * f)
        ),
    )(core, x, w)


def backward_kernel(core_ref, dy_ref, w_ref, act_ref, slope_ref, out_ref):
    h = act_ref.shape[1] // 2
    dy = dy_ref[...].reshape(act_ref.shape[0], dy_ref.shape[2])
    for k in (0, 1):
        part = slice(k * h, (k + 1) * h)
        grad = mm(dy, w_ref[part, :], 1, 1)
        out_ref[:, 2 * k * h : (2 * k + 1) * h] = (grad * slope_ref[:, part].astype(F32)).astype(BF)
        out_ref[:, (2 * k + 1) * h : 2 * (k + 1) * h] = (
            grad * act_ref[:, part].astype(F32)
        ).astype(BF)


def backward(core, dy, w, act, slope, rows):
    t, f = act.shape
    d = dy.shape[1]
    tile = 2 * rows
    given = pl.BlockSpec((tile, f), lambda i, _: (i, 0))
    return pl.pallas_call(
        backward_kernel,
        out_shape=jax.ShapeDtypeStruct((t, 2 * f), BF),
        grid_spec=pltpu.PrefetchScalarGridSpec(
            num_scalar_prefetch=1,
            grid=(t // tile,),
            in_specs=[
                pl.BlockSpec((2, None, rows, d), owner(t // tile)),
                pl.BlockSpec((f, d), lambda i, _: (0, 0)),
                given,
                given,
            ],
            out_specs=pl.BlockSpec((tile, 2 * f), lambda i, _: (i, 0)),
        ),
        compiler_params=pltpu.CompilerParams(vmem_limit_bytes=44 * 2**20),
        cost_estimate=pl.CostEstimate(
            flops=2 * t * d * f, transcendentals=0, bytes_accessed=2 * (t * d + d * f + 4 * t * f)
        ),
    )(core, dy.reshape(t // tile, 2, rows, d), w, act, slope)


def collect_kernel(plane_ref, mine, other, *refs):
    w_ref, b_ref = refs[-2:]
    w_rows = w_ref.shape[0]
    each, _, cols = mine.shape
    for plane in (0, 1):

        @pl.when(plane_ref[0] == plane)
        def _():
            for k in range(each):
                for ref, h in ((mine, plane), (other, 1 - plane)):
                    at = slice((2 * k + h) * cols, (2 * k + h + 1) * cols)
                    w_ref[:, at] = ref[k, :w_rows].astype(F32)
                    b_ref[:, at] = ref[k, w_rows:].astype(F32)


def collect(plane, mine, other, w_rows, part, given):
    n, ext, cols = mine.shape
    each = 4
    piece = pl.BlockSpec((each, ext, cols), lambda s, _: (s, 0, 0))
    held = [] if given is None else list(given)
    steps = n // each
    return pl.pallas_call(
        collect_kernel,
        out_shape=(
            jax.ShapeDtypeStruct((w_rows, 4 * n * cols), F32),
            jax.ShapeDtypeStruct((ext - w_rows, 4 * n * cols), F32),
        ),
        grid_spec=pltpu.PrefetchScalarGridSpec(
            num_scalar_prefetch=1,
            grid=(steps,),
            in_specs=[piece, piece] + [pl.BlockSpec(memory_space=pl.ANY)] * len(held),
            out_specs=(
                pl.BlockSpec((w_rows, 2 * cols * each), lambda s, _: (0, part * steps + s)),
                pl.BlockSpec((ext - w_rows, 2 * cols * each), lambda s, _: (0, part * steps + s)),
            ),
        ),
        input_output_aliases={3: 0, 4: 1} if held else {},
        cost_estimate=pl.CostEstimate(
            flops=0, transcendentals=0, bytes_accessed=12 * n * ext * cols
        ),
    )(plane, mine, other, *held)


def stack_kernel(plane_ref, mine, other, w_ref, a_ref):
    width = w_ref.shape[1]
    own = pl.program_id(0) == plane_ref[0]

    @pl.when(own)
    def _():
        w_ref[...] = mine[:, :width].astype(F32)
        a_ref[...] = mine[:, width:].astype(F32)

    @pl.when(jnp.logical_not(own))
    def _():
        w_ref[...] = other[:, :width].astype(F32)
        a_ref[...] = other[:, width:].astype(F32)


def stack(plane, mine, other, width):
    half, cols = mine.shape
    tile = min(half, 128)
    tiles = half // tile
    given = pl.BlockSpec((tile, cols), lambda h, t, _: (t, 0))
    return pl.pallas_call(
        stack_kernel,
        out_shape=(
            jax.ShapeDtypeStruct((2 * half, width), F32),
            jax.ShapeDtypeStruct((2 * half, cols - width), F32),
        ),
        grid_spec=pltpu.PrefetchScalarGridSpec(
            num_scalar_prefetch=1,
            grid=(2, tiles),
            in_specs=[given, given],
            out_specs=(
                pl.BlockSpec((tile, width), lambda h, t, _: (h * tiles + t, 0)),
                pl.BlockSpec((tile, cols - width), lambda h, t, _: (h * tiles + t, 0)),
            ),
        ),
        cost_estimate=pl.CostEstimate(
            flops=0, transcendentals=0, bytes_accessed=16 * half * cols
        ),
    )(plane, mine, other)


def body(
    tokens,
    segments,
    output_cotangent_rows,
    attention_norm_gain,
    query_key_value_matrix,
    query_key_value_adapter_first,
    query_key_value_adapter_second,
    output_matrix,
    output_adapter_first,
    output_adapter_second,
    feed_norm_gain,
    gate_up_matrix,
    gate_up_adapter_first,
    gate_up_adapter_second,
    down_matrix,
    down_adapter_first,
    down_adapter_second,
):
    n = lax.axis_size("ctx")
    me = lax.axis_index("ctx")
    plane = lax.axis_index("grp")
    lines = n // 4
    rows = tokens.shape[1]
    width = tokens.shape[2]
    seq = rows * n
    rank = query_key_value_adapter_first.shape[1]
    qkv_cols = query_key_value_matrix.shape[1]
    feed_dev = down_matrix.shape[0]
    feed_half = feed_dev // 2
    w_rows = width // n
    r_rows = rank // n
    score_scale = HD ** (-0.5)

    def hop(x, k):
        return lax.ppermute(x, "ctx", [(i, i ^ k) for i in range(n)])

    def swap(x):
        return lax.ppermute(x, "grp", [(0, 1), (1, 0)])

    def swap_pieces(x, count):
        each = x.shape[0] // count
        return [swap(x[k * each : (k + 1) * each]) for k in range(count)]

    rel = jnp.arange(n, dtype=jnp.int32)
    rel = me ^ (rel // (2 * lines) + 2 * (rel // lines % 2) + 4 * (rel % lines))

    def reorder(x):
        r = x.shape[0] // n
        order = [4 * k + 2 * j + i for i in (0, 1) for j in (0, 1) for k in range(lines)]
        return jnp.concatenate(
            [lax.dynamic_slice_in_dim(x, (me ^ k) * r, r) for k in order], axis=0
        )

    def lines_of(x):
        return [x] + [hop(x, 4 * k) for k in range(1, lines)]

    def gather(x):
        along = lines_of(x)
        near = jnp.concatenate(along + [hop(b, 2) for b in along], axis=0)
        return jnp.concatenate([near, hop(near, 1)], axis=0)

    chip, core = me // 2, me % 2

    def gather_chips(along):
        x = along[0]
        blocks = [(2 * k, b) for k, b in enumerate(along)]
        blocks = blocks + [(k + 1, hop(b, 2)) for k, b in blocks]
        near = jnp.zeros((x.shape[0] * n // 2, x.shape[1]), x.dtype)
        for k, b in blocks:
            near = lax.dynamic_update_slice_in_dim(near, b, (chip ^ k) * x.shape[0], 0)
        return near

    def fold_core(near, arrived):
        r = near.shape[0] // (2 * lines)

        def block(k):
            at = (chip ^ k) * r
            a = lax.dynamic_slice_in_dim(near, at, r).astype(F32)
            return a + lax.dynamic_slice_in_dim(arrived, at, r).astype(F32)

        here = [block(2 * k) for k in range(lines)]
        return here, [block(2 * k + 1).astype(near.dtype) for k in range(lines)]

    def all_after(values, *others):
        return lax.optimization_barrier((*values, *others))[: len(values)]

    def scatter(near, far):
        kind = near.dtype
        mine = near.astype(F32) + hop(far, 1).astype(F32)
        half = near.shape[0] // 2
        mine = mine[:half] + hop(mine[half:].astype(kind), 2).astype(F32)
        r = half // lines
        total = mine[:r]
        for k in range(1, lines):
            total = total + hop(mine[k * r : (k + 1) * r].astype(kind), 4 * k).astype(F32)
        return total

    def scatter_whole(partial):
        half = partial.shape[0] // 2
        return scatter(partial[:half], partial[half:])

    x = tokens[0].astype(F32)
    dy = output_cotangent_rows[0]
    plane_id = plane.astype(jnp.int32).reshape(1)
    ext = w_rows + r_rows

    def beside(second):
        return second.reshape(w_rows, second.shape[1] * r_rows // w_rows)

    def apart(columns):
        return columns.reshape(rank, columns.shape[1] * w_rows // r_rows)

    q_second = qkv_cols * r_rows // w_rows
    o_second = width * r_rows // w_rows
    at_q = qkv_cols + rank
    pad = -(at_q + q_second) % 128
    gains = jnp.concatenate(
        [
            attention_norm_gain[:, None],
            feed_norm_gain[:, None],
            jnp.zeros((w_rows, pad - 2), BF),
        ],
        axis=1,
    )
    qkv_ext = jnp.concatenate(
        [
            query_key_value_matrix,
            query_key_value_adapter_first,
            beside(query_key_value_adapter_second),
            gains,
        ],
        axis=1,
    )
    qkv_got = lax.all_gather(qkv_ext, "ctx", axis=0, tiled=True)
    out_ext = jnp.concatenate(
        [
            output_matrix,
            output_adapter_first,
            gate_up_adapter_first,
            beside(output_adapter_second),
            beside(down_adapter_second),
        ],
        axis=1,
    )
    out_got = lax.all_gather(out_ext, "ctx", axis=0, tiled=True)
    qkv_full = qkv_got[:, :at_q]
    qkv_second = apart(qkv_got[:, at_q : at_q + q_second])
    gains_full = qkv_got[:, at_q + q_second : at_q + q_second + 2].astype(F32).T
    attn_gain, feed_gain = gains_full[:1], gains_full[1:]

    def exchange(pieces):
        flat = pieces.reshape(n * ext, feed_half)
        return lax.all_to_all(flat, "ctx", 0, 0, tiled=True).reshape(n, ext, feed_half)

    gate_mine = exchange(deal_out(0, plane_id, gate_up_matrix, gate_up_adapter_second, n))
    up_sent = deal_out(1, plane_id, gate_up_matrix, gate_up_adapter_second, n)

    def own_first(x):
        pair = x.reshape(2, feed_half, x.shape[1])
        a = lax.dynamic_index_in_dim(pair, plane, 0, False)
        b = lax.dynamic_index_in_dim(pair, 1 - plane, 0, False)
        return jnp.concatenate([a, b], axis=0)

    down_first, down_rows = own_first(down_adapter_first), own_first(down_matrix)

    def positions(device):
        within = jnp.arange(rows, dtype=jnp.int32)
        half = rows // 2
        block = jnp.where(within < half, device[:, None], 2 * n - 1 - device[:, None])
        return block * half + within % half

    local_pos = positions(me[None])[0]
    key_pos = positions(rel).reshape(seq)
    half = rows // 2
    local_seg = jnp.concatenate(
        [
            lax.dynamic_slice_in_dim(segments[0], me * half, half),
            lax.dynamic_slice_in_dim(segments[0], (2 * n - 1 - me) * half, half),
        ]
    )
    doc_start = jnp.sum(
        (segments[0][None, :] < local_seg[:, None]).astype(jnp.int32), axis=1
    )
    allowed = (key_pos[None, :] >= doc_start[:, None]) & (key_pos[None, :] <= local_pos[:, None])
    frequency = rope_base ** (-2.0 * jnp.arange(HD // 2, dtype=F32) / HD)
    angle_rows = local_pos.astype(F32)[:, None] * frequency[None, :]
    cosine, sine_rows = jnp.cos(angle_rows), jnp.sin(angle_rows)

    inv_one = inv_rms(x)
    norm_one = (x * inv_one * (1.0 + attn_gain)).astype(BF)
    norm_one = after(norm_one, gate_mine, up_sent)
    qkv_base = mm(norm_one, qkv_full)
    inner_qkv = qkv_base[:, qkv_cols:].astype(BF)
    qkv = qkv_base[:, :qkv_cols] + mm(inner_qkv, qkv_second)
    q = rotate(
        qkv[:, :width].reshape(rows, HEADS, HD), cosine[:, None, :], sine_rows[:, None, :]
    ).astype(BF)
    q_flat = q.reshape(rows * HEADS, HD)
    k_mine = rotate(qkv[:, width : width + HD], cosine, sine_rows).astype(BF)
    kv_mine = jnp.concatenate([k_mine, qkv[:, width + HD :].astype(BF)], axis=1)
    kv_all = gather(kv_mine)
    up_mine = exchange(after(up_sent, kv_all))
    gate_pieces = swap_pieces(gate_mine, 2)
    kv_all = after(kv_all, gate_pieces[0])
    k_all, v_all = kv_all[:, :HD], kv_all[:, HD:]
    raw = mm(q_flat, k_all, 1, 1).reshape(rows, HEADS, seq) * score_scale
    scores = jnp.where(allowed[:, None, :], raw, -jnp.inf)
    peak = jnp.max(scores, axis=-1, keepdims=True)
    unnormed = jnp.exp(scores - peak)
    total = jnp.sum(unnormed, axis=-1, keepdims=True)
    probs = (unnormed / total).astype(BF).reshape(rows * HEADS, seq)
    out_got = after(out_got, probs)
    out_full = out_got[:, : width + rank]
    gate_up_first = out_got[:, width + rank : width + 2 * rank]
    out_second = apart(out_got[:, width + 2 * rank : width + 2 * rank + o_second])
    down_second = apart(out_got[:, width + 2 * rank + o_second :])
    down_eff = (down_rows.astype(F32) + mm(down_first, down_second)).astype(BF)
    attended_f = mm(after(probs, gate_pieces[1]), v_all)
    gate_other = jnp.concatenate(gate_pieces, axis=0)
    attended = attended_f.reshape(rows, width).astype(BF)
    attended = after(attended, up_mine)
    up_pieces = swap_pieces(up_mine, 2)
    out_base = mm(attended, out_full)
    inner_out = out_base[:, width:].astype(BF)
    mid = x + out_base[:, :width] + mm(inner_out, out_second)

    inv_two = inv_rms(mid)
    norm_two = (mid * inv_two * (1.0 + feed_gain)).astype(BF)
    along = lines_of(norm_two)
    near_rows = gather_chips(along)
    dy_got = lax.all_gather(after(dy, *along), "ctx", axis=0, tiled=True)
    core_id = core.astype(jnp.int32).reshape(1)
    up_other = jnp.concatenate(up_pieces, axis=0)
    w_eff, (gate_b, up_b) = fold(gate_mine, up_mine, gate_up_first, 0, None)
    w_eff, _ = fold(gate_other, up_other, gate_up_first, 1, w_eff)
    near_rows = after(near_rows, w_eff, down_eff)
    all_rows = jnp.concatenate([near_rows, hop(near_rows, 1)], axis=0)
    hidden, act, slope = forward(core_id, all_rows, w_eff, rows)
    hidden = hidden.reshape(seq, feed_dev)
    out_part = mm(hidden, down_eff).astype(BF)
    out_sum = lax.psum_scatter(out_part, "ctx", scatter_dimension=0, tiled=True)
    h = feed_half
    half_seq = seq // 2
    down_part = mm(after(hidden, out_part)[:, h:], dy_got, 0, 0).astype(BF)
    grads = backward(core_id, after(dy_got, down_part), down_eff, act, slope, rows)
    down_part = swap(down_part)
    far_part = mm(grads[half_seq:], w_eff, 1, 1).astype(BF)
    near_part = mm(after(grads, far_part)[:half_seq], w_eff, 1, 1).astype(BF)
    here, there = fold_core(near_part, hop(far_part, 1))
    sides = [hop(part, 2) for part in there]

    late_rows, late_grads = lax.optimization_barrier(
        (all_rows, grads, near_part, *there)
    )[:2]
    other_part = mm(late_rows, late_grads[:, 2 * h :], 0, 0).astype(BF)
    gate_part, up_part = swap(other_part[:, :h]), swap(other_part[:, h:])
    sides = all_after(sides, other_part)
    sums = [a + b.astype(F32) for a, b in zip(here, sides)]
    line_sums = [part.astype(BF) for part in sums[1:]]
    arrivals = [hop(part, 4 * (k + 1)) for k, part in enumerate(line_sums)]
    down_half = (
        mm(after(hidden, other_part)[:, :h], dy_got, 0, 0) + down_part.astype(F32)
    ).astype(BF)
    g_down_first = mm(down_half, down_second, 1, 1).astype(BF)
    down_rows = jnp.concatenate([down_half, g_down_first], axis=1)

    late_rows = after(all_rows, down_rows, *line_sums)
    gate_half = (mm(late_rows, grads[:, :h], 0, 0) + gate_part.astype(F32)).astype(BF)

    pieces = jnp.concatenate(
        [
            norm_one.reshape(rows, n, w_rows),
            inner_qkv.reshape(rows, n, r_rows),
            attended.reshape(rows, n, w_rows),
            inner_out.reshape(rows, n, r_rows),
        ],
        axis=2,
    ).transpose(1, 0, 2)
    pieces = after(pieces, all_rows)
    inputs = lax.all_to_all(pieces.reshape(seq, 2 * ext), "ctx", 0, 0, tiled=True)

    arrivals = all_after(arrivals, gate_half, inputs)
    grad_norm_two = sums[0] + sum(part.astype(F32) for part in arrivals)
    feed_gain_rows = jnp.sum(grad_norm_two * mid * inv_two, axis=0, keepdims=True)
    grad_mid = dy.astype(F32) + norm_back(mid, inv_two, feed_gain, grad_norm_two)
    grad_branch = grad_mid.astype(BF)
    branch_all = lax.all_gather(grad_branch, "ctx", axis=0, tiled=True)
    grad_inner_out = mm(grad_branch, out_second, 1, 1).astype(BF)
    grad_attended = mm(
        jnp.concatenate([grad_branch, grad_inner_out], axis=1), out_full, 1, 1
    )
    delta = jnp.sum(
        (grad_attended * attended.astype(F32)).reshape(rows * HEADS, HD), axis=1, keepdims=True
    )
    grad_flat = grad_attended.astype(BF).reshape(rows * HEADS, HD)
    gate_second = mm(gate_up_first, gate_half, 0, 0).astype(BF)
    gate_ext = jnp.concatenate(
        [gate_half.reshape(n, w_rows, h), gate_second.reshape(n, r_rows, h)], axis=1
    )
    gate_got = exchange(gate_ext)
    grad_flat = after(grad_flat, gate_ext, out_sum)
    grad_probs = mm(grad_flat, v_all, 1, 1)
    grad_scores = (probs.astype(F32) * (grad_probs - delta)).astype(BF)
    grad_scores = after(grad_scores, up_part)
    grad_k = mm(grad_scores, q_flat, 0, 0) * score_scale
    grad_v = mm(probs, grad_flat, 0, 0)
    kv_part = jnp.concatenate([grad_k, grad_v], axis=1).astype(BF)
    grad_kv = scatter_whole(kv_part)
    grad_q = mm(after(grad_scores, kv_part), k_all) * score_scale
    grad_q_rows = (
        rotate(grad_q.reshape(rows, HEADS, HD), cosine[:, None, :], -sine_rows[:, None, :])
        .reshape(rows, width)
        .astype(BF)
    )
    q_all = lax.all_gather(grad_q_rows, "ctx", axis=0, tiled=True)
    up_half = (
        mm(after(all_rows, grad_q_rows, gate_got), grads[:, h : 2 * h], 0, 0)
        + up_part.astype(F32)
    ).astype(BF)
    down_back = swap(after(down_rows, up_part))
    grad_kv = after(grad_kv, up_half, down_back)
    grad_k_rows = rotate(grad_kv[:, :HD], cosine, -sine_rows)
    grad_kv_rows = jnp.concatenate([grad_k_rows, grad_kv[:, HD:]], axis=1).astype(BF)
    kv_all_grads = gather(grad_kv_rows)
    up_second = mm(gate_up_first, after(up_half, grad_kv_rows), 0, 0).astype(BF)
    up_ext = jnp.concatenate(
        [up_half.reshape(n, w_rows, h), up_second.reshape(n, r_rows, h)], axis=1
    )
    up_ext = after(up_ext, gate_got)
    up_got = exchange(up_ext)
    grad_qkv = jnp.concatenate([grad_q_rows, grad_kv_rows], axis=1)
    grad_qkv = after(grad_qkv, up_ext)
    grad_inner_qkv = mm(grad_qkv, qkv_second, 1, 1).astype(BF)
    grad_norm_one = mm(
        jnp.concatenate([grad_qkv, grad_inner_qkv], axis=1), qkv_full, 1, 1
    )
    attn_gain_rows = jnp.sum(grad_norm_one * x * inv_one, axis=0, keepdims=True)
    grad_input = (grad_mid + norm_back(x, inv_one, attn_gain, grad_norm_one)).astype(BF)
    gate_back = swap(after(gate_got, down_back))
    output = (mid + out_sum.astype(F32)).astype(BF)

    def both_planes(own):
        own = own.astype(BF)
        return own.astype(F32) + swap(own).astype(F32)


    small = jnp.concatenate(
        [
            (mm(gate_half, gate_b, 1, 1) + mm(up_half, up_b, 1, 1))
            .astype(BF)
            .reshape(n, w_rows, rank),
            mm(down_first[:h], after(down_half, grad_input), 0, 0)
            .astype(BF)
            .reshape(n, w_rows, width * r_rows // w_rows),
        ],
        axis=2,
    )
    small = scatter_whole(reorder(small.reshape(n * w_rows, small.shape[2])))
    gain_rows = jnp.concatenate([attn_gain_rows, feed_gain_rows], axis=0)
    gain_rows = gain_rows.reshape(2, n, w_rows).transpose(1, 0, 2).reshape(2 * n, w_rows)
    gain_rows = scatter_whole(reorder(gain_rows))

    g_out = mm(inputs[:, ext:], after(branch_all, grad_input), 0, 0).astype(BF)
    g_out_other = swap(g_out)
    down_grads = stack(plane_id, down_rows, after(down_back, g_out), width)
    gate_up_grads = collect(
        plane_id, gate_got, after(gate_back, g_out_other), w_rows, 0, None
    )
    up_got_other = swap(after(up_got, gate_back))
    g_q = mm(inputs[:, :ext], q_all, 0, 0)
    inputs_rel = reorder(inputs[:, :ext])
    g_kv = mm(inputs_rel, kv_all_grads, 0, 0)
    g_qkv = jnp.concatenate([g_q, g_kv], axis=1).astype(BF)
    gate_up_grads = collect(
        plane_id, up_got, after(up_got_other, g_qkv), w_rows, 1, gate_up_grads
    )
    g_out = g_out.astype(F32) + g_out_other.astype(F32)
    small = both_planes(after(small, gate_back))
    g_qkv = g_qkv.astype(F32) + after(swap(g_qkv), gate_up_grads[0]).astype(F32)
    gain_rows = gain_rows + swap(after(gain_rows, gate_back))
    g_gu_first = small[:, :rank]
    g_down_second = small[:, rank:].reshape(r_rows, width)
    g_out_first = mm(g_out[:w_rows].astype(BF), out_second, 1, 1)
    g_qkv_first = mm(g_qkv[:w_rows].astype(BF), qkv_second, 1, 1)

    return (
        output[None],
        grad_input[None],
        gain_rows[0],
        g_qkv[:w_rows],
        g_qkv_first,
        g_qkv[w_rows:],
        g_out[:w_rows],
        g_out_first,
        g_out[w_rows:],
        gain_rows[1],
        gate_up_grads[0],
        g_gu_first,
        gate_up_grads[1],
        down_grads[0],
        down_grads[1],
        g_down_second,
    )


def solution(mesh):
    rows = P("grp", "ctx", None)
    vector, matrix = P("ctx"), P("ctx", None)
    return jax.shard_map(
        body,
        mesh=mesh,
        in_specs=(rows, P("grp", None), rows, vector)
        + (matrix,) * 6
        + (vector,)
        + (matrix,) * 6,
        out_specs=(rows, rows, vector) + (matrix,) * 6 + (vector,) + (matrix,) * 6,
        check_vma=False,
    )
```

```python
import functools

import jax
import jax.numpy as jnp
from jax import lax
from jax.experimental import pallas as pl
from jax.experimental.pallas import tpu as pltpu
from jax.sharding import PartitionSpec as P

HEADS = 8
HD = 256
norm_eps = 1e-06
rope_base = 10000.0
BF = jnp.bfloat16
F32 = jnp.float32


def mm(a, b, ca=1, cb=0):
    return lax.dot_general(a, b, (((ca,), (cb,)), ((), ())), preferred_element_type=F32)


def rotate(vectors, cosine, sine_rows):
    front, back = jnp.split(vectors, 2, axis=-1)
    return jnp.concatenate(
        [front * cosine - back * sine_rows, back * cosine + front * sine_rows], axis=-1
    )


def inv_rms(values):
    return lax.rsqrt(jnp.mean(values * values, axis=-1, keepdims=True) + norm_eps)


def norm_back(values, inv, gain, grad):
    weighted = grad * (1.0 + gain)
    inner = jnp.mean(weighted * values, axis=-1, keepdims=True)
    return inv * weighted - values * (inv * inv * inv) * inner


def after(value, *others):
    return lax.optimization_barrier((value,) + others)[0]


def deal_kernel(plane_ref, *refs):
    out_ref = refs[-1]
    each = out_ref.shape[0]
    for k in range(each):
        w_ref, b_ref = refs[k], refs[each + k]
        w_rows = w_ref.shape[0]
        out_ref[k, :w_rows] = w_ref[...]
        out_ref[k, w_rows:] = b_ref[...]


def deal_out(part, plane, matrix, second, n):
    w_rows, r_rows = matrix.shape[0], second.shape[0]
    cols = matrix.shape[1] // (4 * n)
    each = 4

    def column(k, s, plane_ref):
        return (0, (part * n + s * each + k) * 2 + plane_ref[0])

    maps = [functools.partial(column, k) for k in range(each)]
    return pl.pallas_call(
        deal_kernel,
        out_shape=jax.ShapeDtypeStruct((n, w_rows + r_rows, cols), BF),
        grid_spec=pltpu.PrefetchScalarGridSpec(
            num_scalar_prefetch=1,
            grid=(n // each,),
            in_specs=[pl.BlockSpec((w_rows, cols), m) for m in maps]
            + [pl.BlockSpec((r_rows, cols), m) for m in maps],
            out_specs=pl.BlockSpec((each, w_rows + r_rows, cols), lambda s, p: (s, 0, 0)),
        ),
        cost_estimate=pl.CostEstimate(
            flops=0, transcendentals=0, bytes_accessed=4 * n * (w_rows + r_rows) * cols
        ),
    )(plane, *([matrix] * each), *([second] * each))


def fold_kernel(gate_ref, up_ref, b_gate_ref, b_up_ref, a_ref, *refs):
    out_ref = refs[-1]
    each, w_rows = gate_ref.shape[0], a_ref.shape[0] // gate_ref.shape[0]
    cols = b_gate_ref.shape[1]
    gate = mm(a_ref[...], b_gate_ref[...])
    up = mm(a_ref[...], b_up_ref[...])
    for k in range(each):
        part = slice(k * w_rows, (k + 1) * w_rows)
        out_ref[part, :cols] = (gate_ref[k, :w_rows].astype(F32) + gate[part]).astype(BF)
        out_ref[part, cols:] = (up_ref[k, :w_rows].astype(F32) + up[part]).astype(BF)


def fold(gate, up, first, place, given):
    n, ext, cols = gate.shape
    width, rank = first.shape
    w_rows = width // n
    each = max(1, min(4, 512 // w_rows))
    seconds = [x[:, w_rows:].reshape(rank, cols) for x in (gate, up)]
    piece = pl.BlockSpec((each, ext, cols), lambda s: (s, 0, 0))
    whole = pl.BlockSpec((rank, cols), lambda s: (0, 0))
    held = [] if given is None else [given]
    return pl.pallas_call(
        fold_kernel,
        out_shape=jax.ShapeDtypeStruct((width, 4 * cols), BF),
        grid=(n // each,),
        in_specs=[piece, piece, whole, whole]
        + [pl.BlockSpec((each * w_rows, rank), lambda s: (s, 0))]
        + [pl.BlockSpec(memory_space=pl.ANY)] * len(held),
        out_specs=pl.BlockSpec((each * w_rows, 2 * cols), lambda s: (s, place)),
        input_output_aliases={5: 0} if held else {},
        cost_estimate=pl.CostEstimate(
            flops=4 * width * rank * cols, transcendentals=0, bytes_accessed=8 * width * cols
        ),
    )(gate, up, *seconds, first, *held), seconds


def forward_kernel(core_ref, x_ref, w_ref, hidden_ref, act_ref, slope_ref):
    h = act_ref.shape[1] // 2
    rows = hidden_ref.shape[1]
    c = 0.7978845608028654
    for k in (0, 1):
        both = mm(x_ref[...], w_ref[:, 2 * k * h : 2 * (k + 1) * h])
        gate, up = both[:, :h], both[:, h:]
        square = gate * gate
        t = jnp.tanh(c * gate * (1.0 + 0.044715 * square))
        half_up = 0.5 * (1.0 + t)
        act = gate * half_up
        slope = half_up + 0.5 * gate * (1.0 - t * t) * (c * (1.0 + 3 * 0.044715 * square))
        part = slice(k * h, (k + 1) * h)
        hidden = (act * up).astype(BF)
        for j in range(hidden_ref.shape[0]):
            hidden_ref[j, :, part] = hidden[j * rows : (j + 1) * rows]
        act_ref[:, part] = act.astype(BF)
        slope_ref[:, part] = (slope * up).astype(BF)


def owner(tiles):
    def place(i, core_ref):
        mine = i < tiles // 2
        return (i % (tiles // 2), jnp.where(mine, core_ref[0], 1 - core_ref[0]), 0, 0)

    return place


def forward(core, x, w, rows):
    t, d = x.shape
    f = w.shape[1] // 2
    tile = 2 * rows
    out = pl.BlockSpec((tile, f), lambda i, _: (i, 0))
    ordered = pl.BlockSpec((2, None, rows, f), owner(t // tile))
    return pl.pallas_call(
        forward_kernel,
        out_shape=(jax.ShapeDtypeStruct((t // tile, 2, rows, f), BF),)
        + (jax.ShapeDtypeStruct((t, f), BF),) * 2,
        grid_spec=pltpu.PrefetchScalarGridSpec(
            num_scalar_prefetch=1,
            grid=(t // tile,),
            in_specs=[
                pl.BlockSpec((tile, d), lambda i, _: (i, 0)),
                pl.BlockSpec((d, 2 * f), lambda i, _: (0, 0)),
            ],
            out_specs=(ordered, out, out),
        ),
        compiler_params=pltpu.CompilerParams(vmem_limit_bytes=44 * 2**20),
        cost_estimate=pl.CostEstimate(
            flops=4 * t * d * f, transcendentals=t * f, bytes_accessed=2 * (t * d + 2 * d * f + 3 * t * f)
        ),
    )(core, x, w)


def backward_kernel(core_ref, dy_ref, w_ref, act_ref, slope_ref, out_ref):
    h = act_ref.shape[1] // 2
    dy = dy_ref[...].reshape(act_ref.shape[0], dy_ref.shape[2])
    for k in (0, 1):
        part = slice(k * h, (k + 1) * h)
        grad = mm(dy, w_ref[part, :], 1, 1)
        out_ref[:, 2 * k * h : (2 * k + 1) * h] = (grad * slope_ref[:, part].astype(F32)).astype(BF)
        out_ref[:, (2 * k + 1) * h : 2 * (k + 1) * h] = (
            grad * act_ref[:, part].astype(F32)
        ).astype(BF)


def backward(core, dy, w, act, slope, rows):
    t, f = act.shape
    d = dy.shape[1]
    tile = 2 * rows
    given = pl.BlockSpec((tile, f), lambda i, _: (i, 0))
    return pl.pallas_call(
        backward_kernel,
        out_shape=jax.ShapeDtypeStruct((t, 2 * f), BF),
        grid_spec=pltpu.PrefetchScalarGridSpec(
            num_scalar_prefetch=1,
            grid=(t // tile,),
            in_specs=[
                pl.BlockSpec((2, None, rows, d), owner(t // tile)),
                pl.BlockSpec((f, d), lambda i, _: (0, 0)),
                given,
                given,
            ],
            out_specs=pl.BlockSpec((tile, 2 * f), lambda i, _: (i, 0)),
        ),
        compiler_params=pltpu.CompilerParams(vmem_limit_bytes=44 * 2**20),
        cost_estimate=pl.CostEstimate(
            flops=2 * t * d * f, transcendentals=0, bytes_accessed=2 * (t * d + d * f + 4 * t * f)
        ),
    )(core, dy.reshape(t // tile, 2, rows, d), w, act, slope)


def collect_kernel(plane_ref, mine, other, *refs):
    w_ref, b_ref = refs[-2:]
    w_rows = w_ref.shape[0]
    each, _, cols = mine.shape
    for plane in (0, 1):

        @pl.when(plane_ref[0] == plane)
        def _():
            for k in range(each):
                for ref, h in ((mine, plane), (other, 1 - plane)):
                    at = slice((2 * k + h) * cols, (2 * k + h + 1) * cols)
                    w_ref[:, at] = ref[k, :w_rows].astype(F32)
                    b_ref[:, at] = ref[k, w_rows:].astype(F32)


def collect(plane, mine, other, w_rows, part, given):
    n, ext, cols = mine.shape
    each = 4
    piece = pl.BlockSpec((each, ext, cols), lambda s, _: (s, 0, 0))
    held = [] if given is None else list(given)
    steps = n // each
    return pl.pallas_call(
        collect_kernel,
        out_shape=(
            jax.ShapeDtypeStruct((w_rows, 4 * n * cols), F32),
            jax.ShapeDtypeStruct((ext - w_rows, 4 * n * cols), F32),
        ),
        grid_spec=pltpu.PrefetchScalarGridSpec(
            num_scalar_prefetch=1,
            grid=(steps,),
            in_specs=[piece, piece] + [pl.BlockSpec(memory_space=pl.ANY)] * len(held),
            out_specs=(
                pl.BlockSpec((w_rows, 2 * cols * each), lambda s, _: (0, part * steps + s)),
                pl.BlockSpec((ext - w_rows, 2 * cols * each), lambda s, _: (0, part * steps + s)),
            ),
        ),
        input_output_aliases={3: 0, 4: 1} if held else {},
        cost_estimate=pl.CostEstimate(
            flops=0, transcendentals=0, bytes_accessed=12 * n * ext * cols
        ),
    )(plane, mine, other, *held)


def stack_kernel(plane_ref, mine, other, w_ref, a_ref):
    width = w_ref.shape[1]
    own = pl.program_id(0) == plane_ref[0]

    @pl.when(own)
    def _():
        w_ref[...] = mine[:, :width].astype(F32)
        a_ref[...] = mine[:, width:].astype(F32)

    @pl.when(jnp.logical_not(own))
    def _():
        w_ref[...] = other[:, :width].astype(F32)
        a_ref[...] = other[:, width:].astype(F32)


def stack(plane, mine, other, width):
    half, cols = mine.shape
    tile = min(half, 128)
    tiles = half // tile
    given = pl.BlockSpec((tile, cols), lambda h, t, _: (t, 0))
    return pl.pallas_call(
        stack_kernel,
        out_shape=(
            jax.ShapeDtypeStruct((2 * half, width), F32),
            jax.ShapeDtypeStruct((2 * half, cols - width), F32),
        ),
        grid_spec=pltpu.PrefetchScalarGridSpec(
            num_scalar_prefetch=1,
            grid=(2, tiles),
            in_specs=[given, given],
            out_specs=(
                pl.BlockSpec((tile, width), lambda h, t, _: (h * tiles + t, 0)),
                pl.BlockSpec((tile, cols - width), lambda h, t, _: (h * tiles + t, 0)),
            ),
        ),
        cost_estimate=pl.CostEstimate(
            flops=0, transcendentals=0, bytes_accessed=16 * half * cols
        ),
    )(plane, mine, other)


def body(
    tokens,
    segments,
    output_cotangent_rows,
    attention_norm_gain,
    query_key_value_matrix,
    query_key_value_adapter_first,
    query_key_value_adapter_second,
    output_matrix,
    output_adapter_first,
    output_adapter_second,
    feed_norm_gain,
    gate_up_matrix,
    gate_up_adapter_first,
    gate_up_adapter_second,
    down_matrix,
    down_adapter_first,
    down_adapter_second,
):
    n = lax.axis_size("ctx")
    me = lax.axis_index("ctx")
    plane = lax.axis_index("grp")
    lines = n // 4
    rows = tokens.shape[1]
    width = tokens.shape[2]
    seq = rows * n
    rank = query_key_value_adapter_first.shape[1]
    qkv_cols = query_key_value_matrix.shape[1]
    feed_dev = down_matrix.shape[0]
    feed_half = feed_dev // 2
    w_rows = width // n
    r_rows = rank // n
    score_scale = HD ** (-0.5)

    def hop(x, k):
        return lax.ppermute(x, "ctx", [(i, i ^ k) for i in range(n)])

    def swap(x):
        return lax.ppermute(x, "grp", [(0, 1), (1, 0)])

    def swap_pieces(x, count):
        each = x.shape[0] // count
        return [swap(x[k * each : (k + 1) * each]) for k in range(count)]

    rel = jnp.arange(n, dtype=jnp.int32)
    rel = me ^ (rel // (2 * lines) + 2 * (rel // lines % 2) + 4 * (rel % lines))

    def reorder(x):
        r = x.shape[0] // n
        order = [4 * k + 2 * j + i for i in (0, 1) for j in (0, 1) for k in range(lines)]
        return jnp.concatenate(
            [lax.dynamic_slice_in_dim(x, (me ^ k) * r, r) for k in order], axis=0
        )

    def lines_of(x):
        return [x] + [hop(x, 4 * k) for k in range(1, lines)]

    def gather(x):
        along = lines_of(x)
        near = jnp.concatenate(along + [hop(b, 2) for b in along], axis=0)
        return jnp.concatenate([near, hop(near, 1)], axis=0)

    chip, core = me // 2, me % 2

    def gather_chips(x):
        along = lines_of(x)
        blocks = [(2 * k, b) for k, b in enumerate(along)]
        blocks = blocks + [(k + 1, hop(b, 2)) for k, b in blocks]
        near = jnp.zeros((x.shape[0] * n // 2, x.shape[1]), x.dtype)
        for k, b in blocks:
            near = lax.dynamic_update_slice_in_dim(near, b, (chip ^ k) * x.shape[0], 0)
        return near

    def fold_core(near, arrived):
        r = near.shape[0] // (2 * lines)

        def block(k):
            at = (chip ^ k) * r
            a = lax.dynamic_slice_in_dim(near, at, r).astype(F32)
            return a + lax.dynamic_slice_in_dim(arrived, at, r).astype(F32)

        here = [block(2 * k) for k in range(lines)]
        return here, [block(2 * k + 1).astype(near.dtype) for k in range(lines)]

    def all_after(values, *others):
        return lax.optimization_barrier((*values, *others))[: len(values)]

    def scatter(near, far):
        kind = near.dtype
        mine = near.astype(F32) + hop(far, 1).astype(F32)
        half = near.shape[0] // 2
        mine = mine[:half] + hop(mine[half:].astype(kind), 2).astype(F32)
        r = half // lines
        total = mine[:r]
        for k in range(1, lines):
            total = total + hop(mine[k * r : (k + 1) * r].astype(kind), 4 * k).astype(F32)
        return total

    def scatter_whole(partial):
        half = partial.shape[0] // 2
        return scatter(partial[:half], partial[half:])

    x = tokens[0].astype(F32)
    dy = output_cotangent_rows[0]
    plane_id = plane.astype(jnp.int32).reshape(1)
    ext = w_rows + r_rows

    def beside(second):
        return second.reshape(w_rows, second.shape[1] * r_rows // w_rows)

    def apart(columns):
        return columns.reshape(rank, columns.shape[1] * w_rows // r_rows)

    q_second = qkv_cols * r_rows // w_rows
    o_second = width * r_rows // w_rows
    at_q = qkv_cols + rank
    pad = -(at_q + q_second) % 128
    gains = jnp.concatenate(
        [
            attention_norm_gain[:, None],
            feed_norm_gain[:, None],
            jnp.zeros((w_rows, pad - 2), BF),
        ],
        axis=1,
    )
    qkv_ext = jnp.concatenate(
        [
            query_key_value_matrix,
            query_key_value_adapter_first,
            beside(query_key_value_adapter_second),
            gains,
        ],
        axis=1,
    )
    qkv_got = lax.all_gather(qkv_ext, "ctx", axis=0, tiled=True)
    out_ext = jnp.concatenate(
        [
            output_matrix,
            output_adapter_first,
            gate_up_adapter_first,
            beside(output_adapter_second),
            beside(down_adapter_second),
        ],
        axis=1,
    )
    out_got = lax.all_gather(out_ext, "ctx", axis=0, tiled=True)
    qkv_full = qkv_got[:, :at_q]
    qkv_second = apart(qkv_got[:, at_q : at_q + q_second])
    gains_full = qkv_got[:, at_q + q_second : at_q + q_second + 2].astype(F32).T
    attn_gain, feed_gain = gains_full[:1], gains_full[1:]

    def exchange(pieces):
        flat = pieces.reshape(n * ext, feed_half)
        return lax.all_to_all(flat, "ctx", 0, 0, tiled=True).reshape(n, ext, feed_half)

    gate_mine = exchange(deal_out(0, plane_id, gate_up_matrix, gate_up_adapter_second, n))
    up_sent = deal_out(1, plane_id, gate_up_matrix, gate_up_adapter_second, n)

    def own_first(x):
        pair = x.reshape(2, feed_half, x.shape[1])
        a = lax.dynamic_index_in_dim(pair, plane, 0, False)
        b = lax.dynamic_index_in_dim(pair, 1 - plane, 0, False)
        return jnp.concatenate([a, b], axis=0)

    down_first, down_rows = own_first(down_adapter_first), own_first(down_matrix)

    def positions(device):
        within = jnp.arange(rows, dtype=jnp.int32)
        half = rows // 2
        block = jnp.where(within < half, device[:, None], 2 * n - 1 - device[:, None])
        return block * half + within % half

    local_pos = positions(me[None])[0]
    key_pos = positions(rel).reshape(seq)
    half = rows // 2
    local_seg = jnp.concatenate(
        [
            lax.dynamic_slice_in_dim(segments[0], me * half, half),
            lax.dynamic_slice_in_dim(segments[0], (2 * n - 1 - me) * half, half),
        ]
    )
    doc_start = jnp.sum(
        (segments[0][None, :] < local_seg[:, None]).astype(jnp.int32), axis=1
    )
    allowed = (key_pos[None, :] >= doc_start[:, None]) & (key_pos[None, :] <= local_pos[:, None])
    frequency = rope_base ** (-2.0 * jnp.arange(HD // 2, dtype=F32) / HD)
    angle_rows = local_pos.astype(F32)[:, None] * frequency[None, :]
    cosine, sine_rows = jnp.cos(angle_rows), jnp.sin(angle_rows)

    inv_one = inv_rms(x)
    norm_one = (x * inv_one * (1.0 + attn_gain)).astype(BF)
    norm_one = after(norm_one, gate_mine, up_sent)
    qkv_base = mm(norm_one, qkv_full)
    inner_qkv = qkv_base[:, qkv_cols:].astype(BF)
    qkv = qkv_base[:, :qkv_cols] + mm(inner_qkv, qkv_second)
    q = rotate(
        qkv[:, :width].reshape(rows, HEADS, HD), cosine[:, None, :], sine_rows[:, None, :]
    ).astype(BF)
    q_flat = q.reshape(rows * HEADS, HD)
    k_mine = rotate(qkv[:, width : width + HD], cosine, sine_rows).astype(BF)
    kv_mine = jnp.concatenate([k_mine, qkv[:, width + HD :].astype(BF)], axis=1)
    kv_all = gather(kv_mine)
    dy_got = lax.all_gather(after(dy, kv_mine), "ctx", axis=0, tiled=True)
    up_mine = exchange(after(up_sent, kv_all))
    gate_pieces = swap_pieces(gate_mine, 2)
    kv_all = after(kv_all, gate_pieces[0])
    k_all, v_all = kv_all[:, :HD], kv_all[:, HD:]
    raw = mm(q_flat, k_all, 1, 1).reshape(rows, HEADS, seq) * score_scale
    scores = jnp.where(allowed[:, None, :], raw, -jnp.inf)
    peak = jnp.max(scores, axis=-1, keepdims=True)
    unnormed = jnp.exp(scores - peak)
    total = jnp.sum(unnormed, axis=-1, keepdims=True)
    probs = (unnormed / total).astype(BF).reshape(rows * HEADS, seq)
    out_got = after(out_got, probs)
    out_full = out_got[:, : width + rank]
    gate_up_first = out_got[:, width + rank : width + 2 * rank]
    out_second = apart(out_got[:, width + 2 * rank : width + 2 * rank + o_second])
    down_second = apart(out_got[:, width + 2 * rank + o_second :])
    down_eff = (down_rows.astype(F32) + mm(down_first, down_second)).astype(BF)
    attended_f = mm(after(probs, gate_pieces[1]), v_all)
    gate_other = jnp.concatenate(gate_pieces, axis=0)
    attended = attended_f.reshape(rows, width).astype(BF)
    attended = after(attended, up_mine)
    up_pieces = swap_pieces(up_mine, 2)
    out_base = mm(attended, out_full)
    inner_out = out_base[:, width:].astype(BF)
    mid = x + out_base[:, :width] + mm(inner_out, out_second)

    inv_two = inv_rms(mid)
    norm_two = (mid * inv_two * (1.0 + feed_gain)).astype(BF)
    near_rows = gather_chips(norm_two)
    core_id = core.astype(jnp.int32).reshape(1)
    up_other = jnp.concatenate(up_pieces, axis=0)
    w_eff, (gate_b, up_b) = fold(gate_mine, up_mine, gate_up_first, 0, None)
    w_eff, _ = fold(gate_other, up_other, gate_up_first, 1, w_eff)
    near_rows = after(near_rows, w_eff, down_eff)
    all_rows = jnp.concatenate([near_rows, hop(near_rows, 1)], axis=0)
    hidden, act, slope = forward(core_id, all_rows, w_eff, rows)
    hidden = hidden.reshape(seq, feed_dev)
    out_part = mm(hidden, down_eff).astype(BF)
    out_sum = lax.psum_scatter(out_part, "ctx", scatter_dimension=0, tiled=True)
    h = feed_half
    half_seq = seq // 2
    down_part = mm(after(hidden, out_part)[:, h:], dy_got, 0, 0).astype(BF)
    grads = backward(core_id, after(dy_got, down_part), down_eff, act, slope, rows)
    down_part = swap(down_part)
    far_part = mm(grads[half_seq:], w_eff, 1, 1).astype(BF)
    near_part = mm(after(grads, far_part)[:half_seq], w_eff, 1, 1).astype(BF)
    here, there = fold_core(near_part, hop(far_part, 1))
    sides = [hop(part, 2) for part in there]

    late_rows, late_grads = lax.optimization_barrier(
        (all_rows, grads, near_part, *there)
    )[:2]
    other_part = mm(late_rows, late_grads[:, 2 * h :], 0, 0).astype(BF)
    gate_part, up_part = swap(other_part[:, :h]), swap(other_part[:, h:])
    sides = all_after(sides, other_part)
    sums = [a + b.astype(F32) for a, b in zip(here, sides)]
    line_sums = [part.astype(BF) for part in sums[1:]]
    arrivals = [hop(part, 4 * (k + 1)) for k, part in enumerate(line_sums)]
    down_half = (
        mm(after(hidden, other_part)[:, :h], dy_got, 0, 0) + down_part.astype(F32)
    ).astype(BF)
    g_down_first = mm(down_half, down_second, 1, 1).astype(BF)
    down_rows = jnp.concatenate([down_half, g_down_first], axis=1)

    late_rows = after(all_rows, down_rows, *line_sums)
    gate_half = (mm(late_rows, grads[:, :h], 0, 0) + gate_part.astype(F32)).astype(BF)

    pieces = jnp.concatenate(
        [
            norm_one.reshape(rows, n, w_rows),
            inner_qkv.reshape(rows, n, r_rows),
            attended.reshape(rows, n, w_rows),
            inner_out.reshape(rows, n, r_rows),
        ],
        axis=2,
    ).transpose(1, 0, 2)
    pieces = after(pieces, all_rows)
    inputs = lax.all_to_all(pieces.reshape(seq, 2 * ext), "ctx", 0, 0, tiled=True)

    arrivals = all_after(arrivals, gate_half, inputs)
    grad_norm_two = sums[0] + sum(part.astype(F32) for part in arrivals)
    feed_gain_rows = jnp.sum(grad_norm_two * mid * inv_two, axis=0, keepdims=True)
    grad_mid = dy.astype(F32) + norm_back(mid, inv_two, feed_gain, grad_norm_two)
    grad_branch = grad_mid.astype(BF)
    branch_all = lax.all_gather(grad_branch, "ctx", axis=0, tiled=True)
    grad_inner_out = mm(grad_branch, out_second, 1, 1).astype(BF)
    grad_attended = mm(
        jnp.concatenate([grad_branch, grad_inner_out], axis=1), out_full, 1, 1
    )
    delta = jnp.sum(
        (grad_attended * attended.astype(F32)).reshape(rows * HEADS, HD), axis=1, keepdims=True
    )
    grad_flat = grad_attended.astype(BF).reshape(rows * HEADS, HD)
    gate_second = mm(gate_up_first, gate_half, 0, 0).astype(BF)
    gate_ext = jnp.concatenate(
        [gate_half.reshape(n, w_rows, h), gate_second.reshape(n, r_rows, h)], axis=1
    )
    gate_got = exchange(gate_ext)
    grad_flat = after(grad_flat, gate_ext, out_sum)
    grad_probs = mm(grad_flat, v_all, 1, 1)
    grad_scores = (probs.astype(F32) * (grad_probs - delta)).astype(BF)
    grad_scores = after(grad_scores, up_part)
    grad_k = mm(grad_scores, q_flat, 0, 0) * score_scale
    grad_v = mm(probs, grad_flat, 0, 0)
    kv_part = jnp.concatenate([grad_k, grad_v], axis=1).astype(BF)
    grad_kv = scatter_whole(kv_part)
    grad_q = mm(after(grad_scores, kv_part), k_all) * score_scale
    grad_q_rows = (
        rotate(grad_q.reshape(rows, HEADS, HD), cosine[:, None, :], -sine_rows[:, None, :])
        .reshape(rows, width)
        .astype(BF)
    )
    q_all = lax.all_gather(grad_q_rows, "ctx", axis=0, tiled=True)
    up_half = (
        mm(after(all_rows, grad_q_rows), grads[:, h : 2 * h], 0, 0)
        + up_part.astype(F32)
    ).astype(BF)
    down_back = swap(after(down_rows, up_part))
    grad_kv = after(grad_kv, up_half, down_back)
    grad_k_rows = rotate(grad_kv[:, :HD], cosine, -sine_rows)
    grad_kv_rows = jnp.concatenate([grad_k_rows, grad_kv[:, HD:]], axis=1).astype(BF)
    kv_all_grads = gather(grad_kv_rows)
    up_second = mm(gate_up_first, after(up_half, grad_kv_rows), 0, 0).astype(BF)
    up_ext = jnp.concatenate(
        [up_half.reshape(n, w_rows, h), up_second.reshape(n, r_rows, h)], axis=1
    )
    up_ext = after(up_ext, gate_got)
    up_got = exchange(up_ext)
    grad_qkv = jnp.concatenate([grad_q_rows, grad_kv_rows], axis=1)
    grad_qkv = after(grad_qkv, up_ext)
    grad_inner_qkv = mm(grad_qkv, qkv_second, 1, 1).astype(BF)
    grad_norm_one = mm(
        jnp.concatenate([grad_qkv, grad_inner_qkv], axis=1), qkv_full, 1, 1
    )
    attn_gain_rows = jnp.sum(grad_norm_one * x * inv_one, axis=0, keepdims=True)
    grad_input = (grad_mid + norm_back(x, inv_one, attn_gain, grad_norm_one)).astype(BF)
    gate_back = swap(after(gate_got, down_back))
    output = (mid + out_sum.astype(F32)).astype(BF)

    def both_planes(own):
        own = own.astype(BF)
        return own.astype(F32) + swap(own).astype(F32)


    small = jnp.concatenate(
        [
            (mm(gate_half, gate_b, 1, 1) + mm(up_half, up_b, 1, 1))
            .astype(BF)
            .reshape(n, w_rows, rank),
            mm(down_first[:h], after(down_half, grad_input), 0, 0)
            .astype(BF)
            .reshape(n, w_rows, width * r_rows // w_rows),
        ],
        axis=2,
    )
    small = scatter_whole(reorder(small.reshape(n * w_rows, small.shape[2])))
    gain_rows = jnp.concatenate([attn_gain_rows, feed_gain_rows], axis=0)
    gain_rows = gain_rows.reshape(2, n, w_rows).transpose(1, 0, 2).reshape(2 * n, w_rows)
    gain_rows = scatter_whole(reorder(gain_rows))

    down_grads = stack(plane_id, down_rows, after(down_back, grad_input), width)
    gate_up_grads = collect(
        plane_id, gate_got, after(gate_back, grad_input), w_rows, 0, None
    )
    up_got_other = swap(after(up_got, gate_back))
    gate_up_grads = collect(plane_id, up_got, up_got_other, w_rows, 1, gate_up_grads)

    g_out = mm(inputs[:, ext:], after(branch_all, down_grads[0]), 0, 0).astype(BF)
    g_q = mm(inputs[:, :ext], after(q_all, g_out), 0, 0)
    inputs_rel = reorder(inputs[:, :ext])
    g_kv = mm(inputs_rel, kv_all_grads, 0, 0)
    g_qkv = jnp.concatenate([g_q, g_kv], axis=1).astype(BF)
    g_out = both_planes(after(g_out, gate_back))
    small = both_planes(after(small, gate_back))
    g_qkv = g_qkv.astype(F32) + after(swap(g_qkv), gate_up_grads[0]).astype(F32)
    gain_rows = gain_rows + swap(after(gain_rows, up_got_other))
    g_gu_first = small[:, :rank]
    g_down_second = small[:, rank:].reshape(r_rows, width)
    g_out_first = mm(g_out[:w_rows].astype(BF), out_second, 1, 1)
    g_qkv_first = mm(g_qkv[:w_rows].astype(BF), qkv_second, 1, 1)

    return (
        output[None],
        grad_input[None],
        gain_rows[0],
        g_qkv[:w_rows],
        g_qkv_first,
        g_qkv[w_rows:],
        g_out[:w_rows],
        g_out_first,
        g_out[w_rows:],
        gain_rows[1],
        gate_up_grads[0],
        g_gu_first,
        gate_up_grads[1],
        down_grads[0],
        down_grads[1],
        g_down_second,
    )


def solution(mesh):
    rows = P("grp", "ctx", None)
    vector, matrix = P("ctx"), P("ctx", None)
    return jax.shard_map(
        body,
        mesh=mesh,
        in_specs=(rows, P("grp", None), rows, vector)
        + (matrix,) * 6
        + (vector,)
        + (matrix,) * 6,
        out_specs=(rows, rows, vector) + (matrix,) * 6 + (vector,) + (matrix,) * 6,
        check_vma=False,
    )
```
